32 devices in a mesh: head: 4 (over y, x), dp: 8 (over z, core).
Axes of the slice: x: 2, y: 2, z: 4, core: 2. Of those that a mesh axis runs over, the one named last changes fastest.
Arguments:
- inputs: bfloat16 [2048, 8, 768], P('head', 'dp'), may hold values from -6 to 6
- bucket: int32 [8], P('dp'), may hold values from 0 to 1
- norm1_gain: float32 [768], replicated, may hold values from 0.5 to 1.5
- norm1_bias: float32 [768], replicated, may hold values from -1.8 to 1.8
- qkv_weight: bfloat16 [3, 768, 768], P(None, None, 'head'), may hold values from -0.21875 to 0.21875
- qv_bias: float32 [2, 768], P(None, 'head'), may hold values from -3 to 3
- inner_gain: float32 [768], P('head'), may hold values from 0.5 to 1.5
- inner_bias: float32 [768], P('head'), may hold values from -1.8 to 1.8
- out_weight: bfloat16 [768, 768], P('head'), may hold values from -0.21875 to 0.21875
- out_bias: float32 [768], replicated, may hold values from -1.8 to 1.8
- norm2_gain: float32 [768], replicated, may hold values from 0.5 to 1.5
- norm2_bias: float32 [768], replicated, may hold values from -1.8 to 1.8
- fc1_weight: bfloat16 [768, 3072], P(None, 'head'), may hold values from -0.21875 to 0.21875
- fc1_bias: bfloat16 [3072], P('head'), may hold values from -3 to 3
- ffn_gain: bfloat16 [3072], P('head'), may hold values from 0.5 to 1.5
- ffn_bias: bfloat16 [3072], P('head'), may hold values from -1.796875 to 1.796875
- fc2_weight: bfloat16 [3072, 768], P('head'), may hold values from -0.109375 to 0.109375
- fc2_bias: float32 [768], replicated, may hold values from -1.8 to 1.8
- cotangent: bfloat16 [2048, 8, 768], P(None, 'dp'), may hold values from -6 to 6
Outputs:
- output: bfloat16 [2048, 8, 768], P('head', 'dp')
- input_grad: bfloat16 [2048, 8, 768], P('head', 'dp')
- grad_qkv_weight: float32 [3, 768, 768], P(None, 'dp', 'head')
- grad_out_weight: float32 [768, 768], P('head', 'dp')
- grad_fc1_weight: float32 [768, 3072], P('dp', 'head')
- grad_fc2_weight: float32 [3072, 768], P('head', 'dp')
- grad_qv_bias: float32 [2, 768], P(None, ('head', 'dp'))
- grad_inner_gain: float32 [768], P(('head', 'dp'))
- grad_inner_bias: float32 [768], P(('head', 'dp'))
- grad_fc1_bias: float32 [3072], P(('head', 'dp'))
- grad_ffn_gain: float32 [3072], P(('head', 'dp'))
- grad_ffn_bias: float32 [3072], P(('head', 'dp'))
- grad_norm1_gain: float32 [768], P('dp')
- grad_norm1_bias: float32 [768], P('dp')
- grad_out_bias: float32 [768], P('dp')
- grad_norm2_gain: float32 [768], P('dp')
- grad_norm2_bias: float32 [768], P('dp')
- grad_fc2_bias: float32 [768], P('dp')
The draws below stay inside these ranges and needn't reach their ends.
Inputs may be any that keep to these rules, and one draw needn't show every extreme that they name: bucket 1: the slab is one causal sequence of 2048 tokens; bucket 0: it is 4 sequences of 512.
All inputs are finite; a program needn't handle non-finite values.
Results may differ from the reference program's by a relative error of at most 0.019.
Values may be sent and summed in bfloat16 or wider, within the bound.
No kernel may reach another device: no remote copies, remote signals or barrier semaphores. Data moves between devices by JAX's collectives and lax.ppermute only.
A program may use at most 192 MiB of HBM per device.

```python
import jax
import jax.numpy as jnp
from jax import lax

D = 768
HEADS = 12
HEAD_DIM = 64
FF = 3072
LONG_LEN = 2048
SHORT_LEN = 512
SLABS = 8


def with_ends(entries, own_key, low, largest):
    longest = entries.shape.index(max(entries.shape))
    spots = []
    for shift in (0, 1):
        where = [jax.random.randint(jax.random.fold_in(own_key, axis), (), 0, length) for axis, length in enumerate(entries.shape)]
        where[longest] = (where[longest] + shift) % entries.shape[longest]
        spots.append(tuple(where))
    return entries.at[spots[0]].set(low).at[spots[1]].set(largest)


def levels(own_key, extent, split, low, top_value):
    level, own = 1.0, jax.random.fold_in(own_key, 6)
    for dim, parts in split:
        steps = jnp.exp(jax.random.uniform(jax.random.fold_in(own, dim), (parts,), jnp.float32, low / len(split), top_value / len(split)))
        level = level * jnp.repeat(steps, extent[dim] // parts).reshape([-1 if axis == dim else 1 for axis in range(len(extent))])
    return level


def noise(rng, extent, scale, most, pieces=(), kind=jnp.bfloat16):
    loudness = levels(rng, extent, pieces, -0.22, 0.18) if pieces else 1.0
    values = jax.random.normal(rng, extent, jnp.float32) * scale * loudness
    return jnp.minimum(jnp.maximum(values, -most), most).astype(kind)


def setup_inputs(seed: int = 0) -> dict:
    streams_of = jax.random.split(jax.random.key(seed), 20)
    inputs = noise(streams_of[0], (LONG_LEN, SLABS, D), 1.0, 6.0, ((0, 4), (1, 8)))
    bucket = with_ends(jax.random.randint(streams_of[1], (SLABS,), 0, 2), jax.random.fold_in(streams_of[1], 1), 0, 1).astype(jnp.int32)
    norm1_gain = jnp.clip(1.0 + 0.1 * jax.random.normal(streams_of[2], (D,), jnp.float32), 0.5, 1.5)
    norm1_bias = noise(streams_of[3], (D,), 0.3, 1.8, (), jnp.float32)
    qkv_weight = noise(streams_of[4], (3, D, D), D ** -0.5, 0.21875, ((2, 4),))
    qv_bias = noise(streams_of[5], (2, D), 0.5, 3.0, ((1, 4),), jnp.float32)
    inner_gain = jnp.clip(1.0 + 0.1 * jax.random.normal(streams_of[6], (D,), jnp.float32), 0.5, 1.5)
    inner_bias = noise(streams_of[7], (D,), 0.3, 1.8, ((0, 4),), jnp.float32)
    out_weight = noise(streams_of[8], (D, D), D ** -0.5, 0.21875, ((0, 4),))
    out_bias = noise(streams_of[9], (D,), 0.3, 1.8, (), jnp.float32)
    norm2_gain = jnp.clip(1.0 + 0.1 * jax.random.normal(streams_of[10], (D,), jnp.float32), 0.5, 1.5)
    norm2_bias = noise(streams_of[11], (D,), 0.3, 1.8, (), jnp.float32)
    fc1_weight = noise(streams_of[12], (D, FF), D ** -0.5, 0.21875, ((1, 4),))
    fc1_bias = noise(streams_of[13], (FF,), 0.5, 3.0, ((0, 4),))
    ffn_gain = jnp.clip(1.0 + 0.1 * jax.random.normal(streams_of[14], (FF,), jnp.float32), 0.5, 1.5).astype(jnp.bfloat16)
    ffn_bias = noise(streams_of[15], (FF,), 0.3, 1.796875, ((0, 4),))
    fc2_weight = noise(streams_of[16], (FF, D), FF ** -0.5, 0.109375, ((0, 4),))
    fc2_bias = noise(streams_of[17], (D,), 0.3, 1.8, (), jnp.float32)
    cotangent = noise(streams_of[18], (LONG_LEN, SLABS, D), 1.0, 6.0, ((1, 8),))
    return {"inputs": inputs, "bucket": bucket, "norm1_gain": norm1_gain, "norm1_bias": norm1_bias, "qkv_weight": qkv_weight, "qv_bias": qv_bias, "inner_gain": inner_gain, "inner_bias": inner_bias, "out_weight": out_weight, "out_bias": out_bias, "norm2_gain": norm2_gain, "norm2_bias": norm2_bias, "fc1_weight": fc1_weight, "fc1_bias": fc1_bias, "ffn_gain": ffn_gain, "ffn_bias": ffn_bias, "fc2_weight": fc2_weight, "fc2_bias": fc2_bias, "cotangent": cotangent}


@jax.custom_vjp
def low(v):
    return lax.optimization_barrier(v.astype(jnp.bfloat16)).astype(jnp.float32)

@jax.custom_vjp
def low_back(v):
    return v

def low_keep(v):
    return (low(v), None)

def low_pass(kept, grad):
    return (grad,)

def back_keep(v):
    return (v, None)

def back_low(kept, grad):
    return (low(grad),)
low.defvjp(low_keep, low_pass)
low_back.defvjp(back_keep, back_low)
EPS = 1e-05
HIGH = lax.Precision.HIGHEST

def product(left, right):
    return jnp.dot(left, right, precision=HIGH)

def layer_norm(matrix, gain, shift):
    row_mean = lax.optimization_barrier(jnp.mean(matrix, axis=-1, keepdims=True))
    centred = matrix - row_mean
    variance = lax.optimization_barrier(jnp.mean(centred * centred, axis=-1, keepdims=True))
    return centred * lax.rsqrt(variance + EPS) * gain + shift

def attention(queries, key_rows, values, bucket_one):
    score_scale = HEAD_DIM ** (-0.5)
    block_count = LONG_LEN // SHORT_LEN
    query_blocks = queries.reshape(block_count, SHORT_LEN, HEADS, HEAD_DIM)
    key_heads = key_rows.reshape(LONG_LEN, HEADS, HEAD_DIM)
    value_heads = values.reshape(LONG_LEN, HEADS, HEAD_DIM)
    span = jnp.where(bucket_one > 0, LONG_LEN, SHORT_LEN).astype(jnp.int32)
    key_pos = jnp.arange(LONG_LEN, dtype=jnp.int32)

    def one_block(operands):
        query_block, row_begin = operands
        row_pos = row_begin + jnp.arange(SHORT_LEN, dtype=jnp.int32)
        allowed = (row_pos[:, None] // span == key_pos[None, :] // span) & (key_pos[None, :] <= row_pos[:, None])
        scores = low_back(jnp.einsum('qhd,khd->hqk', query_block, key_heads, precision=HIGH) * score_scale)
        scores = jnp.where(allowed[None], scores, -1e+30)
        row_peak = lax.optimization_barrier(jnp.max(scores, axis=-1, keepdims=True))
        exp_scores = jnp.exp(scores - row_peak)
        weights = low(exp_scores / lax.optimization_barrier(jnp.sum(exp_scores, axis=-1, keepdims=True)))
        return jnp.einsum('hqk,khd->qhd', weights, value_heads, precision=HIGH)
    starts = jnp.arange(block_count, dtype=jnp.int32) * SHORT_LEN
    blocks = lax.map(jax.checkpoint(one_block), (query_blocks, starts))
    return blocks.reshape(LONG_LEN, HEADS * HEAD_DIM)

def slab_forward(slab_rows, params, bucket_one):
    norm1_gain, norm1_bias, qkv_weight, qv_bias, inner_gain, inner_bias, out_weight, out_bias, norm2_gain, norm2_bias, fc1_weight, fc1_bias, ffn_gain, ffn_bias, fc2_weight, fc2_bias = params
    first_act = low(layer_norm(slab_rows, norm1_gain, norm1_bias))
    queries = low(low_back(product(first_act, qkv_weight[0]) + qv_bias[0]))
    key_rows = low(low_back(product(first_act, qkv_weight[1])))
    values = low(low_back(product(first_act, qkv_weight[2]) + qv_bias[1]))
    attended = low_back(attention(queries, key_rows, values, bucket_one))
    inner_act = low(layer_norm(attended, inner_gain, inner_bias))
    resid_mid = slab_rows + low_back(product(inner_act, out_weight) + out_bias)
    second_act = low(layer_norm(resid_mid, norm2_gain, norm2_bias))
    pre_act = low_back(product(second_act, fc1_weight) + fc1_bias)
    hid_act = low(layer_norm(jax.nn.gelu(pre_act, approximate=False), ffn_gain, ffn_bias))
    return resid_mid + product(hid_act, fc2_weight) + fc2_bias

def reference(inputs, bucket, norm1_gain, norm1_bias, qkv_weight, qv_bias, inner_gain, inner_bias, out_weight, out_bias, norm2_gain, norm2_bias, fc1_weight, fc1_bias, ffn_gain, ffn_bias, fc2_weight, fc2_bias, cotangent):
    params = tuple((element.astype(jnp.float32) for element in (norm1_gain, norm1_bias, qkv_weight, qv_bias, inner_gain, inner_bias, out_weight, out_bias, norm2_gain, norm2_bias, fc1_weight, fc1_bias, ffn_gain, ffn_bias, fc2_weight, fc2_bias)))
    slab_inputs = jnp.moveaxis(inputs, 1, 0).astype(jnp.float32)
    slab_cots = jnp.moveaxis(cotangent, 1, 0).astype(jnp.float32)
    zeros = tuple((jnp.zeros_like(element) for element in params))

    def step(running, element):
        slab_in, bucket_one, slab_cot = element

        def forward(slab_rows, weights):
            return slab_forward(slab_rows, weights, bucket_one)
        result, pullback = jax.vjp(forward, slab_in, params)
        grad_rows, grad_params = pullback(slab_cot)
        return (jax.tree.map(jnp.add, running, grad_params), (result.astype(jnp.bfloat16), grad_rows.astype(jnp.bfloat16)))
    running, (results, row_grads) = lax.scan(step, zeros, (slab_inputs, bucket, slab_cots))
    return (jnp.moveaxis(results, 0, 1), jnp.moveaxis(row_grads, 0, 1), running[2], running[6], running[10], running[14], running[3], running[4], running[5], running[11], running[12], running[13], running[0], running[1], running[7], running[8], running[9], running[15])
```

```python
import functools

import jax
import jax.numpy as jnp
from jax import lax
from jax.experimental import pallas as pl
from jax.experimental.pallas import tpu as pltpu
from jax.sharding import PartitionSpec as P


HEAD = "head"
DP = "dp"
HEAD_DIM = 64
EPS = 1e-05
NEG = -1e30
F32 = jnp.float32
BF16 = jnp.bfloat16
SQRT_HALF = 0.7071067811865476
INV_SQRT_2PI = 0.3989422804014327


def dot(left, right, contract):
    return lax.dot_general(left, right, ((contract[0:1], contract[1:2]), ((), ())), preferred_element_type=F32)


def diag_mask(scores):
    key_pos = lax.broadcasted_iota(jnp.int32, scores.shape, 0)
    row_pos = lax.broadcasted_iota(jnp.int32, scores.shape, 1)
    return key_pos <= row_pos


def spans(qkv):
    rows = qkv[0].shape[1]
    half = rows // 2
    result = [(slot, slice(0, rows), qkv[slot]) for slot in range(3)]
    return result + [(3, slice(0, half), qkv[3]), (3, slice(half, rows), qkv[4])]


def attend_kernel(heads, info, *refs):
    slots = 4
    qkv = refs[0:5]
    outs = refs[5:9]
    lse_ref = refs[9]
    q_s, k_s, v_s, o_s = refs[10:14]
    width = heads * HEAD_DIM
    scale = HEAD_DIM ** (-0.5)
    for slot, span, array in spans(qkv):
        block = info[slot]
        q_s[block, :, span] = array[0:width, :] * jnp.asarray(scale, BF16)
        v_s[block, :, span] = array[2 * width : 3 * width, :]
        for head in range(heads):
            low = width + head * HEAD_DIM
            k_s[block, head, span, :] = turn(array[low : low + HEAD_DIM, :])
    is_long = info[4]

    def step(row, key, carry, first):
        result = []
        for head in range(heads):
            part = pl.ds(head * HEAD_DIM, HEAD_DIM)
            scores = dot(k_s[key, head], q_s[row, part, :], (1, 0))
            if first:
                scores = jnp.where(diag_mask(scores), scores, NEG)
                peak = jnp.max(scores, axis=0, keepdims=True)
                weights = jnp.exp(scores - peak)
                total = jnp.sum(weights, axis=0, keepdims=True)
                mixed = dot(v_s[key, part, :], weights.astype(BF16), (1, 0))
            else:
                old_peak, old_total, old_mixed = carry[head]
                peak = jnp.maximum(old_peak, jnp.max(scores, axis=0, keepdims=True))
                fade = jnp.exp(old_peak - peak)
                weights = jnp.exp(scores - peak)
                total = old_total * fade + jnp.sum(weights, axis=0, keepdims=True)
                mixed = old_mixed * fade + dot(v_s[key, part, :], weights.astype(BF16), (1, 0))
            result.append((peak, total, mixed))
        return tuple(result)

    def row_block(row, unused):
        carry = step(row, row, None, True)
        low = jnp.where(is_long > 0, 0, row)
        carry = lax.fori_loop(low, row, lambda key, c: step(row, key, c, False), carry)
        for head in range(heads):
            peak, total, mixed = carry[head]
            o_s[row, pl.ds(head * HEAD_DIM, HEAD_DIM), :] = (mixed / total).astype(BF16)
            lse_ref[row, pl.ds(head, 1), :] = peak + jnp.log(total)
        return unused

    lax.fori_loop(0, slots, row_block, 0)
    for slot in range(slots):
        outs[slot][...] = o_s[info[slot]]


def back_step(heads, row, key, carry, first, arrays, grad_out):
    q_s, qr_s, k_s, kr_s, vr_s, g_s, gr_s, delta_s, lse_ref = arrays
    result = []
    for head in range(heads):
        part = pl.ds(head * HEAD_DIM, HEAD_DIM)
        scores = dot(kr_s[key, head], q_s[row, part, :], (1, 0))
        weights = jnp.exp(scores - lse_ref[row, pl.ds(head, 1), :])
        if first:
            weights = jnp.where(diag_mask(scores), weights, 0.0)
        grad_weights = dot(vr_s[key, head], g_s[row, part, :], (1, 0))
        grad_scores = (weights * (grad_weights - delta_s[row, pl.ds(head, 1), :])).astype(BF16)
        grad_out(key, head, dot(grad_scores, qr_s[row, head], (1, 0)), dot(weights.astype(BF16), gr_s[row, head], (1, 0)))
        grad_query = dot(k_s[key, part, :], grad_scores, (1, 0))
        result.append(grad_query if first else carry[head] + grad_query)
    return tuple(result)


def early_kernel(heads, info, *refs):
    qkv = refs[0:5]
    mixed = refs[5:9]
    grads = refs[9:13]
    lse_ref = refs[13]
    q_s, qr_s, k_s, kr_s, vr_s, g_s, gr_s, delta_s, dq_s, dk_s, dv_s = refs[14:25]
    width = heads * HEAD_DIM
    scale = HEAD_DIM ** (-0.5)
    for slot, span, array in spans(qkv):
        block = info[slot]
        scaled = array[0:width, :] * jnp.asarray(scale, BF16)
        q_s[block, :, span] = scaled
        k_s[block, :, span] = array[width : 2 * width, :]
        for head in range(heads):
            low = head * HEAD_DIM
            high = low + HEAD_DIM
            qr_s[block, head, span, :] = turn(scaled[low:high, :])
            kr_s[block, head, span, :] = turn(array[width + low : width + high, :])
            vr_s[block, head, span, :] = turn(array[2 * width + low : 2 * width + high, :])
    for slot in range(4):
        block = info[slot]
        g_s[block] = grads[slot][...]
        for head in range(heads):
            low = head * HEAD_DIM
            high = low + HEAD_DIM
            gr_s[block, head] = turn(grads[slot][low:high, :])
            product = grads[slot][low:high, :].astype(F32) * mixed[slot][low:high, :].astype(F32)
            delta_s[block, pl.ds(head, 1), :] = jnp.sum(product, axis=0, keepdims=True)
    is_long = info[4]
    arrays = (q_s, qr_s, k_s, kr_s, vr_s, g_s, gr_s, delta_s, lse_ref)

    def write(key, head, grad_key, grad_value):
        dk_s[key, head] = grad_key
        dv_s[key, head] = grad_value

    def add(key, head, grad_key, grad_value):
        dk_s[key, head] += grad_key
        dv_s[key, head] += grad_value

    def row_block(row, unused):
        carry = back_step(heads, row, row, None, True, arrays, write)
        low = jnp.where(is_long > 0, 0, row)
        carry = lax.fori_loop(
            low, row, lambda key, c: back_step(heads, row, key, c, False, arrays, add), carry
        )
        for head in range(heads):
            dq_s[row, pl.ds(head * HEAD_DIM, HEAD_DIM), :] = (carry[head] * scale).astype(BF16)
        return unused

    lax.fori_loop(0, 3, row_block, 0)


def late_kernel(heads, info, *refs):
    arrays = refs[0:8] + (refs[11],)
    dq_in, dk_in, dv_in = refs[8:11]
    outs = refs[12:17]
    dq_s, dk_s, dv_s = refs[17:20]
    width = heads * HEAD_DIM
    scale = HEAD_DIM ** (-0.5)
    is_long = info[4]
    last = 3
    dq_s[0:last] = dq_in[0:last]

    def write(key, head, grad_key, grad_value):
        dk_s[key, head] = grad_key
        dv_s[key, head] = grad_value

    def add(key, head, grad_key, grad_value):
        dk_s[key, head] = dk_in[key, head] + grad_key
        dv_s[key, head] = dv_in[key, head] + grad_value

    carry = back_step(heads, last, last, None, True, arrays, write)
    low = jnp.where(is_long > 0, 0, last)
    carry = lax.fori_loop(low, last, lambda key, c: back_step(heads, last, key, c, False, arrays, add), carry)
    for head in range(heads):
        dq_s[last, pl.ds(head * HEAD_DIM, HEAD_DIM), :] = (carry[head] * scale).astype(BF16)

    @pl.when(is_long == 0)
    def _():
        dk_s[0:last] = dk_in[0:last]
        dv_s[0:last] = dv_in[0:last]

    for slot, span, array in spans(outs):
        block = info[slot]
        array[0:width, :] = dq_s[block, :, span]
        for head in range(heads):
            low = width + head * HEAD_DIM
            array[low : low + HEAD_DIM, :] = dk_s[block, head, span, :].T.astype(BF16)
            low = low + width
            array[low : low + HEAD_DIM, :] = dv_s[block, head, span, :].T.astype(BF16)


def turn(value):
    return value.astype(F32).T.astype(BF16)


def vmem_specs(count):
    return [pl.BlockSpec(memory_space=pltpu.VMEM)] * count


def footprint(array):
    shape = (1,) * (2 - len(array.shape)) + tuple(array.shape)
    size = jnp.dtype(array.dtype).itemsize
    rows = -(-shape[-2] // 8) * 8 if shape[-2] > 1 else 1
    lanes = -(-shape[-1] // 128) * 128
    total = rows * lanes * size
    for extent in shape[:-2]:
        total *= extent
    return total


def limit(arrays):
    total = sum(footprint(array) for array in arrays) + SPARE
    return pltpu.CompilerParams(vmem_limit_bytes=total)


SPARE = 6 * 1024 * 1024


def attend(info, qkv, heads):
    rows = qkv[0].shape[1]
    width = heads * HEAD_DIM
    flat = struct((4, width, rows), BF16)
    scratch = [flat, struct((4, heads, rows, HEAD_DIM), BF16), flat, flat]
    outs = [struct((width, rows), BF16)] * 4 + [struct((4, heads, rows), F32)]
    flops = 40 * heads * HEAD_DIM * rows * rows
    result = run(functools.partial(attend_kernel, heads), info, qkv, outs, scratch, flops)
    return result[:4], result[4]


def attend_back(info, qkv, mixed, grads, lse, heads):
    rows = qkv[0].shape[1]
    width = heads * HEAD_DIM
    flat = struct((4, width, rows), BF16)
    turned = struct((4, heads, rows, HEAD_DIM), BF16)
    total = struct((4, heads, rows, HEAD_DIM), F32)
    outs = [flat, turned, flat, turned, turned, flat, turned, struct((4, heads, rows), F32), flat, total, total]
    flops = 50 * heads * HEAD_DIM * rows * rows
    kernel = functools.partial(early_kernel, heads)
    kept = run(kernel, info, (*qkv, *mixed, *grads, lse), outs, [], flops)
    outs = [struct((3 * width, rows), BF16)] * 3 + [struct((3 * width, rows // 2), BF16)] * 2
    kernel = functools.partial(late_kernel, heads)
    return run(kernel, info, (*kept, lse), outs, [flat, total, total], flops)


ROWS = 128


def fold(value):
    total = value[:, 0:128]
    for place in range(128, value.shape[1], 128):
        total = total + value[:, place : place + 128]
    return total


def row_sum(value):
    return jnp.sum(value, axis=1, keepdims=True)


def col_sum(value):
    return jnp.sum(value, axis=0, keepdims=True)


def blocks(rows):
    return [slice(low, low + ROWS) for low in range(0, rows, ROWS)]


def mid_kernel(
    info, mix_own, mix_a, mix_b, mix_d, vec_own, vec_a, vec_b, vec_d, w_own, w_near, w_far, w_b, w_other, rows_ref,
    params, resid_ref, second_ref, turned_ref, hat_ref, inv_ref, act_ref, wo_ref, cols_ref, side_s
):
    core = info[5]
    model = rows_ref.shape[1]
    mixes = (mix_own, mix_a, mix_b, mix_d)
    vecs = (vec_own, vec_a, vec_b, vec_d)
    dim = mix_own.shape[0]
    count = 4 * dim
    half = dim // 2
    split = model // 2
    total = 0.0
    for mix in mixes:
        total = total + col_sum(mix[...].astype(F32))
    mean = total / count
    square = 0.0
    for mix in mixes:
        centred = mix[...].astype(F32) - mean
        square = square + col_sum(centred * centred)
    inv = lax.rsqrt(square / count + EPS)
    inv_ref[...] = inv
    side_s[:, pl.ds(pl.multiple_of(core * split, 128), split)] = w_far[...]
    side_s[:, pl.ds(pl.multiple_of((1 - core) * split, 128), split)] = w_other[...]
    weights = (w_own, w_near, w_b, side_s)
    for slot in range(4):
        cols = vecs[slot][...].T
        for other in range(2):
            part = slice(other * half, other * half + half)
            low = (slot * 2 + other) * 128
            mine = slice(low, low + half)
            pad = slice(low + half, low + 128)
            wo_ref[mine, :] = weights[slot][part, :]
            wo_ref[pad, :] = jnp.zeros((128 - half, model), BF16)
            hat = (mixes[slot][part, :].astype(F32) - mean) * inv
            hat_ref[mine, :] = hat
            hat_ref[pad, :] = jnp.zeros((128 - half, hat.shape[1]), F32)
            cols_ref[mine, :] = cols[part, 3:5]
            cols_ref[pad, :] = jnp.zeros((128 - half, 2), F32)
            act = hat * cols[part, 3:4] + cols[part, 4:5]
            act_ref[:, mine] = turn(act)
            act_ref[:, pad] = jnp.zeros((act_ref.shape[0], 128 - half), BF16)
    for part in blocks(rows_ref.shape[0]):
        branch = dot(act_ref[part, :], wo_ref[...], (1, 0))
        resid = rows_ref[part, :].astype(F32) + branch + params[2:3, :]
        resid_ref[part, :] = resid
        centred = resid - row_sum(resid) / model
        scale = lax.rsqrt(row_sum(centred * centred) / model + EPS)
        second = centred * scale * params[3:4, :] + params[4:5, :]
        second_ref[part, :] = second.astype(BF16)
        turned_ref[:, part] = turn(second)


def expand_kernel(last, info, *refs):
    if last:
        vec_b, vec_d, w_b, w_far, w_other, second, sum_in, square_in = refs[:8]
        hidden, slope, vecs, mean_ref, inv_ref, w_s = refs[8:]
    else:
        vec_own, vec_a, w_own, w_near, second = refs[:5]
        hidden, slope, vecs, sum_ref, square_ref = refs[5:]
    units = hidden.shape[2]
    split = units // 2
    core = info[5]
    if last:
        vecs[0] = vec_b[...]
        vecs[1, :, 0:split] = vec_d[:, pl.ds(pl.multiple_of(core * split, 128), split)]
        vecs[1, :, split:units] = vec_d[:, pl.ds(pl.multiple_of((1 - core) * split, 128), split)]
        w_s[:, 0:split] = w_far[...]
        w_s[:, split:units] = w_other[...]
        pairs = (w_b, w_s)
    else:
        vecs[0] = vec_own[...]
        vecs[1] = vec_a[...]
        pairs = (w_own, w_near)
    for part in blocks(second.shape[0]):
        sums = sum_in[part, :] if last else 0.0
        squares = square_in[part, :] if last else 0.0
        for pair in range(2):
            pre = dot(second[part, :], pairs[pair][...], (1, 0)) + vecs[pair, 0:1, :]
            phi = 0.5 + 0.5 * lax.erf(pre * SQRT_HALF)
            act = pre * phi
            hidden[pair, part, :] = act.astype(BF16)
            slope[pair, part, :] = (phi + pre * (INV_SQRT_2PI * jnp.exp(-0.5 * (pre * pre)))).astype(BF16)
            sums = sums + fold(act)
            squares = squares + fold(act * act)
        if last:
            mean = row_sum(sums) / (4 * units)
            mean_ref[part, :] = mean
            inv_ref[part, :] = lax.rsqrt(row_sum(squares) / (4 * units) - mean * mean + EPS)
        else:
            sum_ref[part, :] = sums
            square_ref[part, :] = squares


def put_first(core, pair, value, own, near):
    target = own if pair == 0 else near
    split = value.shape[1] // 2
    target[core] = value[:, 0:split].astype(BF16)
    target[1 - core] = value[:, split:].astype(BF16)


def put_last(core, pair, value, far, rest):
    split = value.shape[1] // 2
    if pair == 0:
        rest[1 - core] = value[:, 0:split].astype(BF16)
        rest[core] = value[:, split:].astype(BF16)
    else:
        far[0] = value[:, 0:split].astype(BF16)
        rest[2] = value[:, split:].astype(BF16)


def contract_kernel(last, info, *refs):
    if last:
        hidden, vecs, w_b, w_far, w_other, cot, turned, mean, inv, total_in, sum_in, dot_in, resid, params = refs[:14]
        out, grad_hid, far, rest, sums, hat_sum, hat_dot, w_s, act_s = refs[14:]
    else:
        hidden, vecs, w_own, w_near, cot, turned, mean, inv = refs[:8]
        total, grad_hid, own, near, sums, sum_ref, dot_ref, act_s = refs[8:]
    units = hidden.shape[2]
    core = info[5]
    if last:
        w_s[0 : units // 2, :] = w_far[...]
        w_s[units // 2 : units, :] = w_other[...]
        pairs = (w_b, w_s)
    else:
        pairs = (w_own, w_near)
    by_gain = [0.0, 0.0]
    by_bias = [0.0, 0.0]
    for part in blocks(cot.shape[0]):
        shift = mean[part, :]
        scale = inv[part, :]
        hat_sums = sum_in[part, :] if last else 0.0
        hat_dots = dot_in[part, :] if last else 0.0
        ffn = total_in[part, :] if last else 0.0
        for pair in range(2):
            gain = vecs[pair, 1:2, :]
            grad = dot(cot[part, :], pairs[pair][...], (1, 1))
            grad_hid[pair, part, :] = grad.astype(BF16)
            hat = (hidden[pair, part, :].astype(F32) - shift) * scale
            act = (hat * gain + vecs[pair, 2:3, :]).astype(BF16)
            act_s[pair, part, :] = act
            product = grad * hat
            hat_sums = hat_sums + fold(grad * gain)
            hat_dots = hat_dots + fold(product * gain)
            by_gain[pair] = by_gain[pair] + col_sum(product)
            by_bias[pair] = by_bias[pair] + col_sum(grad)
            ffn = ffn + dot(act, pairs[pair][...], (1, 0))
        if last:
            out[part, :] = (resid[part, :] + ffn + params[5:6, :]).astype(BF16)
            hat_sum[part, :] = row_sum(hat_sums) / (4 * units)
            hat_dot[part, :] = row_sum(hat_dots) / (4 * units)
        else:
            total[part, :] = ffn
            sum_ref[part, :] = hat_sums
            dot_ref[part, :] = hat_dots
    for pair in range(2):
        sums[pair, 0:1, :] = by_gain[pair]
        sums[pair, 1:2, :] = by_bias[pair]
        value = dot(turned[...], act_s[pair], (1, 0))
        if last:
            put_last(core, pair, value, far, rest)
        else:
            put_first(core, pair, value, own, near)


def back_kernel(last, info, *refs):
    if last:
        hidden, slope, grad_hid, vecs, w_b, w_far, w_other, turned, mean, inv, hat_sum, hat_dot = refs[:12]
        total, far, rest, sums, w_s, pre_s = refs[12:]
    else:
        hidden, slope, grad_hid, vecs, w_own, w_near, turned, mean, inv, hat_sum, hat_dot, total_in = refs[:12]
        total, own, near, sums, pre_s = refs[12:]
    units = hidden.shape[2]
    core = info[5]
    if last:
        w_s[:, 0 : units // 2] = w_far[...]
        w_s[:, units // 2 : units] = w_other[...]
        pairs = (w_b, w_s)
    else:
        pairs = (w_own, w_near)
    by_bias = [0.0, 0.0]
    for part in blocks(hidden.shape[1]):
        shift = mean[part, :]
        scale = inv[part, :]
        second = 0.0 if last else total_in[part, :]
        for pair in range(2):
            hat = (hidden[pair, part, :].astype(F32) - shift) * scale
            grad = grad_hid[pair, part, :].astype(F32) * vecs[pair, 1:2, :] - hat_sum[part, :] - hat * hat_dot[part, :]
            pre = (scale * grad * slope[pair, part, :].astype(F32)).astype(BF16)
            pre_s[pair, part, :] = pre
            by_bias[pair] = by_bias[pair] + col_sum(pre.astype(F32))
            second = second + dot(pre, pairs[pair][...], (1, 1))
        total[part, :] = second
    for pair in range(2):
        sums[pair, 0:1, :] = by_bias[pair]
        value = dot(turned[...], pre_s[pair], (1, 0))
        if last:
            put_last(core, pair, value, far, rest)
        else:
            put_first(core, pair, value, own, near)


def tail_kernel(
    info, total, resid, cot, params, hat_in, inv_in, act_in, wo, cols, sums_c0, sums_c1, sums_b0, sums_b1, own, near,
    far, rest, mid_ref, ga_own, ga_a, ga_b, ga_d, turned_s, gi_s, og_s, low_s, wide_s, slim_s
):
    rows, model = cot.shape
    core = info[5]
    to_gain = to_bias = to_out = to_last = 0.0
    for part in blocks(rows):
        centred = resid[part, :]
        centred = centred - row_sum(centred) / model
        scale = lax.rsqrt(row_sum(centred * centred) / model + EPS)
        hat = centred * scale
        up = total[part, :]
        grad = up * params[3:4, :]
        back = scale * (grad - row_sum(grad) / model - hat * (row_sum(grad * hat) / model))
        wide = cot[part, :].astype(F32)
        mid = wide + back
        mid_ref[part, :] = mid
        low = mid.astype(BF16)
        low_s[part, :] = low
        turned_s[:, part] = turn(low)
        to_gain = to_gain + col_sum(up * hat)
        to_bias = to_bias + col_sum(up)
        to_out = to_out + col_sum(low.astype(F32))
        to_last = to_last + col_sum(wide)
    gi_s[...] = dot(wo[...], turned_s[...], (1, 0))
    og_s[...] = dot(turned_s[...], act_in[...], (1, 0)).astype(BF16)
    features = 4 * ga_own.shape[0]
    half = ga_own.shape[0] // 2
    first = 0.0
    second = 0.0
    lane = lax.broadcasted_iota(jnp.int32, (128, 128), 1)
    for tile in range(8):
        part = slice(tile * 128, tile * 128 + 128)
        up = gi_s[part, :]
        hat = hat_in[part, :]
        side = jnp.where(lane == 0, row_sum(up * hat), jnp.where(lane == 1, row_sum(up), 0.0)).T
        slim_s[tile] = side[0:8, :]
        grad = up * cols[part, 0:1]
        gi_s[part, :] = grad
        first = first + col_sum(grad)
        second = second + col_sum(grad * hat)
    first = first / features
    second = second / features
    outs = (ga_own, ga_a, ga_b, ga_d)
    for tile in range(8):
        part = slice(tile * 128, tile * 128 + half)
        back = inv_in[...] * (gi_s[part, :] - first - hat_in[part, :] * second)
        low = (tile % 2) * half
        outs[tile // 2][low : low + half, :] = back.astype(BF16)
    split = sums_c0.shape[2] // 2
    whole_rows = (to_out, to_gain, to_bias, to_last)
    for pair in range(4):
        contract = (sums_c0, sums_c0, sums_c1, sums_c1)[pair]
        backward = (sums_b0, sums_b0, sums_b1, sums_b1)[pair]
        for other in range(2):
            base = other * split
            index = pair * 2 + other
            for place in range(split // 128):
                lanes = slice(base + place * 128, base + place * 128 + 128)
                wide_s[index, place : place + 1, :] = backward[pair % 2, 0:1, lanes]
                wide_s[index, 3 + place : 4 + place, :] = contract[pair % 2, 0:1, lanes]
                wide_s[index, 6 + place : 7 + place, :] = contract[pair % 2, 1:2, lanes]
                for row in range(4):
                    spot = 9 + 3 * row + place
                    if pair < 3:
                        wide_s[index, spot : spot + 1, :] = whole_rows[row][:, lanes]
                    else:
                        mine = slice(place * 128, place * 128 + 128)
                        yours = slice(split + place * 128, split + place * 128 + 128)
                        swap = core if other == 0 else 1 - core
                        value = jnp.where(swap == 0, whole_rows[row][:, mine], whole_rows[row][:, yours])
                        wide_s[index, spot : spot + 1, :] = value

    def write(target, place, tile, index, inner):
        target[place, 0:model, :] = og_s[:, tile]
        target[place, model : model + 21, :] = wide_s[index, 0:21, :].astype(BF16)
        target[place, model + 21 : model + 23, :] = inner[0:2, :].astype(BF16)
        target[place, model + 23 : model + 32, :] = jnp.zeros((9, 128), BF16)

    for other in range(2):
        swap = core if other == 0 else 1 - core
        write(own, swap, slice(other * 128, other * 128 + 128), other, slim_s[other])
        write(near, swap, slice((2 + other) * 128, (2 + other) * 128 + 128), 2 + other, slim_s[2 + other])
        write(rest, 1 - swap, slice((4 + other) * 128, (4 + other) * 128 + 128), 4 + other, slim_s[4 + other])
    write(far, 0, pl.ds(pl.multiple_of((6 + core) * 128, 128), 128), 6, slim_s[6 + core])
    write(rest, 2, pl.ds(pl.multiple_of((7 - core) * 128, 128), 128), 7, slim_s[7 - core])


def struct(shape, kind):
    return jax.ShapeDtypeStruct(shape, kind)


def run(kernel, info, operands, outs, scratch, flops):
    specs = vmem_specs(len(operands))
    return pl.pallas_call(
        kernel,
        out_shape=outs,
        in_specs=[pl.BlockSpec(memory_space=pltpu.SMEM)] + specs,
        out_specs=vmem_specs(len(outs)),
        scratch_shapes=[pltpu.VMEM(value.shape, value.dtype) for value in scratch],
        cost_estimate=pl.CostEstimate(flops=flops, transcendentals=0, bytes_accessed=8 << 20),
        compiler_params=limit(scratch),
    )(info, *operands)


def mid_block(info, mixes, vecs, pieces, rows, params):
    count, model = rows.shape
    dim = mixes[0].shape[0]
    operands = (*mixes, *vecs, *pieces, rows, params)
    wide = 8 * 128
    outs = [
        struct((count, model), F32),
        struct((count, model), BF16),
        struct((model, count), BF16),
        struct((wide, count), F32),
        struct((1, count), F32),
        struct((count, wide), BF16),
        struct((wide, model), BF16),
        struct((wide, 2), F32),
    ]
    scratch = [struct((dim, model), BF16)]
    return run(mid_kernel, info, operands, outs, scratch, 2 * count * model * wide)


def expand_block(info, last, vecs, pieces, second, sums):
    count, model = second.shape
    own, near, far, w_b, other = pieces
    units = near.shape[1]
    column = struct((count, 1), F32)
    partial = struct((count, 128), F32)
    outs = [struct((2, count, units), BF16)] * 2 + [struct((2, 8, units), F32)]
    flops = 8 * count * model * units
    kernel = functools.partial(expand_kernel, last)
    if last:
        operands = (*vecs[2:], w_b, far, other, second, *sums)
        scratch = [struct((model, units), BF16)]
        return run(kernel, info, operands, outs + [column] * 2, scratch, flops)
    operands = (*vecs[:2], own, near, second)
    return run(kernel, info, operands, outs + [partial] * 2, [], flops)


def grad_outs(last, model, split):
    if last:
        return [struct((1, model, split), BF16), struct((3, model, split), BF16)]
    return [struct((2, model, split), BF16)] * 2


def contract_block(info, last, hidden, vecs, pieces, cot, turned, mean, inv, more):
    count, model = cot.shape
    units = hidden.shape[2]
    own, near, far, w_b, other = pieces
    column = struct((count, 1), F32)
    partial = struct((count, 128), F32)
    act = struct((2, count, units), BF16)
    grads = grad_outs(last, model, units // 2)
    shared = [struct((2, count, units), BF16)] + grads + [struct((2, 8, units), F32)]
    flops = 12 * count * model * units
    kernel = functools.partial(contract_kernel, last)
    if last:
        operands = (hidden, vecs, w_b, far, other, cot, turned, mean, inv, *more)
        outs = [struct((count, model), BF16)] + shared + [column] * 2
        scratch = [struct((units, model), BF16), act]
        return run(kernel, info, operands, outs, scratch, flops)
    operands = (hidden, vecs, own, near, cot, turned, mean, inv)
    outs = [struct((count, model), F32)] + shared + [partial] * 2
    return run(kernel, info, operands, outs, [act], flops)


def back_block(info, last, hidden, slope, grad_hid, vecs, pieces, turned, columns, more):
    count, units = hidden.shape[1:]
    model = turned.shape[0]
    own, near, far, w_b, other = pieces
    pre = struct((2, count, units), BF16)
    outs = [struct((count, model), F32)] + grad_outs(last, model, units // 2) + [struct((2, 8, units), F32)]
    flops = 8 * count * model * units
    kernel = functools.partial(back_kernel, last)
    if last:
        operands = (hidden, slope, grad_hid, vecs, w_b, far, other, turned, *columns)
        scratch = [struct((model, units), BF16), pre]
        return run(kernel, info, operands, outs, scratch, flops)
    operands = (hidden, slope, grad_hid, vecs, own, near, turned, *columns, *more)
    return run(kernel, info, operands, outs, [pre], flops)


EXTRA = 32


def tail_block(info, total, resid, cot, params, hat_in, inv_in, act_in, wo, cols, sums, dim):
    count, model = cot.shape
    operands = (total, resid, cot, params, hat_in, inv_in, act_in, wo, cols, *sums)
    outs = [struct((places, model + EXTRA, 128), BF16) for places in (2, 2, 1, 3)]
    outs += [struct((count, model), F32)] + [struct((dim, count), BF16)] * 4
    scratch = [
        struct((model, count), BF16),
        struct((8 * 128, count), F32),
        struct((model, 8 * 128), BF16),
        struct((count, model), BF16),
        struct((8, 24, 128), F32),
        struct((8, 8, 128), F32),
    ]
    return run(tail_kernel, info, operands, outs, scratch, 4 * count * model * 1024)


class Links:
    def __init__(self):
        self.ranks = lax.axis_size(HEAD)
        self.parts = lax.axis_size(DP)
        self.core = lax.rem(lax.axis_index(DP), 2)

    def over(self, value, near, far):
        pairs = []
        for rank in range(self.ranks):
            for part in range(self.parts):
                flip = near if part % 2 == 0 else far
                pairs.append((rank * self.parts + part, (rank ^ flip) * self.parts + part))
        return lax.ppermute(value, (HEAD, DP), pairs)

    def a(self, value):
        return self.over(value, 1, 2)

    def b(self, value):
        return self.over(value, 2, 1)

    def d(self, value):
        return self.over(value, 3, 3)

    def dp(self, value, flip):
        return lax.ppermute(value, DP, [(part, part ^ flip) for part in range(self.parts)])


def gather_weight(links, own, axis):
    near = links.a(own)
    shape = list(own.shape)
    shape[axis] //= 2
    (half,) = simple(functools.partial(half_kernel, axis), links.info, (near,), [struct(tuple(shape), BF16)])
    far = links.b(half)
    return own, near, far, links.dp(near, 1), links.dp(far, 1)


def join_core_kernel(info, near, far, got, near_out, far_out):
    count = near.shape[0]

    def step(place, unused):
        for tile in range(count):
            total = near[tile, place].astype(F32) + got[tile, place].astype(F32)
            near_out[tile, place] = total.astype(BF16)
        total = far[0, place].astype(F32) + got[count, place].astype(F32)
        far_out[0, place] = total.astype(BF16)
        return unused

    lax.fori_loop(0, near.shape[1], step, 0)


def join_far_kernel(info, near, got, near_out):
    def step(place, unused):
        total = near[0, place].astype(F32) + got[0, place].astype(F32)
        near_out[0, place] = total.astype(BF16)
        near_out[1, place] = near[1, place]
        return unused

    lax.fori_loop(0, near.shape[1], step, 0)


def simple(kernel, info, operands, outs, scratch=()):
    return run(kernel, info, operands, outs, list(scratch), 1 << 28)


def halve_kernel(swap, extra, per, level, info, value, got, keep, send):
    tiles = value.shape[0]
    blocks = value.shape[1] - extra
    bit = info[7 + level]

    def step(place, unused):
        group = place // per
        for tile in range(tiles):
            other = tiles - 1 - tile if swap else tile
            mine = place + (group + bit) * per
            yours = place + (group + 1 - bit) * per
            keep[tile, place] = value[tile, mine].astype(F32) + got[tile, mine].astype(F32)
            total = value[tile, yours].astype(F32) + got[tile, yours].astype(F32)
            send[other, place] = total.astype(BF16)
        return unused

    lax.fori_loop(0, blocks // 2, step, 0)
    for place in range(extra):
        for tile in range(tiles):
            other = tiles - 1 - tile if swap else tile
            total = value[tile, blocks + place].astype(F32) + got[tile, blocks + place].astype(F32)
            keep[tile, blocks // 2 + place] = total
            send[other, blocks // 2 + place] = total.astype(BF16)


def weight_kernel(extra, per, info, *refs):
    acts, grads = refs[0:5], refs[5:10]
    own, got, keep, send, total_s = refs[10:15]
    width = grads[0].shape[0]
    base = keep.shape[3] - 256
    rows = keep.shape[2]
    blocks = own.shape[1] - extra
    bit = info[7]
    total = 0.0
    tokens = 0.0
    for act, grad in zip(acts, grads):
        total = total + dot(grad[...], act[...], (1, 0))
        tokens = tokens + fold(grad[...].astype(F32))
    total = total.T
    for place in range(blocks):
        total_s[place] = total[place * rows : place * rows + rows, :]
    tokens = jnp.broadcast_to(row_sum(tokens), (width, 128)).T[0:1, :]

    def step(place, unused):
        mine = place + (place // per + bit) * per
        yours = place + (place // per + 1 - bit) * per
        keep[0, place, :, 0:width] = total_s[mine]
        send[0, place, :, 0:width] = total_s[yours].astype(BF16)
        for tile in range(2):
            low = base + tile * 128
            swapped = base + (1 - tile) * 128
            keep[0, place, :, low : low + 128] = own[tile, mine].astype(F32) + got[tile, mine].astype(F32)
            value = own[tile, yours].astype(F32) + got[tile, yours].astype(F32)
            send[0, place, :, swapped : swapped + 128] = value.astype(BF16)
        return unused

    lax.fori_loop(0, blocks // 2, step, 0)
    for place in range(extra):
        spot = blocks // 2 + place
        value = jnp.broadcast_to(tokens, (rows, width))
        keep[0, spot, :, 0:width] = value
        send[0, spot, :, 0:width] = value.astype(BF16)
        for tile in range(2):
            low = base + tile * 128
            swapped = base + (1 - tile) * 128
            value = own[tile, blocks + place].astype(F32) + got[tile, blocks + place].astype(F32)
            keep[0, spot, :, low : low + 128] = value
            send[0, spot, :, swapped : swapped + 128] = value.astype(BF16)


def cot_kernel(info, whole, rows_out, turned, sem):
    count = rows_out.shape[0]
    low = pl.multiple_of(info[6] * count, count)
    copy = pltpu.make_async_copy(whole.at[pl.ds(low, count), :], rows_out, sem)
    copy.start()
    copy.wait()
    for part in blocks(count):
        turned[:, part] = turn(rows_out[part, :])


def cot_block(info, whole, count):
    model = whole.shape[1]
    return pl.pallas_call(
        cot_kernel,
        out_shape=[struct((count, model), BF16), struct((model, count), BF16)],
        in_specs=[pl.BlockSpec(memory_space=pltpu.SMEM), pl.BlockSpec(memory_space=pl.ANY)],
        out_specs=vmem_specs(2),
        scratch_shapes=[pltpu.SemaphoreType.DMA(())],
        cost_estimate=pl.CostEstimate(flops=1 << 28, transcendentals=0, bytes_accessed=4 << 20),
        compiler_params=limit([]),
        name="ct",
    )(info, whole)


def half_kernel(axis, info, value, out):
    size = out.shape[axis]
    part = pl.ds(pl.multiple_of(info[5] * size, 128), size)
    out[...] = value[:, part] if axis else value[part, :]


def halve(links, value, got, flip, extra, per, swap):
    tiles, count, rows, units = value.shape
    shape = (tiles, (count - extra) // 2 + extra, rows, units)
    kernel = functools.partial(halve_kernel, swap, extra, per, flip.bit_length() - 1)
    return simple(kernel, links.info, (value, got), [struct(shape, F32), struct(shape, BF16)])


def block_rows(share):
    return EXTRA if share % EXTRA == 0 else share


def by_part(links, value, extra):
    tiles, rows, units = value.shape
    size = block_rows((rows - extra) // links.parts)
    spare = -rows % size
    if spare:
        value = jnp.concatenate((value, jnp.zeros((tiles, spare, units), value.dtype)), axis=1)
    return value.reshape(tiles, -1, size, units)


def over_head(links, own, near, far, rest, extra):
    own, near, far, rest = [by_part(links, value, extra) for value in (own, near, far, rest)]
    got = links.dp(rest, 1)
    near, far = simple(
        join_core_kernel, links.info, (near, far, got), [struct(near.shape, BF16), struct(far.shape, BF16)]
    )
    got = links.b(far)
    (near,) = simple(join_far_kernel, links.info, (near, got), [struct(near.shape, BF16)])
    return own, links.a(near)


def finish_scatter(links, keep, got, flip, extra, per):
    while flip < links.parts:
        keep, send = halve(links, keep, got, flip, extra, per, False)
        got = links.dp(send, flip)
        flip *= 2
    return keep + got.astype(F32)


def scatter_all(links, own, got):
    per = own.shape[1] // links.parts
    keep, send = halve(links, own, got, 1, 0, per, True)
    got = links.dp(send, 1)
    done = finish_scatter(links, keep, got, 2, 0, per)
    return done.reshape(done.shape[0], -1, done.shape[3])


def pack_kernel(info, fc1_bias, ffn_gain, ffn_bias, inner_gain, inner_bias, qv_bias, vec, column):
    wide = vec.shape[1]
    dim = inner_gain.shape[0]
    vec[...] = jnp.zeros_like(vec)
    for row, value in enumerate((fc1_bias, ffn_gain, ffn_bias)):
        vec[row : row + 1, :] = value[...].astype(F32).reshape(1, wide)
    for row, value in enumerate((inner_gain, inner_bias)):
        vec[3 + row : 4 + row, 0:dim] = value[...].reshape(1, dim)
    zero = jnp.zeros((6, dim), F32)
    turned = jnp.concatenate((qv_bias[...], zero), axis=0).T
    column[0:dim, :] = turned[:, 0:1]
    column[dim : 2 * dim, :] = jnp.zeros((dim, 1), F32)
    column[2 * dim : 3 * dim, :] = turned[:, 1:2]


def first_norm_kernel(info, rows, gain1, bias1, out_bias, gain2, bias2, last_bias, out, params):
    model = rows.shape[1]
    params[...] = jnp.zeros_like(params)
    for row, value in enumerate((gain1, bias1, out_bias, gain2, bias2, last_bias)):
        params[row : row + 1, :] = value[...].reshape(1, model)
    for part in blocks(rows.shape[0]):
        value = rows[part, :].astype(F32)
        centred = value - row_sum(value) / model
        scale = lax.rsqrt(row_sum(centred * centred) / model + EPS)
        out[part, :] = (centred * scale * params[0:1, :] + params[1:2, :]).astype(BF16)


def partial_kernel(info, part_a, part_b, low, high, out_a, out_b):
    half = low.shape[0]
    for part in blocks(half):
        upper = slice(half + part.start, half + part.stop)
        out_a[part, :] = (part_a[part, :] + low[part, :].astype(F32)).astype(BF16)
        out_a[upper, :] = part_a[upper, :].astype(BF16)
        out_b[part, :] = part_b[part, :].astype(BF16)
        out_b[upper, :] = (part_b[upper, :] + high[part, :].astype(F32)).astype(BF16)


def final_kernel(info, rows, params, mid, mine, got_a, got_b, out):
    model = rows.shape[1]
    for part in blocks(rows.shape[0]):
        value = rows[part, :].astype(F32)
        centred = value - row_sum(value) / model
        scale = lax.rsqrt(row_sum(centred * centred) / model + EPS)
        hat = centred * scale
        grad = mine[part, :] + got_a[part, :].astype(F32) + got_b[part, :].astype(F32)
        grad = grad * params[0:1, :]
        back = scale * (grad - row_sum(grad) / model - hat * (row_sum(grad * hat) / model))
        out[part, :] = (mid[part, :] + back).astype(BF16)


def layer(
    inputs,
    bucket,
    norm1_gain,
    norm1_bias,
    qkv_weight,
    qv_bias,
    inner_gain,
    inner_bias,
    out_weight,
    out_bias,
    norm2_gain,
    norm2_bias,
    fc1_weight,
    fc1_bias,
    ffn_gain,
    ffn_bias,
    fc2_weight,
    fc2_bias,
    cotangent,
):
    links = Links()
    core = links.core
    rows = inputs.shape[0]
    model = inputs.shape[2]
    dim = qkv_weight.shape[2]
    heads = dim // HEAD_DIM
    hidden_share = fc1_weight.shape[1]
    units = hidden_share // 2
    rank = lax.axis_index(HEAD)
    part = lax.axis_index(DP)
    bits = []
    while 2 ** len(bits) < links.parts:
        bits.append(lax.rem(part // 2 ** len(bits), 2))
    info = jnp.stack([rank, rank ^ (1 + core), rank ^ (2 - core), rank ^ 3, bucket[0], core, rank] + bits)
    info = info.astype(jnp.int32)
    links.info = info

    own_rows = inputs.reshape(rows, model)
    first_own, params = simple(
        first_norm_kernel,
        info,
        (own_rows, norm1_gain, norm1_bias, out_bias, norm2_gain, norm2_bias, fc2_bias),
        [struct((rows, model), BF16), struct((8, model), F32)],
    )
    first_a = links.a(first_own)
    first_b = links.b(first_own)
    half = rows // 2
    low_d = links.b(first_a[:half])
    high_d = links.a(first_b[half:])
    first_acts = (first_own, first_a, first_b, low_d, high_d)

    vec_own, bias_t = simple(
        pack_kernel,
        info,
        (fc1_bias, ffn_gain, ffn_bias, inner_gain, inner_bias, qv_bias),
        [struct((8, hidden_share), F32), struct((3 * dim, 1), F32)],
    )
    vecs = (vec_own, links.a(vec_own), links.b(vec_own), links.d(vec_own))

    w0 = gather_weight(links, out_weight, 1)
    w1 = gather_weight(links, fc1_weight, 1)
    w2 = gather_weight(links, fc2_weight, 0)

    qkv_t = jnp.swapaxes(qkv_weight, 1, 2).reshape(3 * dim, model)
    qkv = []
    for act in first_acts:
        qkv.append((dot(qkv_t, act, (1, 1)) + bias_t).astype(BF16))
    mixed, lse = attend(info, qkv, heads)

    mixes = (mixed[0], links.a(mixed[1]), links.b(mixed[2]), links.d(mixed[3]))
    resid_mid, second_act, second_t, hat_in, inv_in, act_in, wo, cols = mid_block(
        info, mixes, vecs, w0, own_rows, params
    )
    cot, cot_t = cot_block(info, cotangent.reshape(-1, model), rows)
    hidden0, slope0, vecs0, *sums = expand_block(info, False, vecs, w1, second_act, ())
    hidden1, slope1, vecs1, mean, inv = expand_block(info, True, vecs, w1, second_act, sums)
    ffn, grad0, fc2_own, fc2_near, sums_c0, *sums = contract_block(
        info, False, hidden0, vecs0, w2, cot, cot_t, mean, inv, ()
    )
    output, grad1, fc2_far, fc2_rest, sums_c1, hat_sum, hat_dot = contract_block(
        info, True, hidden1, vecs1, w2, cot, cot_t, mean, inv, (ffn, *sums, resid_mid, params)
    )
    columns = (mean, inv, hat_sum, hat_dot)
    total, fc1_far, fc1_rest, sums_b1 = back_block(
        info, True, hidden1, slope1, grad1, vecs1, w1, second_t, columns, ()
    )
    total, fc1_own, fc1_near, sums_b0 = back_block(
        info, False, hidden0, slope0, grad0, vecs0, w1, second_t, columns, (total,)
    )
    out_own, out_near, out_far, out_rest, grad_mid, ga_own, ga_a, ga_b, ga_d = tail_block(
        info, total, resid_mid, cot, params, hat_in, inv_in, act_in, wo, cols,
        (sums_c0, sums_c1, sums_b0, sums_b1), dim
    )

    fc2_grad = scatter_all(links, *over_head(links, fc2_own, fc2_near, fc2_far, fc2_rest, 0))
    fc1_grad = scatter_all(links, *over_head(links, fc1_own, fc1_near, fc1_far, fc1_rest, 0))
    group0 = over_head(links, out_own, out_near, out_far, out_rest, EXTRA)

    grads = (ga_own, links.a(ga_a), links.b(ga_b), links.d(ga_d))
    grad_qkv = attend_back(info, qkv, mixed, grads, lse, heads)

    low_d = links.b(dot(grad_qkv[3], qkv_t, (0, 0)).astype(BF16))
    high_d = links.a(dot(grad_qkv[4], qkv_t, (0, 0)).astype(BF16))
    part_a = dot(grad_qkv[1], qkv_t, (0, 0))
    part_b = dot(grad_qkv[2], qkv_t, (0, 0))
    mine = dot(grad_qkv[0], qkv_t, (0, 0))
    part_a, part_b = simple(partial_kernel, info, (part_a, part_b, low_d, high_d), [struct((rows, model), BF16)] * 2)
    got_a = links.a(part_a)
    got_b = links.b(part_b)
    (input_grad,) = simple(
        final_kernel, info, (own_rows, params, grad_mid, mine, got_a, got_b), [struct((rows, model), BF16)]
    )

    share = model // links.parts
    size = block_rows(share)
    per = share // size
    spare = -(-EXTRA // size)
    lanes = -(-3 * dim // 128) * 128 + 256
    shape = (1, links.parts // 2 * per + spare, size, lanes)
    keep, send = run(
        functools.partial(weight_kernel, spare, per), info, (*first_acts, *grad_qkv, *group0),
        [struct(shape, F32), struct(shape, BF16)], [struct((links.parts * per, size, 3 * dim), F32)], 1 << 31
    )
    got = links.dp(send, 1)
    done = finish_scatter(links, keep, got, 2, spare, per)[0]
    vec_all = done[per:, :, lanes - 256 :].reshape(-1, 256)[:EXTRA]
    token_all = done[per, 0, : 3 * dim]
    done = done[:per].reshape(share, lanes)
    qkv_grad = done[:, : 3 * dim]
    out_grad = jnp.stack((done[:, lanes - 256 : lanes - 128], done[:, lanes - 128 :]))
    vec_all = jnp.stack((vec_all[:, :128], vec_all[:, 128:]))

    my_weight = lax.dynamic_slice_in_dim(qkv_t, part * share, share, 1).astype(F32)
    norm1_part = jnp.stack(
        (jnp.sum(my_weight * token_all[:, None], axis=0), jnp.sum(my_weight * qkv_grad.T, axis=0))
    )
    norm1_sum = norm1_part + links.a(norm1_part) + links.b(norm1_part) + links.d(norm1_part)
    my_gain = lax.dynamic_slice_in_dim(norm1_gain, part * share, share, 0)
    my_bias = lax.dynamic_slice_in_dim(norm1_bias, part * share, share, 0)
    grad_norm1_bias = norm1_sum[0]
    grad_norm1_gain = (norm1_sum[1] - my_bias * norm1_sum[0]) / my_gain

    def in_order(value):
        return jnp.where(core == 0, value, value[::-1])

    fc2_grad = jnp.swapaxes(in_order(fc2_grad), 1, 2).reshape(hidden_share, share)
    fc1_grad = jnp.swapaxes(in_order(fc1_grad), 0, 1).reshape(share, hidden_share)
    out_grad = in_order(out_grad)[:, :, : dim // 2]
    out_grad = jnp.swapaxes(out_grad, 1, 2).reshape(dim, share)
    vec_all = in_order(vec_all)
    wide = vec_all[:, :21].reshape(2, 7, units)
    wide = jnp.swapaxes(wide, 0, 1).reshape(7, model)
    slim = jnp.swapaxes(vec_all[:, 21:23, : dim // 2], 0, 1).reshape(2, dim)
    mine = lax.dynamic_slice_in_dim(wide, part * share, share, 1)
    thin = lax.dynamic_slice_in_dim(slim, part * (dim // links.parts), dim // links.parts, 1)
    qv_all = token_all.reshape(3, dim)
    qv_grad = lax.dynamic_slice_in_dim(
        jnp.stack((qv_all[0], qv_all[2])), part * (dim // links.parts), dim // links.parts, 1
    )

    return (
        output.reshape(rows, 1, model),
        input_grad.reshape(rows, 1, model),
        jnp.swapaxes(qkv_grad.reshape(share, 3, dim), 0, 1),
        out_grad,
        fc1_grad,
        fc2_grad,
        qv_grad,
        thin[0],
        thin[1],
        mine[0],
        mine[1],
        mine[2],
        grad_norm1_gain,
        grad_norm1_bias,
        mine[3],
        mine[4],
        mine[5],
        mine[6],
    )


def solution(mesh):
    in_specs = (
        P(HEAD, DP, None),
        P(DP),
        P(),
        P(),
        P(None, None, HEAD),
        P(None, HEAD),
        P(HEAD),
        P(HEAD),
        P(HEAD, None),
        P(),
        P(),
        P(),
        P(None, HEAD),
        P(HEAD),
        P(HEAD),
        P(HEAD),
        P(HEAD, None),
        P(),
        P(None, DP, None),
    )
    out_specs = (
        P(HEAD, DP, None),
        P(HEAD, DP, None),
        P(None, DP, HEAD),
        P(HEAD, DP),
        P(DP, HEAD),
        P(HEAD, DP),
        P(None, (HEAD, DP)),
        P((HEAD, DP)),
        P((HEAD, DP)),
        P((HEAD, DP)),
        P((HEAD, DP)),
        P((HEAD, DP)),
        P(DP),
        P(DP),
        P(DP),
        P(DP),
        P(DP),
        P(DP),
    )

    return jax.shard_map(layer, mesh=mesh, in_specs=in_specs, out_specs=out_specs, check_vma=False)
```

```python
import functools

import jax
import jax.numpy as jnp
from jax import lax
from jax.experimental import pallas as pl
from jax.experimental.pallas import tpu as pltpu
from jax.sharding import PartitionSpec as P


HEAD = "head"
DP = "dp"
HEAD_DIM = 64
EPS = 1e-05
NEG = -1e30
F32 = jnp.float32
BF16 = jnp.bfloat16
SQRT_HALF = 0.7071067811865476
INV_SQRT_2PI = 0.3989422804014327


def dot(left, right, contract):
    return lax.dot_general(left, right, ((contract[0:1], contract[1:2]), ((), ())), preferred_element_type=F32)


def diag_mask(scores, start=0):
    key_pos = lax.broadcasted_iota(jnp.int32, scores.shape, 0)
    row_pos = lax.broadcasted_iota(jnp.int32, scores.shape, 1)
    return key_pos <= row_pos + start


def halves(rows):
    half = rows // 2
    return ((slice(0, half), slice(0, half)), (slice(0, rows), slice(half, rows)))


def spans(qkv):
    rows = qkv[0].shape[1]
    half = rows // 2
    result = [(slot, slice(0, rows), qkv[slot]) for slot in range(3)]
    return result + [(3, slice(0, half), qkv[3]), (3, slice(half, rows), qkv[4])]


def attend_kernel(heads, info, *refs):
    slots = 4
    qkv = refs[0:5]
    outs = refs[5:9]
    lse_ref = refs[9]
    q_s, k_s, v_s, o_s = refs[10:14]
    width = heads * HEAD_DIM
    scale = HEAD_DIM ** (-0.5)
    for slot, span, array in spans(qkv):
        block = info[slot]
        q_s[block, :, span] = array[0:width, :] * jnp.asarray(scale, BF16)
        v_s[block, :, span] = array[2 * width : 3 * width, :]
        for head in range(heads):
            low = width + head * HEAD_DIM
            k_s[block, head, span, :] = turn(array[low : low + HEAD_DIM, :])
    is_long = info[4]

    def step(row, key, carry, first):
        result = []
        for head in range(heads):
            part = pl.ds(head * HEAD_DIM, HEAD_DIM)
            scores = dot(k_s[key, head], q_s[row, part, :], (1, 0))
            if first:
                scores = jnp.where(diag_mask(scores), scores, NEG)
                peak = jnp.max(scores, axis=0, keepdims=True)
                weights = jnp.exp(scores - peak)
                total = jnp.sum(weights, axis=0, keepdims=True)
                mixed = dot(v_s[key, part, :], weights.astype(BF16), (1, 0))
            else:
                old_peak, old_total, old_mixed = carry[head]
                peak = jnp.maximum(old_peak, jnp.max(scores, axis=0, keepdims=True))
                fade = jnp.exp(old_peak - peak)
                weights = jnp.exp(scores - peak)
                total = old_total * fade + jnp.sum(weights, axis=0, keepdims=True)
                mixed = old_mixed * fade + dot(v_s[key, part, :], weights.astype(BF16), (1, 0))
            result.append((peak, total, mixed))
        return tuple(result)

    def row_block(row, unused):
        carry = step(row, row, None, True)
        low = jnp.where(is_long > 0, 0, row)
        carry = lax.fori_loop(low, row, lambda key, c: step(row, key, c, False), carry)
        for head in range(heads):
            peak, total, mixed = carry[head]
            o_s[row, pl.ds(head * HEAD_DIM, HEAD_DIM), :] = (mixed / total).astype(BF16)
            lse_ref[row, pl.ds(head, 1), :] = peak + jnp.log(total)
        return unused

    lax.fori_loop(0, slots, row_block, 0)
    for slot in range(slots):
        outs[slot][...] = o_s[info[slot]]


def back_step(heads, row, key, carry, first, arrays, grad_out):
    q_s, qr_s, k_s, kr_s, vr_s, g_s, gr_s, delta_s, lse_ref = arrays
    result = []
    for head in range(heads):
        part = pl.ds(head * HEAD_DIM, HEAD_DIM)
        if first:
            found = []
            for keys, rows in halves(kr_s.shape[2]):
                scores = dot(kr_s[key, head, keys, :], q_s[row, part, rows], (1, 0))
                weights = jnp.exp(scores - lse_ref[row, pl.ds(head, 1), rows])
                weights = jnp.where(diag_mask(scores, rows.start), weights, 0.0)
                grad_weights = dot(vr_s[key, head, keys, :], g_s[row, part, rows], (1, 0))
                grad_scores = (weights * (grad_weights - delta_s[row, pl.ds(head, 1), rows])).astype(BF16)
                grad_key = dot(grad_scores, qr_s[row, head, rows, :], (1, 0))
                grad_value = dot(weights.astype(BF16), gr_s[row, head, rows, :], (1, 0))
                found.append((grad_key, grad_value, dot(k_s[key, part, keys], grad_scores, (1, 0))))
            half = found[0][0].shape[0]
            sums = [
                jnp.concatenate((found[1][index][:half] + found[0][index], found[1][index][half:]), axis=0)
                for index in range(2)
            ]
            grad_out(key, head, *sums)
            result.append(jnp.concatenate((found[0][2], found[1][2]), axis=1))
            continue
        scores = dot(kr_s[key, head], q_s[row, part, :], (1, 0))
        weights = jnp.exp(scores - lse_ref[row, pl.ds(head, 1), :])
        grad_weights = dot(vr_s[key, head], g_s[row, part, :], (1, 0))
        grad_scores = (weights * (grad_weights - delta_s[row, pl.ds(head, 1), :])).astype(BF16)
        grad_out(key, head, dot(grad_scores, qr_s[row, head], (1, 0)), dot(weights.astype(BF16), gr_s[row, head], (1, 0)))
        grad_query = dot(k_s[key, part, :], grad_scores, (1, 0))
        result.append(carry[head] + grad_query)
    return tuple(result)


def early_kernel(heads, info, *refs):
    qkv = refs[0:5]
    mixed = refs[5:9]
    grads = refs[9:13]
    lse_ref = refs[13]
    q_s, qr_s, k_s, kr_s, vr_s, g_s, gr_s, delta_s, dq_s, dk_s, dv_s = refs[14:25]
    width = heads * HEAD_DIM
    scale = HEAD_DIM ** (-0.5)
    for slot, span, array in spans(qkv):
        block = info[slot]
        scaled = array[0:width, :] * jnp.asarray(scale, BF16)
        q_s[block, :, span] = scaled
        k_s[block, :, span] = array[width : 2 * width, :]
        for head in range(heads):
            low = head * HEAD_DIM
            high = low + HEAD_DIM
            qr_s[block, head, span, :] = turn(scaled[low:high, :])
            kr_s[block, head, span, :] = turn(array[width + low : width + high, :])
            vr_s[block, head, span, :] = turn(array[2 * width + low : 2 * width + high, :])
    for slot in range(4):
        block = info[slot]
        g_s[block] = grads[slot][...]
        for head in range(heads):
            low = head * HEAD_DIM
            high = low + HEAD_DIM
            gr_s[block, head] = turn(grads[slot][low:high, :])
            product = grads[slot][low:high, :].astype(F32) * mixed[slot][low:high, :].astype(F32)
            delta_s[block, pl.ds(head, 1), :] = jnp.sum(product, axis=0, keepdims=True)
    is_long = info[4]
    arrays = (q_s, qr_s, k_s, kr_s, vr_s, g_s, gr_s, delta_s, lse_ref)

    def write(key, head, grad_key, grad_value):
        dk_s[key, head] = grad_key
        dv_s[key, head] = grad_value

    def add(key, head, grad_key, grad_value):
        dk_s[key, head] += grad_key
        dv_s[key, head] += grad_value

    def row_block(row, unused):
        carry = back_step(heads, row, row, None, True, arrays, write)
        low = jnp.where(is_long > 0, 0, row)
        carry = lax.fori_loop(
            low, row, lambda key, c: back_step(heads, row, key, c, False, arrays, add), carry
        )
        for head in range(heads):
            dq_s[row, pl.ds(head * HEAD_DIM, HEAD_DIM), :] = (carry[head] * scale).astype(BF16)
        return unused

    lax.fori_loop(0, 3, row_block, 0)


def late_kernel(heads, info, *refs):
    arrays = refs[0:8] + (refs[11],)
    dq_in, dk_in, dv_in = refs[8:11]
    outs = refs[12:17]
    dq_s, dk_s, dv_s = refs[17:20]
    width = heads * HEAD_DIM
    scale = HEAD_DIM ** (-0.5)
    is_long = info[4]
    last = 3
    dq_s[0:last] = dq_in[0:last]

    def write(key, head, grad_key, grad_value):
        dk_s[key, head] = grad_key
        dv_s[key, head] = grad_value

    def add(key, head, grad_key, grad_value):
        dk_s[key, head] = dk_in[key, head] + grad_key
        dv_s[key, head] = dv_in[key, head] + grad_value

    carry = back_step(heads, last, last, None, True, arrays, write)
    low = jnp.where(is_long > 0, 0, last)
    carry = lax.fori_loop(low, last, lambda key, c: back_step(heads, last, key, c, False, arrays, add), carry)
    for head in range(heads):
        dq_s[last, pl.ds(head * HEAD_DIM, HEAD_DIM), :] = (carry[head] * scale).astype(BF16)

    @pl.when(is_long == 0)
    def _():
        dk_s[0:last] = dk_in[0:last]
        dv_s[0:last] = dv_in[0:last]

    for slot, span, array in spans(outs):
        block = info[slot]
        array[0:width, :] = dq_s[block, :, span]
        for head in range(heads):
            low = width + head * HEAD_DIM
            array[low : low + HEAD_DIM, :] = dk_s[block, head, span, :].T.astype(BF16)
            low = low + width
            array[low : low + HEAD_DIM, :] = dv_s[block, head, span, :].T.astype(BF16)


def turn(value):
    return value.astype(F32).T.astype(BF16)


def vmem_specs(count):
    return [pl.BlockSpec(memory_space=pltpu.VMEM)] * count


def footprint(array):
    shape = (1,) * (2 - len(array.shape)) + tuple(array.shape)
    size = jnp.dtype(array.dtype).itemsize
    rows = -(-shape[-2] // 8) * 8 if shape[-2] > 1 else 1
    lanes = -(-shape[-1] // 128) * 128
    total = rows * lanes * size
    for extent in shape[:-2]:
        total *= extent
    return total


def limit(arrays):
    total = sum(footprint(array) for array in arrays) + SPARE
    return pltpu.CompilerParams(vmem_limit_bytes=total)


SPARE = 6 * 1024 * 1024


def attend(info, qkv, heads):
    rows = qkv[0].shape[1]
    width = heads * HEAD_DIM
    flat = struct((4, width, rows), BF16)
    scratch = [flat, struct((4, heads, rows, HEAD_DIM), BF16), flat, flat]
    outs = [struct((width, rows), BF16)] * 4 + [struct((4, heads, rows), F32)]
    flops = 40 * heads * HEAD_DIM * rows * rows
    result = run(functools.partial(attend_kernel, heads), info, qkv, outs, scratch, flops)
    return result[:4], result[4]


def attend_back(info, qkv, mixed, grads, lse, heads):
    rows = qkv[0].shape[1]
    width = heads * HEAD_DIM
    flat = struct((4, width, rows), BF16)
    turned = struct((4, heads, rows, HEAD_DIM), BF16)
    total = struct((4, heads, rows, HEAD_DIM), F32)
    outs = [flat, turned, flat, turned, turned, flat, turned, struct((4, heads, rows), F32), flat, total, total]
    flops = 50 * heads * HEAD_DIM * rows * rows
    kernel = functools.partial(early_kernel, heads)
    kept = run(kernel, info, (*qkv, *mixed, *grads, lse), outs, [], flops)
    outs = [struct((3 * width, rows), BF16)] * 3 + [struct((3 * width, rows // 2), BF16)] * 2
    kernel = functools.partial(late_kernel, heads)
    return run(kernel, info, (*kept, lse), outs, [flat, total, total], flops)


ROWS = 128
UNROLL = 4


def fold(value):
    total = value[:, 0:128]
    for place in range(128, value.shape[1], 128):
        total = total + value[:, place : place + 128]
    return total


def row_sum(value):
    return jnp.sum(value, axis=1, keepdims=True)


def col_sum(value):
    return jnp.sum(value, axis=0, keepdims=True)


def each(rows, body, carry=0, unroll=UNROLL):
    def step(index, state):
        for place in range(unroll):
            state = body(pl.ds(pl.multiple_of((index * unroll + place) * ROWS, ROWS), ROWS), state)
        return state

    if rows == unroll * ROWS:
        for place in range(unroll):
            carry = body(pl.ds(place * ROWS, ROWS), carry)
        return carry
    return lax.fori_loop(0, rows // ROWS // unroll, step, carry)


def mid_kernel(
    info, mix_own, mix_a, mix_b, mix_d, vec_own, vec_a, vec_b, vec_d, w_own, w_near, w_far, w_b, w_other, rows_ref,
    params, resid_ref, second_ref, turned_ref, hat_ref, inv_ref, act_ref, wo_ref, cols_ref, side_s
):
    core = info[5]
    model = rows_ref.shape[1]
    mixes = (mix_own, mix_a, mix_b, mix_d)
    vecs = (vec_own, vec_a, vec_b, vec_d)
    dim = mix_own.shape[0]
    count = 4 * dim
    half = dim // 2
    split = model // 2
    total = 0.0
    for mix in mixes:
        total = total + col_sum(mix[...].astype(F32))
    mean = total / count
    square = 0.0
    for mix in mixes:
        centred = mix[...].astype(F32) - mean
        square = square + col_sum(centred * centred)
    inv = lax.rsqrt(square / count + EPS)
    inv_ref[...] = inv
    side_s[:, pl.ds(pl.multiple_of(core * split, 128), split)] = w_far[...]
    side_s[:, pl.ds(pl.multiple_of((1 - core) * split, 128), split)] = w_other[...]
    weights = (w_own, w_near, w_b, side_s)
    for slot in range(4):
        cols = vecs[slot][...].T
        for other in range(2):
            part = slice(other * half, other * half + half)
            low = (slot * 2 + other) * 128
            mine = slice(low, low + half)
            pad = slice(low + half, low + 128)
            wo_ref[mine, :] = weights[slot][part, :]
            wo_ref[pad, :] = jnp.zeros((128 - half, model), BF16)
            hat = (mixes[slot][part, :].astype(F32) - mean) * inv
            hat_ref[mine, :] = hat
            hat_ref[pad, :] = jnp.zeros((128 - half, hat.shape[1]), F32)
            cols_ref[mine, :] = cols[part, 3:5]
            cols_ref[pad, :] = jnp.zeros((128 - half, 2), F32)
            act = hat * cols[part, 3:4] + cols[part, 4:5]
            act_ref[:, mine] = turn(act)
            act_ref[:, pad] = jnp.zeros((act_ref.shape[0], 128 - half), BF16)

    def finish(part, state):
        branch = dot(act_ref[part, :], wo_ref[...], (1, 0))
        resid = rows_ref[part, :].astype(F32) + branch + params[2:3, :]
        resid_ref[part, :] = resid
        centred = resid - row_sum(resid) / model
        scale = lax.rsqrt(row_sum(centred * centred) / model + EPS)
        second = centred * scale * params[3:4, :] + params[4:5, :]
        second_ref[part, :] = second.astype(BF16)
        turned_ref[:, part] = turn(second)
        return state

    each(rows_ref.shape[0], finish)


def expand_kernel(last, info, *refs):
    if last:
        vec_b, vec_d, w_b, w_far, w_other, second, sum_in, square_in = refs[:8]
        hidden, slope, vecs, mean_ref, inv_ref, w_s = refs[8:]
    else:
        vec_own, vec_a, w_own, w_near, second = refs[:5]
        hidden, slope, vecs, sum_ref, square_ref = refs[5:]
    units = hidden.shape[2]
    split = units // 2
    core = info[5]
    if last:
        vecs[0] = vec_b[...]
        vecs[1, :, 0:split] = vec_d[:, pl.ds(pl.multiple_of(core * split, 128), split)]
        vecs[1, :, split:units] = vec_d[:, pl.ds(pl.multiple_of((1 - core) * split, 128), split)]
        w_s[:, 0:split] = w_far[...]
        w_s[:, split:units] = w_other[...]
        pairs = (w_b, w_s)
    else:
        vecs[0] = vec_own[...]
        vecs[1] = vec_a[...]
        pairs = (w_own, w_near)

    def work(part, state):
        sums = sum_in[part, :] if last else 0.0
        squares = square_in[part, :] if last else 0.0
        for pair in range(2):
            pre = dot(second[part, :], pairs[pair][...], (1, 0)) + vecs[pair, 0:1, :]
            phi = 0.5 + 0.5 * lax.erf(pre * SQRT_HALF)
            act = pre * phi
            hidden[pair, part, :] = act.astype(BF16)
            slope[pair, part, :] = (phi + pre * (INV_SQRT_2PI * jnp.exp(-0.5 * (pre * pre)))).astype(BF16)
            sums = sums + fold(act)
            squares = squares + fold(act * act)
        if last:
            mean = row_sum(sums) / (4 * units)
            mean_ref[part, :] = mean
            inv_ref[part, :] = lax.rsqrt(row_sum(squares) / (4 * units) - mean * mean + EPS)
        else:
            sum_ref[part, :] = sums
            square_ref[part, :] = squares
        return state

    each(second.shape[0], work)


def put_first(core, pair, value, own, near):
    target = own if pair == 0 else near
    split = value.shape[1] // 2
    target[core] = value[:, 0:split].astype(BF16)
    target[1 - core] = value[:, split:].astype(BF16)


def put_last(core, pair, value, far, rest):
    split = value.shape[1] // 2
    if pair == 0:
        rest[1 - core] = value[:, 0:split].astype(BF16)
        rest[core] = value[:, split:].astype(BF16)
    else:
        far[0] = value[:, 0:split].astype(BF16)
        rest[2] = value[:, split:].astype(BF16)


def contract_kernel(last, info, *refs):
    if last:
        hidden, vecs, w_b, w_far, w_other, cot, turned, mean, inv, total_in, sum_in, dot_in, resid, params = refs[:14]
        out, grad_hid, far, rest, sums, hat_sum, hat_dot, w_s, act_s = refs[14:]
    else:
        hidden, vecs, w_own, w_near, cot, turned, mean, inv = refs[:8]
        total, grad_hid, own, near, sums, sum_ref, dot_ref, act_s = refs[8:]
    units = hidden.shape[2]
    core = info[5]
    if last:
        w_s[0 : units // 2, :] = w_far[...]
        w_s[units // 2 : units, :] = w_other[...]
        pairs = (w_b, w_s)
    else:
        pairs = (w_own, w_near)

    def work(part, state):
        by_gain, by_bias = [list(value) for value in state]
        shift = mean[part, :]
        scale = inv[part, :]
        hat_sums = sum_in[part, :] if last else 0.0
        hat_dots = dot_in[part, :] if last else 0.0
        ffn = total_in[part, :] if last else 0.0
        for pair in range(2):
            gain = vecs[pair, 1:2, :]
            grad = dot(cot[part, :], pairs[pair][...], (1, 1))
            grad_hid[pair, part, :] = grad.astype(BF16)
            hat = (hidden[pair, part, :].astype(F32) - shift) * scale
            act = (hat * gain + vecs[pair, 2:3, :]).astype(BF16)
            act_s[pair, part, :] = act
            product = grad * hat
            hat_sums = hat_sums + fold(grad * gain)
            hat_dots = hat_dots + fold(product * gain)
            by_gain[pair] = by_gain[pair] + col_sum(product)
            by_bias[pair] = by_bias[pair] + col_sum(grad)
            ffn = ffn + dot(act, pairs[pair][...], (1, 0))
        if last:
            out[part, :] = (resid[part, :] + ffn + params[5:6, :]).astype(BF16)
            hat_sum[part, :] = row_sum(hat_sums) / (4 * units)
            hat_dot[part, :] = row_sum(hat_dots) / (4 * units)
        else:
            total[part, :] = ffn
            sum_ref[part, :] = hat_sums
            dot_ref[part, :] = hat_dots
        return tuple(by_gain), tuple(by_bias)

    zero = jnp.zeros((1, units), F32)
    by_gain, by_bias = each(cot.shape[0], work, ((zero, zero), (zero, zero)))
    for pair in range(2):
        sums[pair, 0:1, :] = by_gain[pair]
        sums[pair, 1:2, :] = by_bias[pair]
        value = dot(turned[...], act_s[pair], (1, 0))
        if last:
            put_last(core, pair, value, far, rest)
        else:
            put_first(core, pair, value, own, near)


def back_kernel(last, info, *refs):
    if last:
        hidden, slope, grad_hid, vecs, w_b, w_far, w_other, turned, mean, inv, hat_sum, hat_dot = refs[:12]
        total, far, rest, sums, w_s, pre_s = refs[12:]
    else:
        hidden, slope, grad_hid, vecs, w_own, w_near, turned, mean, inv, hat_sum, hat_dot, total_in = refs[:12]
        total, own, near, sums, pre_s = refs[12:]
    units = hidden.shape[2]
    core = info[5]
    if last:
        w_s[:, 0 : units // 2] = w_far[...]
        w_s[:, units // 2 : units] = w_other[...]
        pairs = (w_b, w_s)
    else:
        pairs = (w_own, w_near)

    def work(part, state):
        by_bias = list(state)
        shift = mean[part, :]
        scale = inv[part, :]
        second = 0.0 if last else total_in[part, :]
        for pair in range(2):
            hat = (hidden[pair, part, :].astype(F32) - shift) * scale
            grad = grad_hid[pair, part, :].astype(F32) * vecs[pair, 1:2, :] - hat_sum[part, :] - hat * hat_dot[part, :]
            pre = (scale * grad * slope[pair, part, :].astype(F32)).astype(BF16)
            pre_s[pair, part, :] = pre
            by_bias[pair] = by_bias[pair] + col_sum(pre.astype(F32))
            second = second + dot(pre, pairs[pair][...], (1, 1))
        total[part, :] = second
        return tuple(by_bias)

    zero = jnp.zeros((1, units), F32)
    by_bias = each(hidden.shape[1], work, (zero, zero))
    for pair in range(2):
        sums[pair, 0:1, :] = by_bias[pair]
        value = dot(turned[...], pre_s[pair], (1, 0))
        if last:
            put_last(core, pair, value, far, rest)
        else:
            put_first(core, pair, value, own, near)


def tail_kernel(
    info, total, resid, cot, params, hat_in, inv_in, act_in, wo, cols, sums_c0, sums_c1, sums_b0, sums_b1, own, near,
    far, rest, mid_ref, ga_own, ga_a, ga_b, ga_d, turned_s, gi_s, og_s, low_s, wide_s, slim_s
):
    rows, model = cot.shape
    core = info[5]

    def second_norm(part, state):
        to_gain, to_bias, to_out, to_last = state
        centred = resid[part, :]
        centred = centred - row_sum(centred) / model
        scale = lax.rsqrt(row_sum(centred * centred) / model + EPS)
        hat = centred * scale
        up = total[part, :]
        grad = up * params[3:4, :]
        back = scale * (grad - row_sum(grad) / model - hat * (row_sum(grad * hat) / model))
        wide = cot[part, :].astype(F32)
        mid = wide + back
        mid_ref[part, :] = mid
        low = mid.astype(BF16)
        low_s[part, :] = low
        turned_s[:, part] = turn(low)
        to_gain = to_gain + col_sum(up * hat)
        to_bias = to_bias + col_sum(up)
        to_out = to_out + col_sum(low.astype(F32))
        to_last = to_last + col_sum(wide)
        return to_gain, to_bias, to_out, to_last

    zero = jnp.zeros((1, model), F32)
    to_gain, to_bias, to_out, to_last = each(rows, second_norm, (zero, zero, zero, zero))
    gi_s[...] = dot(wo[...], turned_s[...], (1, 0))
    og_s[...] = dot(turned_s[...], act_in[...], (1, 0)).astype(BF16)
    features = 4 * ga_own.shape[0]
    half = ga_own.shape[0] // 2
    lane = lax.broadcasted_iota(jnp.int32, (128, 128), 1)

    def inner(part, state):
        index, first, second = state
        up = gi_s[part, :]
        hat = hat_in[part, :]
        side = jnp.where(lane == 0, row_sum(up * hat), jnp.where(lane == 1, row_sum(up), 0.0)).T
        slim_s[index] = side[0:8, :]
        grad = up * cols[part, 0:1]
        gi_s[part, :] = grad
        return index + 1, first + col_sum(grad), second + col_sum(grad * hat)

    zero = jnp.zeros((1, rows), F32)
    _, first, second = each(gi_s.shape[0], inner, (0, zero, zero))
    first = first / features
    second = second / features
    outs = (ga_own, ga_a, ga_b, ga_d)
    for tile in range(8):
        part = slice(tile * 128, tile * 128 + half)
        back = inv_in[...] * (gi_s[part, :] - first - hat_in[part, :] * second)
        low = (tile % 2) * half
        outs[tile // 2][low : low + half, :] = back.astype(BF16)
    split = sums_c0.shape[2] // 2
    whole_rows = (to_out, to_gain, to_bias, to_last)
    for pair in range(4):
        contract = (sums_c0, sums_c0, sums_c1, sums_c1)[pair]
        backward = (sums_b0, sums_b0, sums_b1, sums_b1)[pair]
        for other in range(2):
            base = other * split
            index = pair * 2 + other
            for place in range(split // 128):
                lanes = slice(base + place * 128, base + place * 128 + 128)
                wide_s[index, place : place + 1, :] = backward[pair % 2, 0:1, lanes]
                wide_s[index, 3 + place : 4 + place, :] = contract[pair % 2, 0:1, lanes]
                wide_s[index, 6 + place : 7 + place, :] = contract[pair % 2, 1:2, lanes]
                for row in range(4):
                    spot = 9 + 3 * row + place
                    if pair < 3:
                        wide_s[index, spot : spot + 1, :] = whole_rows[row][:, lanes]
                    else:
                        mine = slice(place * 128, place * 128 + 128)
                        yours = slice(split + place * 128, split + place * 128 + 128)
                        swap = core if other == 0 else 1 - core
                        value = jnp.where(swap == 0, whole_rows[row][:, mine], whole_rows[row][:, yours])
                        wide_s[index, spot : spot + 1, :] = value

    def write(target, place, tile, index, inner):
        target[place, 0:model, :] = og_s[:, tile]
        target[place, model : model + 21, :] = wide_s[index, 0:21, :].astype(BF16)
        target[place, model + 21 : model + 23, :] = inner[0:2, :].astype(BF16)
        target[place, model + 23 : model + 32, :] = jnp.zeros((9, 128), BF16)

    for other in range(2):
        swap = core if other == 0 else 1 - core
        write(own, swap, slice(other * 128, other * 128 + 128), other, slim_s[other])
        write(near, swap, slice((2 + other) * 128, (2 + other) * 128 + 128), 2 + other, slim_s[2 + other])
        write(rest, 1 - swap, slice((4 + other) * 128, (4 + other) * 128 + 128), 4 + other, slim_s[4 + other])
    write(far, 0, pl.ds(pl.multiple_of((6 + core) * 128, 128), 128), 6, slim_s[6 + core])
    write(rest, 2, pl.ds(pl.multiple_of((7 - core) * 128, 128), 128), 7, slim_s[7 - core])


def struct(shape, kind):
    return jax.ShapeDtypeStruct(shape, kind)


def run(kernel, info, operands, outs, scratch, flops):
    specs = vmem_specs(len(operands))
    return pl.pallas_call(
        kernel,
        out_shape=outs,
        in_specs=[pl.BlockSpec(memory_space=pltpu.SMEM)] + specs,
        out_specs=vmem_specs(len(outs)),
        scratch_shapes=[pltpu.VMEM(value.shape, value.dtype) for value in scratch],
        cost_estimate=pl.CostEstimate(flops=flops, transcendentals=0, bytes_accessed=8 << 20),
        compiler_params=limit(scratch),
    )(info, *operands)


def mid_block(info, mixes, vecs, pieces, rows, params):
    count, model = rows.shape
    dim = mixes[0].shape[0]
    operands = (*mixes, *vecs, *pieces, rows, params)
    wide = 8 * 128
    outs = [
        struct((count, model), F32),
        struct((count, model), BF16),
        struct((model, count), BF16),
        struct((wide, count), F32),
        struct((1, count), F32),
        struct((count, wide), BF16),
        struct((wide, model), BF16),
        struct((wide, 2), F32),
    ]
    scratch = [struct((dim, model), BF16)]
    return run(mid_kernel, info, operands, outs, scratch, 2 * count * model * wide)


def expand_block(info, last, vecs, pieces, second, sums):
    count, model = second.shape
    own, near, far, w_b, other = pieces
    units = near.shape[1]
    column = struct((count, 1), F32)
    partial = struct((count, 128), F32)
    outs = [struct((2, count, units), BF16)] * 2 + [struct((2, 8, units), F32)]
    flops = 8 * count * model * units
    kernel = functools.partial(expand_kernel, last)
    if last:
        operands = (*vecs[2:], w_b, far, other, second, *sums)
        scratch = [struct((model, units), BF16)]
        return run(kernel, info, operands, outs + [column] * 2, scratch, flops)
    operands = (*vecs[:2], own, near, second)
    return run(kernel, info, operands, outs + [partial] * 2, [], flops)


def grad_outs(last, model, split):
    if last:
        return [struct((1, model, split), BF16), struct((3, model, split), BF16)]
    return [struct((2, model, split), BF16)] * 2


def contract_block(info, last, hidden, vecs, pieces, cot, turned, mean, inv, more):
    count, model = cot.shape
    units = hidden.shape[2]
    own, near, far, w_b, other = pieces
    column = struct((count, 1), F32)
    partial = struct((count, 128), F32)
    act = struct((2, count, units), BF16)
    grads = grad_outs(last, model, units // 2)
    shared = [struct((2, count, units), BF16)] + grads + [struct((2, 8, units), F32)]
    flops = 12 * count * model * units
    kernel = functools.partial(contract_kernel, last)
    if last:
        operands = (hidden, vecs, w_b, far, other, cot, turned, mean, inv, *more)
        outs = [struct((count, model), BF16)] + shared + [column] * 2
        scratch = [struct((units, model), BF16), act]
        return run(kernel, info, operands, outs, scratch, flops)
    operands = (hidden, vecs, own, near, cot, turned, mean, inv)
    outs = [struct((count, model), F32)] + shared + [partial] * 2
    return run(kernel, info, operands, outs, [act], flops)


def back_block(info, last, hidden, slope, grad_hid, vecs, pieces, turned, columns, more):
    count, units = hidden.shape[1:]
    model = turned.shape[0]
    own, near, far, w_b, other = pieces
    pre = struct((2, count, units), BF16)
    outs = [struct((count, model), F32)] + grad_outs(last, model, units // 2) + [struct((2, 8, units), F32)]
    flops = 8 * count * model * units
    kernel = functools.partial(back_kernel, last)
    if last:
        operands = (hidden, slope, grad_hid, vecs, w_b, far, other, turned, *columns)
        scratch = [struct((model, units), BF16), pre]
        return run(kernel, info, operands, outs, scratch, flops)
    operands = (hidden, slope, grad_hid, vecs, own, near, turned, *columns, *more)
    return run(kernel, info, operands, outs, [pre], flops)


EXTRA = 32


def tail_block(info, total, resid, cot, params, hat_in, inv_in, act_in, wo, cols, sums, dim):
    count, model = cot.shape
    operands = (total, resid, cot, params, hat_in, inv_in, act_in, wo, cols, *sums)
    outs = [struct((places, model + EXTRA, 128), BF16) for places in (2, 2, 1, 3)]
    outs += [struct((count, model), F32)] + [struct((dim, count), BF16)] * 4
    scratch = [
        struct((model, count), BF16),
        struct((8 * 128, count), F32),
        struct((model, 8 * 128), BF16),
        struct((count, model), BF16),
        struct((8, 24, 128), F32),
        struct((8, 8, 128), F32),
    ]
    return run(tail_kernel, info, operands, outs, scratch, 4 * count * model * 1024)


class Links:
    def __init__(self):
        self.ranks = lax.axis_size(HEAD)
        self.parts = lax.axis_size(DP)
        self.core = lax.rem(lax.axis_index(DP), 2)

    def over(self, value, near, far):
        pairs = []
        for rank in range(self.ranks):
            for part in range(self.parts):
                flip = near if part % 2 == 0 else far
                pairs.append((rank * self.parts + part, (rank ^ flip) * self.parts + part))
        return lax.ppermute(value, (HEAD, DP), pairs)

    def a(self, value):
        return self.over(value, 1, 2)

    def b(self, value):
        return self.over(value, 2, 1)

    def d(self, value):
        return self.over(value, 3, 3)

    def dp(self, value, flip):
        return lax.ppermute(value, DP, [(part, part ^ flip) for part in range(self.parts)])


def gather_weight(links, own, axis):
    near = links.a(own)
    shape = list(own.shape)
    shape[axis] //= 2
    (half,) = simple(functools.partial(half_kernel, axis), links.info, (near,), [struct(tuple(shape), BF16)])
    far = links.b(half)
    return own, near, far, links.dp(near, 1), links.dp(far, 1)


def join_core_kernel(info, near, far, got, near_out, far_out):
    count = near.shape[0]

    def step(place, unused):
        for tile in range(count):
            total = near[tile, place].astype(F32) + got[tile, place].astype(F32)
            near_out[tile, place] = total.astype(BF16)
        total = far[0, place].astype(F32) + got[count, place].astype(F32)
        far_out[0, place] = total.astype(BF16)
        return unused

    lax.fori_loop(0, near.shape[1], step, 0)


def join_far_kernel(info, near, got, near_out):
    def step(place, unused):
        total = near[0, place].astype(F32) + got[0, place].astype(F32)
        near_out[0, place] = total.astype(BF16)
        near_out[1, place] = near[1, place]
        return unused

    lax.fori_loop(0, near.shape[1], step, 0)


def simple(kernel, info, operands, outs, scratch=()):
    return run(kernel, info, operands, outs, list(scratch), 1 << 28)


def halve_kernel(swap, extra, per, level, info, value, got, keep, send):
    tiles = value.shape[0]
    blocks = value.shape[1] - extra
    bit = info[7 + level]

    def step(place, unused):
        group = place // per
        for tile in range(tiles):
            other = tiles - 1 - tile if swap else tile
            mine = place + (group + bit) * per
            yours = place + (group + 1 - bit) * per
            keep[tile, place] = value[tile, mine].astype(F32) + got[tile, mine].astype(F32)
            total = value[tile, yours].astype(F32) + got[tile, yours].astype(F32)
            send[other, place] = total.astype(BF16)
        return unused

    lax.fori_loop(0, blocks // 2, step, 0)
    for place in range(extra):
        for tile in range(tiles):
            other = tiles - 1 - tile if swap else tile
            total = value[tile, blocks + place].astype(F32) + got[tile, blocks + place].astype(F32)
            keep[tile, blocks // 2 + place] = total
            send[other, blocks // 2 + place] = total.astype(BF16)


def weight_kernel(extra, per, info, *refs):
    acts, grads = refs[0:5], refs[5:10]
    own, got, weights, keep, send, total_s = refs[10:16]
    width = grads[0].shape[0]
    thin = (keep.shape[3] - width) // 2
    rows = keep.shape[2]
    blocks = own.shape[1] - extra
    bit = info[7]
    total = 0.0
    tokens = 0.0
    for act, grad in zip(acts, grads):
        total = total + dot(grad[...], act[...], (1, 0))
        tokens = tokens + fold(grad[...].astype(F32))
    tokens = row_sum(tokens)
    wide = weights[...].astype(F32)
    norm_rows = jnp.concatenate((col_sum(wide * tokens), col_sum(wide * total)), axis=0)
    total = total.T
    for place in range(blocks):
        total_s[place] = total[place * rows : place * rows + rows, :]
    tokens = jnp.broadcast_to(tokens, (width, 128)).T[0:1, :]
    base = keep.shape[3] - 256

    def step(place, unused):
        mine = place + (place // per + bit) * per
        yours = place + (place // per + 1 - bit) * per
        keep[0, place, :, 0:width] = total_s[mine]
        send[0, place, :, 0:width] = total_s[yours].astype(BF16)
        for tile in range(2):
            low = width + tile * thin
            swapped = width + (1 - tile) * thin
            value = own[tile, mine].astype(F32) + got[tile, mine].astype(F32)
            keep[0, place, :, low : low + thin] = value[:, 0:thin]
            value = own[tile, yours].astype(F32) + got[tile, yours].astype(F32)
            send[0, place, :, swapped : swapped + thin] = value[:, 0:thin].astype(BF16)
        return unused

    lax.fori_loop(0, blocks // 2, step, 0)
    for place in range(extra):
        spot = blocks // 2 + place
        keep[0, spot] = jnp.zeros(keep.shape[2:], F32)
        send[0, spot] = jnp.zeros(send.shape[2:], BF16)
        if place == 0:
            side = norm_rows.shape[1] // 2
            pieces = [tokens[:, : width // 2]]
            for row in range(4):
                pieces.append(norm_rows[row // 2 : row // 2 + 1, (row % 2) * side : (row % 2) * side + side])
            pieces.append(tokens[:, width // 2 :])
            for row, value in enumerate(pieces):
                keep[0, spot, row : row + 1, 0 : value.shape[1]] = value
                send[0, spot, row : row + 1, 0 : value.shape[1]] = value.astype(BF16)
        for tile in range(2):
            low = base + tile * 128
            swapped = base + (1 - tile) * 128
            value = own[tile, blocks + place].astype(F32) + got[tile, blocks + place].astype(F32)
            keep[0, spot, :, low : low + 128] = value
            send[0, spot, :, swapped : swapped + 128] = value.astype(BF16)


def cot_kernel(info, whole, rows_out, turned, sem):
    count = rows_out.shape[0]
    low = pl.multiple_of(info[6] * count, count)
    copy = pltpu.make_async_copy(whole.at[pl.ds(low, count), :], rows_out, sem)
    copy.start()
    copy.wait()

    def work(part, state):
        turned[:, part] = turn(rows_out[part, :])
        return state

    each(count, work, unroll=1)


def cot_block(info, whole, count):
    model = whole.shape[1]
    return pl.pallas_call(
        cot_kernel,
        out_shape=[struct((count, model), BF16), struct((model, count), BF16)],
        in_specs=[pl.BlockSpec(memory_space=pltpu.SMEM), pl.BlockSpec(memory_space=pl.ANY)],
        out_specs=vmem_specs(2),
        scratch_shapes=[pltpu.SemaphoreType.DMA(())],
        cost_estimate=pl.CostEstimate(flops=1 << 28, transcendentals=0, bytes_accessed=4 << 20),
        compiler_params=limit([]),
        name="ct",
    )(info, whole)


def half_kernel(axis, info, value, out):
    size = out.shape[axis]
    part = pl.ds(pl.multiple_of(info[5] * size, 128), size)
    out[...] = value[:, part] if axis else value[part, :]


def halve(links, value, got, flip, extra, per, swap):
    tiles, count, rows, units = value.shape
    shape = (tiles, (count - extra) // 2 + extra, rows, units)
    kernel = functools.partial(halve_kernel, swap, extra, per, flip.bit_length() - 1)
    return simple(kernel, links.info, (value, got), [struct(shape, F32), struct(shape, BF16)])


def block_rows(share):
    return EXTRA if share % EXTRA == 0 else share


def by_part(links, value, extra):
    tiles, rows, units = value.shape
    size = block_rows((rows - extra) // links.parts)
    spare = -rows % size
    if spare:
        value = jnp.concatenate((value, jnp.zeros((tiles, spare, units), value.dtype)), axis=1)
    return value.reshape(tiles, -1, size, units)


def over_head(links, own, near, far, rest, extra):
    own, near, far, rest = [by_part(links, value, extra) for value in (own, near, far, rest)]
    got = links.dp(rest, 1)
    near, far = simple(
        join_core_kernel, links.info, (near, far, got), [struct(near.shape, BF16), struct(far.shape, BF16)]
    )
    got = links.b(far)
    (near,) = simple(join_far_kernel, links.info, (near, got), [struct(near.shape, BF16)])
    return own, links.a(near)


def last_kernel(extra, per, level, info, value, got, other, other_got, keep, other_keep, send):
    bit = info[7 + level]
    mine = bit * per
    yours = (1 - bit) * per
    units = other.shape[3]
    base = per + extra
    for place in range(per):
        keep[0, place] = value[0, mine + place].astype(F32) + got[0, mine + place].astype(F32)
        total = value[0, yours + place].astype(F32) + got[0, yours + place].astype(F32)
        send[0, place] = total.astype(BF16)
        for tile in range(2):
            lanes = slice(tile * units, tile * units + units)
            total = other[tile, mine + place].astype(F32) + other_got[tile, mine + place].astype(F32)
            other_keep[0, place, :, lanes] = total
            total = other[tile, yours + place].astype(F32) + other_got[tile, yours + place].astype(F32)
            send[0, base + place, :, lanes] = total.astype(BF16)
    for place in range(extra):
        total = value[0, 2 * per + place].astype(F32) + got[0, 2 * per + place].astype(F32)
        keep[0, per + place] = total
        send[0, per + place] = total.astype(BF16)


def scatter_some(links, keep, got, flip, stop, extra, per, swap):
    while flip < stop:
        keep, send = halve(links, keep, got, flip, extra, per, swap and flip == 1)
        got = links.dp(send, flip)
        flip *= 2
    return keep, got


def scatter_all(links, own, got):
    per = own.shape[1] // links.parts
    keep, got = scatter_some(links, own, got, 1, links.parts, 0, per, True)
    done = keep + got.astype(F32)
    return done.reshape(done.shape[0], -1, done.shape[3])


def fetch(pairs, sems):
    copies = [pltpu.make_async_copy(source, target, sems.at[index]) for index, (source, target) in enumerate(pairs)]
    for copy in copies:
        copy.start()
    for copy in copies:
        copy.wait()


def pack_kernel(info, *refs):
    sources = refs[0:12]
    vec, column, params = refs[12:15]
    held = refs[15:27]
    fetch(list(zip(sources, held)), refs[27])
    wide = vec.shape[1]
    dim = held[9].shape[0]
    params[...] = jnp.zeros_like(params)
    for row in range(6):
        params[row : row + 1, :] = held[row][...].reshape(1, wide)
    vec[...] = jnp.zeros_like(vec)
    for row in range(3):
        vec[row : row + 1, :] = held[6 + row][...].astype(F32).reshape(1, wide)
    vec[3:4, 0:dim] = held[9][...].reshape(1, dim)
    vec[4:5, 0:dim] = held[10][...].reshape(1, dim)
    qv_bias = held[11]
    zero = jnp.zeros((6, dim), F32)
    turned = jnp.concatenate((qv_bias[...], zero), axis=0).T
    column[0:dim, :] = turned[:, 0:1]
    column[dim : 2 * dim, :] = jnp.zeros((dim, 1), F32)
    column[2 * dim : 3 * dim, :] = turned[:, 1:2]


def first_norm_kernel(info, rows_in, gain_in, bias_in, out, rows, gain, bias, sems):
    fetch([(rows_in, rows), (gain_in, gain), (bias_in, bias)], sems)
    model = rows.shape[1]
    wide_gain = gain[...].reshape(1, model)
    wide_bias = bias[...].reshape(1, model)

    def work(part, state):
        value = rows[part, :].astype(F32)
        centred = value - row_sum(value) / model
        scale = lax.rsqrt(row_sum(centred * centred) / model + EPS)
        out[part, :] = (centred * scale * wide_gain + wide_bias).astype(BF16)
        return state

    each(rows.shape[0], work, unroll=1)


def fetching(kernel, info, operands, outs):
    scratch = [pltpu.VMEM(value.shape, value.dtype) for value in operands]
    return pl.pallas_call(
        kernel,
        out_shape=outs,
        in_specs=[pl.BlockSpec(memory_space=pltpu.SMEM)] + [pl.BlockSpec(memory_space=pl.ANY)] * len(operands),
        out_specs=vmem_specs(len(outs)),
        scratch_shapes=scratch + [pltpu.SemaphoreType.DMA((len(operands),))],
        cost_estimate=pl.CostEstimate(flops=1 << 28, transcendentals=0, bytes_accessed=4 << 20),
        compiler_params=limit(operands),
    )(info, *operands)


def partial_kernel(info, part_a, part_b, low, high, out_a, out_b):
    half = low.shape[0]

    def work(part, state):
        upper = pl.ds(pl.multiple_of(part.start + half, ROWS), ROWS)
        out_a[part, :] = (part_a[part, :] + low[part, :].astype(F32)).astype(BF16)
        out_a[upper, :] = part_a[upper, :].astype(BF16)
        out_b[part, :] = part_b[part, :].astype(BF16)
        out_b[upper, :] = (part_b[upper, :] + high[part, :].astype(F32)).astype(BF16)
        return state

    each(half, work, unroll=1)


def final_kernel(info, rows, params, mid, mine, got_a, got_b, out):
    model = rows.shape[1]

    def work(part, state):
        value = rows[part, :].astype(F32)
        centred = value - row_sum(value) / model
        scale = lax.rsqrt(row_sum(centred * centred) / model + EPS)
        hat = centred * scale
        grad = mine[part, :] + got_a[part, :].astype(F32) + got_b[part, :].astype(F32)
        grad = grad * params[0:1, :]
        back = scale * (grad - row_sum(grad) / model - hat * (row_sum(grad * hat) / model))
        out[part, :] = (mid[part, :] + back).astype(BF16)
        return state

    each(rows.shape[0], work, unroll=1)


def layer(
    inputs,
    bucket,
    norm1_gain,
    norm1_bias,
    qkv_weight,
    qv_bias,
    inner_gain,
    inner_bias,
    out_weight,
    out_bias,
    norm2_gain,
    norm2_bias,
    fc1_weight,
    fc1_bias,
    ffn_gain,
    ffn_bias,
    fc2_weight,
    fc2_bias,
    cotangent,
):
    links = Links()
    core = links.core
    rows = inputs.shape[0]
    model = inputs.shape[2]
    dim = qkv_weight.shape[2]
    heads = dim // HEAD_DIM
    hidden_share = fc1_weight.shape[1]
    units = hidden_share // 2
    rank = lax.axis_index(HEAD)
    part = lax.axis_index(DP)
    bits = []
    while 2 ** len(bits) < links.parts:
        bits.append(lax.rem(part // 2 ** len(bits), 2))
    info = jnp.stack([rank, rank ^ (1 + core), rank ^ (2 - core), rank ^ 3, bucket[0], core, rank] + bits)
    info = info.astype(jnp.int32)
    links.info = info

    own_rows = inputs.reshape(rows, model)
    (first_own,) = fetching(first_norm_kernel, info, (own_rows, norm1_gain, norm1_bias), [struct((rows, model), BF16)])
    vec_own, bias_t, params = fetching(
        pack_kernel,
        info,
        (norm1_gain, norm1_bias, out_bias, norm2_gain, norm2_bias, fc2_bias)
        + (fc1_bias, ffn_gain, ffn_bias, inner_gain, inner_bias, qv_bias),
        [struct((8, hidden_share), F32), struct((3 * dim, 1), F32), struct((8, model), F32)],
    )
    first_a = links.a(first_own)
    first_b = links.b(first_own)
    half = rows // 2
    low_d = links.b(first_a[:half])
    high_d = links.a(first_b[half:])
    first_acts = (first_own, first_a, first_b, low_d, high_d)

    vecs = (vec_own, links.a(vec_own), links.b(vec_own), links.d(vec_own))

    w0 = gather_weight(links, out_weight, 1)
    w1 = gather_weight(links, fc1_weight, 1)
    w2 = gather_weight(links, fc2_weight, 0)

    qkv_t = jnp.swapaxes(qkv_weight, 1, 2).reshape(3 * dim, model)
    qkv = []
    for act in first_acts:
        qkv.append((dot(qkv_t, act, (1, 1)) + bias_t).astype(BF16))
    mixed, lse = attend(info, qkv, heads)

    mixes = (mixed[0], links.a(mixed[1]), links.b(mixed[2]), links.d(mixed[3]))
    resid_mid, second_act, second_t, hat_in, inv_in, act_in, wo, cols = mid_block(
        info, mixes, vecs, w0, own_rows, params
    )
    cot, cot_t = cot_block(info, cotangent.reshape(-1, model), rows)
    hidden0, slope0, vecs0, *sums = expand_block(info, False, vecs, w1, second_act, ())
    hidden1, slope1, vecs1, mean, inv = expand_block(info, True, vecs, w1, second_act, sums)
    ffn, grad0, fc2_own, fc2_near, sums_c0, *sums = contract_block(
        info, False, hidden0, vecs0, w2, cot, cot_t, mean, inv, ()
    )
    output, grad1, fc2_far, fc2_rest, sums_c1, hat_sum, hat_dot = contract_block(
        info, True, hidden1, vecs1, w2, cot, cot_t, mean, inv, (ffn, *sums, resid_mid, params)
    )
    columns = (mean, inv, hat_sum, hat_dot)
    total, fc1_far, fc1_rest, sums_b1 = back_block(
        info, True, hidden1, slope1, grad1, vecs1, w1, second_t, columns, ()
    )
    total, fc1_own, fc1_near, sums_b0 = back_block(
        info, False, hidden0, slope0, grad0, vecs0, w1, second_t, columns, (total,)
    )
    out_own, out_near, out_far, out_rest, grad_mid, ga_own, ga_a, ga_b, ga_d = tail_block(
        info, total, resid_mid, cot, params, hat_in, inv_in, act_in, wo, cols,
        (sums_c0, sums_c1, sums_b0, sums_b1), dim
    )

    fc2_grad = scatter_all(links, *over_head(links, fc2_own, fc2_near, fc2_far, fc2_rest, 0))
    group1 = over_head(links, fc1_own, fc1_near, fc1_far, fc1_rest, 0)
    group0 = over_head(links, out_own, out_near, out_far, out_rest, EXTRA)

    grads = (ga_own, links.a(ga_a), links.b(ga_b), links.d(ga_d))
    grad_qkv = attend_back(info, qkv, mixed, grads, lse, heads)

    low_d = links.b(dot(grad_qkv[3], qkv_t, (0, 0)).astype(BF16))
    high_d = links.a(dot(grad_qkv[4], qkv_t, (0, 0)).astype(BF16))
    part_a = dot(grad_qkv[1], qkv_t, (0, 0))
    part_b = dot(grad_qkv[2], qkv_t, (0, 0))
    mine = dot(grad_qkv[0], qkv_t, (0, 0))
    part_a, part_b = simple(partial_kernel, info, (part_a, part_b, low_d, high_d), [struct((rows, model), BF16)] * 2)
    got_a = links.a(part_a)
    got_b = links.b(part_b)
    (input_grad,) = simple(
        final_kernel, info, (own_rows, params, grad_mid, mine, got_a, got_b), [struct((rows, model), BF16)]
    )

    share = model // links.parts
    size = block_rows(share)
    per = share // size
    spare = -(-EXTRA // size)
    lanes = 4 * dim
    shape = (1, links.parts // 2 * per + spare, size, lanes)
    keep, send = run(
        functools.partial(weight_kernel, spare, per), info, (*first_acts, *grad_qkv, *group0, qkv_t),
        [struct(shape, F32), struct(shape, BF16)], [struct((links.parts * per, size, 3 * dim), F32)], 1 << 31
    )
    got = links.dp(send, 1)
    last = links.parts // 2
    value, got = scatter_some(links, keep, got, 2, last, spare, per, False)
    other, other_got = scatter_some(links, *group1, 1, last, 0, per, True)
    keep, other_keep, send = run(
        functools.partial(last_kernel, spare, per, last.bit_length() - 1),
        info,
        (value, got, other, other_got),
        [
            struct((1, per + spare, size, lanes), F32),
            struct((1, per, size, hidden_share), F32),
            struct((1, 2 * per + spare, size, lanes), BF16),
        ],
        [],
        1 << 28,
    )
    got = links.dp(send, last)
    norm1_sum = keep[0, per, 1:5, : model // 2]
    norm1_sum = norm1_sum + links.a(norm1_sum) + links.b(norm1_sum) + links.d(norm1_sum)
    norm1_sum = norm1_sum + links.dp(norm1_sum, last)
    norm1_sum = norm1_sum.reshape(2, model)
    fc1_grad = (other_keep + got[:, per + spare :, :, :hidden_share].astype(F32)).reshape(share, hidden_share)
    fc1_grad = jnp.stack((fc1_grad[:, :units], fc1_grad[:, units:]))
    done = (keep + got[:, : per + spare].astype(F32))[0]
    vec_all = done[per:, :, lanes - 256 :].reshape(-1, 256)[:EXTRA]
    vec_all = jnp.stack((vec_all[:, :128], vec_all[:, 128:]))
    side = 3 * dim // 2
    token_all = jnp.concatenate((done[per, 0, :side], done[per, 5, :side]))
    done = done[:per].reshape(share, lanes)
    qkv_grad = done[:, : 3 * dim]
    out_grad = jnp.stack((done[:, 3 * dim : 3 * dim + dim // 2], done[:, 3 * dim + dim // 2 :]))

    norm1_sum = lax.dynamic_slice_in_dim(norm1_sum, part * share, share, 1)
    my_gain = lax.dynamic_slice_in_dim(norm1_gain, part * share, share, 0)
    my_bias = lax.dynamic_slice_in_dim(norm1_bias, part * share, share, 0)
    grad_norm1_bias = norm1_sum[0]
    grad_norm1_gain = (norm1_sum[1] - my_bias * norm1_sum[0]) / my_gain

    def in_order(value):
        return jnp.where(core == 0, value, value[::-1])

    fc2_grad = jnp.swapaxes(in_order(fc2_grad), 1, 2).reshape(hidden_share, share)
    fc1_grad = jnp.swapaxes(in_order(fc1_grad), 0, 1).reshape(share, hidden_share)
    out_grad = in_order(out_grad)[:, :, : dim // 2]
    out_grad = jnp.swapaxes(out_grad, 1, 2).reshape(dim, share)
    vec_all = in_order(vec_all)
    wide = vec_all[:, :21].reshape(2, 7, units)
    wide = jnp.swapaxes(wide, 0, 1).reshape(7, model)
    slim = jnp.swapaxes(vec_all[:, 21:23, : dim // 2], 0, 1).reshape(2, dim)
    mine = lax.dynamic_slice_in_dim(wide, part * share, share, 1)
    thin = lax.dynamic_slice_in_dim(slim, part * (dim // links.parts), dim // links.parts, 1)
    qv_all = token_all.reshape(3, dim)
    qv_grad = lax.dynamic_slice_in_dim(
        jnp.stack((qv_all[0], qv_all[2])), part * (dim // links.parts), dim // links.parts, 1
    )

    return (
        output.reshape(rows, 1, model),
        input_grad.reshape(rows, 1, model),
        jnp.swapaxes(qkv_grad.reshape(share, 3, dim), 0, 1),
        out_grad,
        fc1_grad,
        fc2_grad,
        qv_grad,
        thin[0],
        thin[1],
        mine[0],
        mine[1],
        mine[2],
        grad_norm1_gain,
        grad_norm1_bias,
        mine[3],
        mine[4],
        mine[5],
        mine[6],
    )


def solution(mesh):
    in_specs = (
        P(HEAD, DP, None),
        P(DP),
        P(),
        P(),
        P(None, None, HEAD),
        P(None, HEAD),
        P(HEAD),
        P(HEAD),
        P(HEAD, None),
        P(),
        P(),
        P(),
        P(None, HEAD),
        P(HEAD),
        P(HEAD),
        P(HEAD),
        P(HEAD, None),
        P(),
        P(None, DP, None),
    )
    out_specs = (
        P(HEAD, DP, None),
        P(HEAD, DP, None),
        P(None, DP, HEAD),
        P(HEAD, DP),
        P(DP, HEAD),
        P(HEAD, DP),
        P(None, (HEAD, DP)),
        P((HEAD, DP)),
        P((HEAD, DP)),
        P((HEAD, DP)),
        P((HEAD, DP)),
        P((HEAD, DP)),
        P(DP),
        P(DP),
        P(DP),
        P(DP),
        P(DP),
        P(DP),
    )

    return jax.shard_map(layer, mesh=mesh, in_specs=in_specs, out_specs=out_specs, check_vma=False)
```

```python
import functools

import jax
import jax.numpy as jnp
from jax import lax
from jax.experimental import pallas as pl
from jax.experimental.pallas import tpu as pltpu
from jax.sharding import PartitionSpec as P


HEAD = "head"
DP = "dp"
HEAD_DIM = 64
EPS = 1e-05
NEG = -1e30
F32 = jnp.float32
BF16 = jnp.bfloat16
SQRT_HALF = 0.7071067811865476
INV_SQRT_2PI = 0.3989422804014327


def dot(left, right, contract):
    return lax.dot_general(left, right, ((contract[0:1], contract[1:2]), ((), ())), preferred_element_type=F32)


def diag_mask(scores, start=0):
    key_pos = lax.broadcasted_iota(jnp.int32, scores.shape, 0)
    row_pos = lax.broadcasted_iota(jnp.int32, scores.shape, 1)
    return key_pos <= row_pos + start


def halves(rows):
    half = rows // 2
    return ((slice(0, half), slice(0, half)), (slice(0, rows), slice(half, rows)))


def spans(qkv):
    rows = qkv[0].shape[1]
    half = rows // 2
    result = [(slot, slice(0, rows), qkv[slot]) for slot in range(3)]
    return result + [(3, slice(0, half), qkv[3]), (3, slice(half, rows), qkv[4])]


def attend_kernel(heads, info, *refs):
    slots = 4
    qkv = refs[0:5]
    outs = refs[5:9]
    lse_ref = refs[9]
    q_s, k_s, v_s, o_s = refs[10:14]
    width = heads * HEAD_DIM
    scale = HEAD_DIM ** (-0.5)
    for slot, span, array in spans(qkv):
        block = info[slot]
        q_s[block, :, span] = array[0:width, :] * jnp.asarray(scale, BF16)
        v_s[block, :, span] = array[2 * width : 3 * width, :]
        for head in range(heads):
            low = width + head * HEAD_DIM
            k_s[block, head, span, :] = turn(array[low : low + HEAD_DIM, :])
    is_long = info[4]

    def step(row, key, carry, first):
        result = []
        for head in range(heads):
            part = pl.ds(head * HEAD_DIM, HEAD_DIM)
            scores = dot(k_s[key, head], q_s[row, part, :], (1, 0))
            if first:
                scores = jnp.where(diag_mask(scores), scores, NEG)
                peak = jnp.max(scores, axis=0, keepdims=True)
                weights = jnp.exp(scores - peak)
                total = jnp.sum(weights, axis=0, keepdims=True)
                mixed = dot(v_s[key, part, :], weights.astype(BF16), (1, 0))
            else:
                old_peak, old_total, old_mixed = carry[head]
                peak = jnp.maximum(old_peak, jnp.max(scores, axis=0, keepdims=True))
                fade = jnp.exp(old_peak - peak)
                weights = jnp.exp(scores - peak)
                total = old_total * fade + jnp.sum(weights, axis=0, keepdims=True)
                mixed = old_mixed * fade + dot(v_s[key, part, :], weights.astype(BF16), (1, 0))
            result.append((peak, total, mixed))
        return tuple(result)

    def row_block(row, unused):
        carry = step(row, row, None, True)
        low = jnp.where(is_long > 0, 0, row)
        carry = lax.fori_loop(low, row, lambda key, c: step(row, key, c, False), carry)
        for head in range(heads):
            peak, total, mixed = carry[head]
            o_s[row, pl.ds(head * HEAD_DIM, HEAD_DIM), :] = (mixed / total).astype(BF16)
            lse_ref[row, pl.ds(head, 1), :] = peak + jnp.log(total)
        return unused

    lax.fori_loop(0, slots, row_block, 0)
    for slot in range(slots):
        outs[slot][...] = o_s[info[slot]]


def back_step(heads, row, key, carry, first, arrays, grad_out):
    q_s, qr_s, k_s, kr_s, vr_s, g_s, gr_s, delta_s, lse_ref = arrays
    result = []
    for head in range(heads):
        part = pl.ds(head * HEAD_DIM, HEAD_DIM)
        if first:
            found = []
            for keys, rows in halves(kr_s.shape[2]):
                scores = dot(kr_s[key, head, keys, :], q_s[row, part, rows], (1, 0))
                weights = jnp.exp(scores - lse_ref[row, pl.ds(head, 1), rows])
                weights = jnp.where(diag_mask(scores, rows.start), weights, 0.0)
                grad_weights = dot(vr_s[key, head, keys, :], g_s[row, part, rows], (1, 0))
                grad_scores = (weights * (grad_weights - delta_s[row, pl.ds(head, 1), rows])).astype(BF16)
                grad_key = dot(grad_scores, qr_s[row, head, rows, :], (1, 0))
                grad_value = dot(weights.astype(BF16), gr_s[row, head, rows, :], (1, 0))
                found.append((grad_key, grad_value, dot(k_s[key, part, keys], grad_scores, (1, 0))))
            half = found[0][0].shape[0]
            sums = [
                jnp.concatenate((found[1][index][:half] + found[0][index], found[1][index][half:]), axis=0)
                for index in range(2)
            ]
            grad_out(key, head, *sums)
            result.append(jnp.concatenate((found[0][2], found[1][2]), axis=1))
            continue
        scores = dot(kr_s[key, head], q_s[row, part, :], (1, 0))
        weights = jnp.exp(scores - lse_ref[row, pl.ds(head, 1), :])
        grad_weights = dot(vr_s[key, head], g_s[row, part, :], (1, 0))
        grad_scores = (weights * (grad_weights - delta_s[row, pl.ds(head, 1), :])).astype(BF16)
        grad_out(key, head, dot(grad_scores, qr_s[row, head], (1, 0)), dot(weights.astype(BF16), gr_s[row, head], (1, 0)))
        grad_query = dot(k_s[key, part, :], grad_scores, (1, 0))
        result.append(carry[head] + grad_query)
    return tuple(result)


def early_kernel(heads, info, *refs):
    qkv = refs[0:5]
    mixed = refs[5:9]
    grads = refs[9:13]
    lse_ref = refs[13]
    q_s, qr_s, k_s, kr_s, vr_s, g_s, gr_s, delta_s, dq_s, dk_s, dv_s = refs[14:25]
    width = heads * HEAD_DIM
    scale = HEAD_DIM ** (-0.5)
    for slot, span, array in spans(qkv):
        block = info[slot]
        scaled = array[0:width, :] * jnp.asarray(scale, BF16)
        q_s[block, :, span] = scaled
        k_s[block, :, span] = array[width : 2 * width, :]
        for head in range(heads):
            low = head * HEAD_DIM
            high = low + HEAD_DIM
            qr_s[block, head, span, :] = turn(scaled[low:high, :])
            kr_s[block, head, span, :] = turn(array[width + low : width + high, :])
            vr_s[block, head, span, :] = turn(array[2 * width + low : 2 * width + high, :])
    for slot in range(4):
        block = info[slot]
        g_s[block] = grads[slot][...]
        for head in range(heads):
            low = head * HEAD_DIM
            high = low + HEAD_DIM
            gr_s[block, head] = turn(grads[slot][low:high, :])
            product = grads[slot][low:high, :].astype(F32) * mixed[slot][low:high, :].astype(F32)
            delta_s[block, pl.ds(head, 1), :] = jnp.sum(product, axis=0, keepdims=True)
    is_long = info[4]
    arrays = (q_s, qr_s, k_s, kr_s, vr_s, g_s, gr_s, delta_s, lse_ref)

    def write(key, head, grad_key, grad_value):
        dk_s[key, head] = grad_key
        dv_s[key, head] = grad_value

    def add(key, head, grad_key, grad_value):
        dk_s[key, head] += grad_key
        dv_s[key, head] += grad_value

    def row_block(row, unused):
        carry = back_step(heads, row, row, None, True, arrays, write)
        low = jnp.where(is_long > 0, 0, row)
        carry = lax.fori_loop(
            low, row, lambda key, c: back_step(heads, row, key, c, False, arrays, add), carry
        )
        for head in range(heads):
            dq_s[row, pl.ds(head * HEAD_DIM, HEAD_DIM), :] = (carry[head] * scale).astype(BF16)
        return unused

    lax.fori_loop(0, 3, row_block, 0)


def late_kernel(heads, info, *refs):
    arrays = refs[0:8] + (refs[11],)
    dq_in, dk_in, dv_in = refs[8:11]
    outs = refs[12:17]
    dq_s, dk_s, dv_s = refs[17:20]
    width = heads * HEAD_DIM
    scale = HEAD_DIM ** (-0.5)
    is_long = info[4]
    last = 3
    dq_s[0:last] = dq_in[0:last]

    def write(key, head, grad_key, grad_value):
        dk_s[key, head] = grad_key
        dv_s[key, head] = grad_value

    def add(key, head, grad_key, grad_value):
        dk_s[key, head] = dk_in[key, head] + grad_key
        dv_s[key, head] = dv_in[key, head] + grad_value

    carry = back_step(heads, last, last, None, True, arrays, write)
    low = jnp.where(is_long > 0, 0, last)
    carry = lax.fori_loop(low, last, lambda key, c: back_step(heads, last, key, c, False, arrays, add), carry)
    for head in range(heads):
        dq_s[last, pl.ds(head * HEAD_DIM, HEAD_DIM), :] = (carry[head] * scale).astype(BF16)

    @pl.when(is_long == 0)
    def _():
        dk_s[0:last] = dk_in[0:last]
        dv_s[0:last] = dv_in[0:last]

    for slot, span, array in spans(outs):
        block = info[slot]
        array[0:width, :] = dq_s[block, :, span]
        for head in range(heads):
            low = width + head * HEAD_DIM
            array[low : low + HEAD_DIM, :] = dk_s[block, head, span, :].T.astype(BF16)
            low = low + width
            array[low : low + HEAD_DIM, :] = dv_s[block, head, span, :].T.astype(BF16)


def turn(value):
    return value.astype(F32).T.astype(BF16)


def vmem_specs(count):
    return [pl.BlockSpec(memory_space=pltpu.VMEM)] * count


def footprint(array):
    shape = (1,) * (2 - len(array.shape)) + tuple(array.shape)
    size = jnp.dtype(array.dtype).itemsize
    rows = -(-shape[-2] // 8) * 8 if shape[-2] > 1 else 1
    lanes = -(-shape[-1] // 128) * 128
    total = rows * lanes * size
    for extent in shape[:-2]:
        total *= extent
    return total


def limit(arrays):
    total = sum(footprint(array) for array in arrays) + SPARE
    return pltpu.CompilerParams(vmem_limit_bytes=total)


SPARE = 6 * 1024 * 1024


def attend(info, qkv, heads):
    rows = qkv[0].shape[1]
    width = heads * HEAD_DIM
    flat = struct((4, width, rows), BF16)
    scratch = [flat, struct((4, heads, rows, HEAD_DIM), BF16), flat, flat]
    outs = [struct((width, rows), BF16)] * 4 + [struct((4, heads, rows), F32)]
    flops = 40 * heads * HEAD_DIM * rows * rows
    result = run(functools.partial(attend_kernel, heads), info, qkv, outs, scratch, flops)
    return result[:4], result[4]


def attend_back(info, qkv, mixed, grads, lse, heads):
    rows = qkv[0].shape[1]
    width = heads * HEAD_DIM
    flat = struct((4, width, rows), BF16)
    turned = struct((4, heads, rows, HEAD_DIM), BF16)
    total = struct((4, heads, rows, HEAD_DIM), F32)
    outs = [flat, turned, flat, turned, turned, flat, turned, struct((4, heads, rows), F32), flat, total, total]
    flops = 50 * heads * HEAD_DIM * rows * rows
    kernel = functools.partial(early_kernel, heads)
    kept = run(kernel, info, (*qkv, *mixed, *grads, lse), outs, [], flops)
    outs = [struct((3 * width, rows), BF16)] * 3 + [struct((3 * width, rows // 2), BF16)] * 2
    kernel = functools.partial(late_kernel, heads)
    return run(kernel, info, (*kept, lse), outs, [flat, total, total], flops)


ROWS = 128
UNROLL = 4


def fold(value):
    total = value[:, 0:128]
    for place in range(128, value.shape[1], 128):
        total = total + value[:, place : place + 128]
    return total


def row_sum(value):
    return jnp.sum(value, axis=1, keepdims=True)


def col_sum(value):
    return jnp.sum(value, axis=0, keepdims=True)


def each(rows, body, carry=0, unroll=UNROLL):
    def step(index, state):
        for place in range(unroll):
            state = body(pl.ds(pl.multiple_of((index * unroll + place) * ROWS, ROWS), ROWS), state)
        return state

    if rows == unroll * ROWS:
        for place in range(unroll):
            carry = body(pl.ds(place * ROWS, ROWS), carry)
        return carry
    return lax.fori_loop(0, rows // ROWS // unroll, step, carry)


def mid_kernel(
    info, mix_own, mix_a, mix_b, mix_d, vec_own, vec_a, vec_b, vec_d, w_own, w_near, w_far, w_b, w_other, rows_ref,
    params, resid_ref, second_ref, turned_ref, hat_ref, inv_ref, act_ref, wo_ref, cols_ref, side_s
):
    core = info[5]
    model = rows_ref.shape[1]
    mixes = (mix_own, mix_a, mix_b, mix_d)
    vecs = (vec_own, vec_a, vec_b, vec_d)
    dim = mix_own.shape[0]
    count = 4 * dim
    half = dim // 2
    split = model // 2
    total = 0.0
    for mix in mixes:
        total = total + col_sum(mix[...].astype(F32))
    mean = total / count
    square = 0.0
    for mix in mixes:
        centred = mix[...].astype(F32) - mean
        square = square + col_sum(centred * centred)
    inv = lax.rsqrt(square / count + EPS)
    inv_ref[...] = inv
    side_s[:, pl.ds(pl.multiple_of(core * split, 128), split)] = w_far[...]
    side_s[:, pl.ds(pl.multiple_of((1 - core) * split, 128), split)] = w_other[...]
    weights = (w_own, w_near, w_b, side_s)
    for slot in range(4):
        cols = vecs[slot][...].T
        for other in range(2):
            part = slice(other * half, other * half + half)
            low = (slot * 2 + other) * 128
            mine = slice(low, low + half)
            pad = slice(low + half, low + 128)
            wo_ref[mine, :] = weights[slot][part, :]
            wo_ref[pad, :] = jnp.zeros((128 - half, model), BF16)
            hat = (mixes[slot][part, :].astype(F32) - mean) * inv
            hat_ref[mine, :] = hat
            hat_ref[pad, :] = jnp.zeros((128 - half, hat.shape[1]), F32)
            cols_ref[mine, :] = cols[part, 3:5]
            cols_ref[pad, :] = jnp.zeros((128 - half, 2), F32)
            act = hat * cols[part, 3:4] + cols[part, 4:5]
            act_ref[:, mine] = turn(act)
            act_ref[:, pad] = jnp.zeros((act_ref.shape[0], 128 - half), BF16)

    def finish(part, state):
        branch = dot(act_ref[part, :], wo_ref[...], (1, 0))
        resid = rows_ref[part, :].astype(F32) + branch + params[2:3, :]
        resid_ref[part, :] = resid
        centred = resid - row_sum(resid) / model
        scale = lax.rsqrt(row_sum(centred * centred) / model + EPS)
        second = centred * scale * params[3:4, :] + params[4:5, :]
        second_ref[part, :] = second.astype(BF16)
        turned_ref[:, part] = turn(second)
        return state

    each(rows_ref.shape[0], finish)


def expand_kernel(last, info, *refs):
    if last:
        vec_b, vec_d, w_b, w_far, w_other, second, sum_in, square_in = refs[:8]
        hidden, slope, vecs, mean_ref, inv_ref, w_s = refs[8:]
    else:
        vec_own, vec_a, w_own, w_near, second = refs[:5]
        hidden, slope, vecs, sum_ref, square_ref = refs[5:]
    units = hidden.shape[2]
    split = units // 2
    core = info[5]
    if last:
        vecs[0] = vec_b[...]
        vecs[1, :, 0:split] = vec_d[:, pl.ds(pl.multiple_of(core * split, 128), split)]
        vecs[1, :, split:units] = vec_d[:, pl.ds(pl.multiple_of((1 - core) * split, 128), split)]
        w_s[:, 0:split] = w_far[...]
        w_s[:, split:units] = w_other[...]
        pairs = (w_b, w_s)
    else:
        vecs[0] = vec_own[...]
        vecs[1] = vec_a[...]
        pairs = (w_own, w_near)

    def work(part, state):
        sums = sum_in[part, :] if last else 0.0
        squares = square_in[part, :] if last else 0.0
        for pair in range(2):
            pre = dot(second[part, :], pairs[pair][...], (1, 0)) + vecs[pair, 0:1, :]
            phi = 0.5 + 0.5 * lax.erf(pre * SQRT_HALF)
            act = pre * phi
            hidden[pair, part, :] = act.astype(BF16)
            slope[pair, part, :] = (phi + pre * (INV_SQRT_2PI * jnp.exp(-0.5 * (pre * pre)))).astype(BF16)
            sums = sums + fold(act)
            squares = squares + fold(act * act)
        if last:
            mean = row_sum(sums) / (4 * units)
            mean_ref[part, :] = mean
            inv_ref[part, :] = lax.rsqrt(row_sum(squares) / (4 * units) - mean * mean + EPS)
        else:
            sum_ref[part, :] = sums
            square_ref[part, :] = squares
        return state

    each(second.shape[0], work)


def put_first(core, pair, value, own, near):
    target = own if pair == 0 else near
    split = value.shape[1] // 2
    target[core] = value[:, 0:split].astype(BF16)
    target[1 - core] = value[:, split:].astype(BF16)


def put_last(core, pair, value, far, rest):
    split = value.shape[1] // 2
    if pair == 0:
        rest[1 - core] = value[:, 0:split].astype(BF16)
        rest[core] = value[:, split:].astype(BF16)
    else:
        far[0] = value[:, 0:split].astype(BF16)
        rest[2] = value[:, split:].astype(BF16)


def contract_kernel(last, info, *refs):
    if last:
        hidden, vecs, w_b, w_far, w_other, cot, turned, mean, inv, total_in, sum_in, dot_in, resid, params = refs[:14]
        out, grad_hid, far, rest, sums, hat_sum, hat_dot, w_s, act_s = refs[14:]
    else:
        hidden, vecs, w_own, w_near, cot, turned, mean, inv = refs[:8]
        total, grad_hid, own, near, sums, sum_ref, dot_ref, act_s = refs[8:]
    units = hidden.shape[2]
    core = info[5]
    if last:
        w_s[0 : units // 2, :] = w_far[...]
        w_s[units // 2 : units, :] = w_other[...]
        pairs = (w_b, w_s)
    else:
        pairs = (w_own, w_near)

    def work(part, state):
        by_gain, by_bias = [list(value) for value in state]
        shift = mean[part, :]
        scale = inv[part, :]
        hat_sums = sum_in[part, :] if last else 0.0
        hat_dots = dot_in[part, :] if last else 0.0
        ffn = total_in[part, :] if last else 0.0
        for pair in range(2):
            gain = vecs[pair, 1:2, :]
            grad = dot(cot[part, :], pairs[pair][...], (1, 1))
            grad_hid[pair, part, :] = grad.astype(BF16)
            hat = (hidden[pair, part, :].astype(F32) - shift) * scale
            act = (hat * gain + vecs[pair, 2:3, :]).astype(BF16)
            act_s[pair, part, :] = act
            product = grad * hat
            hat_sums = hat_sums + fold(grad * gain)
            hat_dots = hat_dots + fold(product * gain)
            by_gain[pair] = by_gain[pair] + col_sum(product)
            by_bias[pair] = by_bias[pair] + col_sum(grad)
            ffn = ffn + dot(act, pairs[pair][...], (1, 0))
        if last:
            out[part, :] = (resid[part, :] + ffn + params[5:6, :]).astype(BF16)
            hat_sum[part, :] = row_sum(hat_sums) / (4 * units)
            hat_dot[part, :] = row_sum(hat_dots) / (4 * units)
        else:
            total[part, :] = ffn
            sum_ref[part, :] = hat_sums
            dot_ref[part, :] = hat_dots
        return tuple(by_gain), tuple(by_bias)

    zero = jnp.zeros((1, units), F32)
    by_gain, by_bias = each(cot.shape[0], work, ((zero, zero), (zero, zero)), unroll=1)
    for pair in range(2):
        sums[pair, 0:1, :] = by_gain[pair]
        sums[pair, 1:2, :] = by_bias[pair]
        value = dot(turned[...], act_s[pair], (1, 0))
        if last:
            put_last(core, pair, value, far, rest)
        else:
            put_first(core, pair, value, own, near)


def back_kernel(last, info, *refs):
    if last:
        hidden, slope, grad_hid, vecs, w_b, w_far, w_other, turned, mean, inv, hat_sum, hat_dot = refs[:12]
        total, far, rest, sums, w_s, pre_s = refs[12:]
    else:
        hidden, slope, grad_hid, vecs, w_own, w_near, turned, mean, inv, hat_sum, hat_dot, total_in = refs[:12]
        total, own, near, sums, pre_s = refs[12:]
    units = hidden.shape[2]
    core = info[5]
    if last:
        w_s[:, 0 : units // 2] = w_far[...]
        w_s[:, units // 2 : units] = w_other[...]
        pairs = (w_b, w_s)
    else:
        pairs = (w_own, w_near)

    def work(part, state):
        by_bias = list(state)
        shift = mean[part, :]
        scale = inv[part, :]
        second = 0.0 if last else total_in[part, :]
        for pair in range(2):
            hat = (hidden[pair, part, :].astype(F32) - shift) * scale
            grad = grad_hid[pair, part, :].astype(F32) * vecs[pair, 1:2, :] - hat_sum[part, :] - hat * hat_dot[part, :]
            pre = (scale * grad * slope[pair, part, :].astype(F32)).astype(BF16)
            pre_s[pair, part, :] = pre
            by_bias[pair] = by_bias[pair] + col_sum(pre.astype(F32))
            second = second + dot(pre, pairs[pair][...], (1, 1))
        total[part, :] = second
        return tuple(by_bias)

    zero = jnp.zeros((1, units), F32)
    by_bias = each(hidden.shape[1], work, (zero, zero), unroll=2)
    for pair in range(2):
        sums[pair, 0:1, :] = by_bias[pair]
        value = dot(turned[...], pre_s[pair], (1, 0))
        if last:
            put_last(core, pair, value, far, rest)
        else:
            put_first(core, pair, value, own, near)


def tail_kernel(
    info, total, resid, cot, params, hat_in, inv_in, act_in, wo, cols, sums_c0, sums_c1, sums_b0, sums_b1, own, near,
    far, rest, mid_ref, ga_own, ga_a, ga_b, ga_d, turned_s, gi_s, og_s, low_s, wide_s, slim_s
):
    rows, model = cot.shape
    core = info[5]

    def second_norm(part, state):
        to_gain, to_bias, to_out, to_last = state
        centred = resid[part, :]
        centred = centred - row_sum(centred) / model
        scale = lax.rsqrt(row_sum(centred * centred) / model + EPS)
        hat = centred * scale
        up = total[part, :]
        grad = up * params[3:4, :]
        back = scale * (grad - row_sum(grad) / model - hat * (row_sum(grad * hat) / model))
        wide = cot[part, :].astype(F32)
        mid = wide + back
        mid_ref[part, :] = mid
        low = mid.astype(BF16)
        low_s[part, :] = low
        turned_s[:, part] = turn(low)
        to_gain = to_gain + col_sum(up * hat)
        to_bias = to_bias + col_sum(up)
        to_out = to_out + col_sum(low.astype(F32))
        to_last = to_last + col_sum(wide)
        return to_gain, to_bias, to_out, to_last

    zero = jnp.zeros((1, model), F32)
    to_gain, to_bias, to_out, to_last = each(rows, second_norm, (zero, zero, zero, zero))
    gi_s[...] = dot(wo[...], turned_s[...], (1, 0))
    og_s[...] = dot(turned_s[...], act_in[...], (1, 0)).astype(BF16)
    features = 4 * ga_own.shape[0]
    half = ga_own.shape[0] // 2
    lane = lax.broadcasted_iota(jnp.int32, (128, 128), 1)

    def inner(part, state):
        index, first, second = state
        up = gi_s[part, :]
        hat = hat_in[part, :]
        side = jnp.where(lane == 0, row_sum(up * hat), jnp.where(lane == 1, row_sum(up), 0.0)).T
        slim_s[index] = side[0:8, :]
        grad = up * cols[part, 0:1]
        gi_s[part, :] = grad
        return index + 1, first + col_sum(grad), second + col_sum(grad * hat)

    zero = jnp.zeros((1, rows), F32)
    _, first, second = each(gi_s.shape[0], inner, (0, zero, zero), unroll=1)
    first = first / features
    second = second / features
    outs = (ga_own, ga_a, ga_b, ga_d)
    for tile in range(8):
        part = slice(tile * 128, tile * 128 + half)
        back = inv_in[...] * (gi_s[part, :] - first - hat_in[part, :] * second)
        low = (tile % 2) * half
        outs[tile // 2][low : low + half, :] = back.astype(BF16)
    split = sums_c0.shape[2] // 2
    whole_rows = (to_out, to_gain, to_bias, to_last)
    for pair in range(4):
        contract = (sums_c0, sums_c0, sums_c1, sums_c1)[pair]
        backward = (sums_b0, sums_b0, sums_b1, sums_b1)[pair]
        for other in range(2):
            base = other * split
            index = pair * 2 + other
            for place in range(split // 128):
                lanes = slice(base + place * 128, base + place * 128 + 128)
                wide_s[index, place : place + 1, :] = backward[pair % 2, 0:1, lanes]
                wide_s[index, 3 + place : 4 + place, :] = contract[pair % 2, 0:1, lanes]
                wide_s[index, 6 + place : 7 + place, :] = contract[pair % 2, 1:2, lanes]
                for row in range(4):
                    spot = 9 + 3 * row + place
                    if pair < 3:
                        wide_s[index, spot : spot + 1, :] = whole_rows[row][:, lanes]
                    else:
                        mine = slice(place * 128, place * 128 + 128)
                        yours = slice(split + place * 128, split + place * 128 + 128)
                        swap = core if other == 0 else 1 - core
                        value = jnp.where(swap == 0, whole_rows[row][:, mine], whole_rows[row][:, yours])
                        wide_s[index, spot : spot + 1, :] = value

    def write(target, place, tile, index, inner):
        target[place, 0:model, :] = og_s[:, tile]
        target[place, model : model + 21, :] = wide_s[index, 0:21, :].astype(BF16)
        target[place, model + 21 : model + 23, :] = inner[0:2, :].astype(BF16)
        target[place, model + 23 : model + 32, :] = jnp.zeros((9, 128), BF16)

    for other in range(2):
        swap = core if other == 0 else 1 - core
        write(own, swap, slice(other * 128, other * 128 + 128), other, slim_s[other])
        write(near, swap, slice((2 + other) * 128, (2 + other) * 128 + 128), 2 + other, slim_s[2 + other])
        write(rest, 1 - swap, slice((4 + other) * 128, (4 + other) * 128 + 128), 4 + other, slim_s[4 + other])
    write(far, 0, pl.ds(pl.multiple_of((6 + core) * 128, 128), 128), 6, slim_s[6 + core])
    write(rest, 2, pl.ds(pl.multiple_of((7 - core) * 128, 128), 128), 7, slim_s[7 - core])


def struct(shape, kind):
    return jax.ShapeDtypeStruct(shape, kind)


def run(kernel, info, operands, outs, scratch, flops):
    specs = vmem_specs(len(operands))
    return pl.pallas_call(
        kernel,
        out_shape=outs,
        in_specs=[pl.BlockSpec(memory_space=pltpu.SMEM)] + specs,
        out_specs=vmem_specs(len(outs)),
        scratch_shapes=[pltpu.VMEM(value.shape, value.dtype) for value in scratch],
        cost_estimate=pl.CostEstimate(flops=flops, transcendentals=0, bytes_accessed=8 << 20),
        compiler_params=limit(scratch),
    )(info, *operands)


def mid_block(info, mixes, vecs, pieces, rows, params):
    count, model = rows.shape
    dim = mixes[0].shape[0]
    operands = (*mixes, *vecs, *pieces, rows, params)
    wide = 8 * 128
    outs = [
        struct((count, model), F32),
        struct((count, model), BF16),
        struct((model, count), BF16),
        struct((wide, count), F32),
        struct((1, count), F32),
        struct((count, wide), BF16),
        struct((wide, model), BF16),
        struct((wide, 2), F32),
    ]
    scratch = [struct((dim, model), BF16)]
    return run(mid_kernel, info, operands, outs, scratch, 2 * count * model * wide)


def expand_block(info, last, vecs, pieces, second, sums):
    count, model = second.shape
    own, near, far, w_b, other = pieces
    units = near.shape[1]
    column = struct((count, 1), F32)
    partial = struct((count, 128), F32)
    outs = [struct((2, count, units), BF16)] * 2 + [struct((2, 8, units), F32)]
    flops = 8 * count * model * units
    kernel = functools.partial(expand_kernel, last)
    if last:
        operands = (*vecs[2:], w_b, far, other, second, *sums)
        scratch = [struct((model, units), BF16)]
        return run(kernel, info, operands, outs + [column] * 2, scratch, flops)
    operands = (*vecs[:2], own, near, second)
    return run(kernel, info, operands, outs + [partial] * 2, [], flops)


def grad_outs(last, model, split):
    if last:
        return [struct((1, model, split), BF16), struct((3, model, split), BF16)]
    return [struct((2, model, split), BF16)] * 2


def contract_block(info, last, hidden, vecs, pieces, cot, turned, mean, inv, more):
    count, model = cot.shape
    units = hidden.shape[2]
    own, near, far, w_b, other = pieces
    column = struct((count, 1), F32)
    partial = struct((count, 128), F32)
    act = struct((2, count, units), BF16)
    grads = grad_outs(last, model, units // 2)
    shared = [struct((2, count, units), BF16)] + grads + [struct((2, 8, units), F32)]
    flops = 12 * count * model * units
    kernel = functools.partial(contract_kernel, last)
    if last:
        operands = (hidden, vecs, w_b, far, other, cot, turned, mean, inv, *more)
        outs = [struct((count, model), BF16)] + shared + [column] * 2
        scratch = [struct((units, model), BF16), act]
        return run(kernel, info, operands, outs, scratch, flops)
    operands = (hidden, vecs, own, near, cot, turned, mean, inv)
    outs = [struct((count, model), F32)] + shared + [partial] * 2
    return run(kernel, info, operands, outs, [act], flops)


def back_block(info, last, hidden, slope, grad_hid, vecs, pieces, turned, columns, more):
    count, units = hidden.shape[1:]
    model = turned.shape[0]
    own, near, far, w_b, other = pieces
    pre = struct((2, count, units), BF16)
    outs = [struct((count, model), F32)] + grad_outs(last, model, units // 2) + [struct((2, 8, units), F32)]
    flops = 8 * count * model * units
    kernel = functools.partial(back_kernel, last)
    if last:
        operands = (hidden, slope, grad_hid, vecs, w_b, far, other, turned, *columns)
        scratch = [struct((model, units), BF16), pre]
        return run(kernel, info, operands, outs, scratch, flops)
    operands = (hidden, slope, grad_hid, vecs, own, near, turned, *columns, *more)
    return run(kernel, info, operands, outs, [pre], flops)


EXTRA = 32


def tail_block(info, total, resid, cot, params, hat_in, inv_in, act_in, wo, cols, sums, dim):
    count, model = cot.shape
    operands = (total, resid, cot, params, hat_in, inv_in, act_in, wo, cols, *sums)
    outs = [struct((places, model + EXTRA, 128), BF16) for places in (2, 2, 1, 3)]
    outs += [struct((count, model), F32)] + [struct((dim, count), BF16)] * 4
    scratch = [
        struct((model, count), BF16),
        struct((8 * 128, count), F32),
        struct((model, 8 * 128), BF16),
        struct((count, model), BF16),
        struct((8, 24, 128), F32),
        struct((8, 8, 128), F32),
    ]
    return run(tail_kernel, info, operands, outs, scratch, 4 * count * model * 1024)


class Links:
    def __init__(self):
        self.ranks = lax.axis_size(HEAD)
        self.parts = lax.axis_size(DP)
        self.core = lax.rem(lax.axis_index(DP), 2)

    def over(self, value, near, far):
        pairs = []
        for rank in range(self.ranks):
            for part in range(self.parts):
                flip = near if part % 2 == 0 else far
                pairs.append((rank * self.parts + part, (rank ^ flip) * self.parts + part))
        return lax.ppermute(value, (HEAD, DP), pairs)

    def a(self, value):
        return self.over(value, 1, 2)

    def b(self, value):
        return self.over(value, 2, 1)

    def d(self, value):
        return self.over(value, 3, 3)

    def dp(self, value, flip):
        return lax.ppermute(value, DP, [(part, part ^ flip) for part in range(self.parts)])


def gather_weight(links, own, axis):
    near = links.a(own)
    shape = list(own.shape)
    shape[axis] //= 2
    (half,) = simple(functools.partial(half_kernel, axis), links.info, (near,), [struct(tuple(shape), BF16)])
    far = links.b(half)
    return own, near, far, links.dp(near, 1), links.dp(far, 1)


def join_core_kernel(info, near, far, got, near_out, far_out):
    count = near.shape[0]

    def step(place, unused):
        for tile in range(count):
            total = near[tile, place].astype(F32) + got[tile, place].astype(F32)
            near_out[tile, place] = total.astype(BF16)
        total = far[0, place].astype(F32) + got[count, place].astype(F32)
        far_out[0, place] = total.astype(BF16)
        return unused

    lax.fori_loop(0, near.shape[1], step, 0)


def join_far_kernel(info, near, got, near_out):
    def step(place, unused):
        total = near[0, place].astype(F32) + got[0, place].astype(F32)
        near_out[0, place] = total.astype(BF16)
        near_out[1, place] = near[1, place]
        return unused

    lax.fori_loop(0, near.shape[1], step, 0)


def simple(kernel, info, operands, outs, scratch=()):
    return run(kernel, info, operands, outs, list(scratch), 1 << 28)


def halve_kernel(swap, extra, per, level, info, value, got, keep, send):
    tiles = value.shape[0]
    blocks = value.shape[1] - extra
    bit = info[7 + level]

    def step(place, unused):
        group = place // per
        for tile in range(tiles):
            other = tiles - 1 - tile if swap else tile
            mine = place + (group + bit) * per
            yours = place + (group + 1 - bit) * per
            keep[tile, place] = value[tile, mine].astype(F32) + got[tile, mine].astype(F32)
            total = value[tile, yours].astype(F32) + got[tile, yours].astype(F32)
            send[other, place] = total.astype(BF16)
        return unused

    lax.fori_loop(0, blocks // 2, step, 0)
    for place in range(extra):
        for tile in range(tiles):
            other = tiles - 1 - tile if swap else tile
            total = value[tile, blocks + place].astype(F32) + got[tile, blocks + place].astype(F32)
            keep[tile, blocks // 2 + place] = total
            send[other, blocks // 2 + place] = total.astype(BF16)


def weight_kernel(extra, per, info, *refs):
    acts, grads = refs[0:5], refs[5:10]
    own, got, weights, keep, send, total_s = refs[10:16]
    width = grads[0].shape[0]
    thin = (keep.shape[3] - width) // 2
    rows = keep.shape[2]
    blocks = own.shape[1] - extra
    bit = info[7]
    total = 0.0
    tokens = 0.0
    for act, grad in zip(acts, grads):
        total = total + dot(grad[...], act[...], (1, 0))
        tokens = tokens + fold(grad[...].astype(F32))
    tokens = row_sum(tokens)
    wide = weights[...].astype(F32)
    norm_rows = jnp.concatenate((col_sum(wide * tokens), col_sum(wide * total)), axis=0)
    total = total.T
    for place in range(blocks):
        total_s[place] = total[place * rows : place * rows + rows, :]
    tokens = jnp.broadcast_to(tokens, (width, 128)).T[0:1, :]
    base = keep.shape[3] - 256

    def step(place, unused):
        mine = place + (place // per + bit) * per
        yours = place + (place // per + 1 - bit) * per
        keep[0, place, :, 0:width] = total_s[mine]
        send[0, place, :, 0:width] = total_s[yours].astype(BF16)
        for tile in range(2):
            low = width + tile * thin
            swapped = width + (1 - tile) * thin
            value = own[tile, mine].astype(F32) + got[tile, mine].astype(F32)
            keep[0, place, :, low : low + thin] = value[:, 0:thin]
            value = own[tile, yours].astype(F32) + got[tile, yours].astype(F32)
            send[0, place, :, swapped : swapped + thin] = value[:, 0:thin].astype(BF16)
        return unused

    lax.fori_loop(0, blocks // 2, step, 0)
    for place in range(extra):
        spot = blocks // 2 + place
        keep[0, spot] = jnp.zeros(keep.shape[2:], F32)
        send[0, spot] = jnp.zeros(send.shape[2:], BF16)
        if place == 0:
            side = norm_rows.shape[1] // 2
            pieces = [tokens[:, : width // 2]]
            for row in range(4):
                pieces.append(norm_rows[row // 2 : row // 2 + 1, (row % 2) * side : (row % 2) * side + side])
            pieces.append(tokens[:, width // 2 :])
            for row, value in enumerate(pieces):
                keep[0, spot, row : row + 1, 0 : value.shape[1]] = value
                send[0, spot, row : row + 1, 0 : value.shape[1]] = value.astype(BF16)
        for tile in range(2):
            low = base + tile * 128
            swapped = base + (1 - tile) * 128
            value = own[tile, blocks + place].astype(F32) + got[tile, blocks + place].astype(F32)
            keep[0, spot, :, low : low + 128] = value
            send[0, spot, :, swapped : swapped + 128] = value.astype(BF16)


def cot_kernel(info, whole, rows_out, turned, sem):
    count = rows_out.shape[0]
    low = pl.multiple_of(info[6] * count, count)
    copy = pltpu.make_async_copy(whole.at[pl.ds(low, count), :], rows_out, sem)
    copy.start()
    copy.wait()

    def work(part, state):
        turned[:, part] = turn(rows_out[part, :])
        return state

    each(count, work, unroll=1)


def cot_block(info, whole, count):
    model = whole.shape[1]
    return pl.pallas_call(
        cot_kernel,
        out_shape=[struct((count, model), BF16), struct((model, count), BF16)],
        in_specs=[pl.BlockSpec(memory_space=pltpu.SMEM), pl.BlockSpec(memory_space=pl.ANY)],
        out_specs=vmem_specs(2),
        scratch_shapes=[pltpu.SemaphoreType.DMA(())],
        cost_estimate=pl.CostEstimate(flops=1 << 28, transcendentals=0, bytes_accessed=4 << 20),
        compiler_params=limit([]),
        name="ct",
    )(info, whole)


def half_kernel(axis, info, value, out):
    size = out.shape[axis]
    part = pl.ds(pl.multiple_of(info[5] * size, 128), size)
    out[...] = value[:, part] if axis else value[part, :]


def halve(links, value, got, flip, extra, per, swap):
    tiles, count, rows, units = value.shape
    shape = (tiles, (count - extra) // 2 + extra, rows, units)
    kernel = functools.partial(halve_kernel, swap, extra, per, flip.bit_length() - 1)
    return simple(kernel, links.info, (value, got), [struct(shape, F32), struct(shape, BF16)])


def block_rows(share):
    return EXTRA if share % EXTRA == 0 else share


def by_part(links, value, extra):
    tiles, rows, units = value.shape
    size = block_rows((rows - extra) // links.parts)
    spare = -rows % size
    if spare:
        value = jnp.concatenate((value, jnp.zeros((tiles, spare, units), value.dtype)), axis=1)
    return value.reshape(tiles, -1, size, units)


def over_head(links, own, near, far, rest, extra):
    own, near, far, rest = [by_part(links, value, extra) for value in (own, near, far, rest)]
    got = links.dp(rest, 1)
    near, far = simple(
        join_core_kernel, links.info, (near, far, got), [struct(near.shape, BF16), struct(far.shape, BF16)]
    )
    got = links.b(far)
    (near,) = simple(join_far_kernel, links.info, (near, got), [struct(near.shape, BF16)])
    return own, links.a(near)


def last_kernel(extra, per, level, info, value, got, other, other_got, keep, other_keep, send):
    bit = info[7 + level]
    mine = bit * per
    yours = (1 - bit) * per
    units = other.shape[3]
    base = per + extra
    for place in range(per):
        keep[0, place] = value[0, mine + place].astype(F32) + got[0, mine + place].astype(F32)
        total = value[0, yours + place].astype(F32) + got[0, yours + place].astype(F32)
        send[0, place] = total.astype(BF16)
        for tile in range(2):
            lanes = slice(tile * units, tile * units + units)
            total = other[tile, mine + place].astype(F32) + other_got[tile, mine + place].astype(F32)
            other_keep[0, place, :, lanes] = total
            total = other[tile, yours + place].astype(F32) + other_got[tile, yours + place].astype(F32)
            send[0, base + place, :, lanes] = total.astype(BF16)
    for place in range(extra):
        total = value[0, 2 * per + place].astype(F32) + got[0, 2 * per + place].astype(F32)
        keep[0, per + place] = total
        send[0, per + place] = total.astype(BF16)


def end_kernel(info, keep, got, other, qkv, out_grad, fc1, raw, side_s):
    per = other.shape[1]
    rows = other.shape[2]
    extra = keep.shape[1] - per
    dim = qkv.shape[2]
    half = dim // 2
    units = fc1.shape[1] // 2
    core = info[5]
    for place in range(per):
        part = slice(place * rows, place * rows + rows)
        value = keep[0, place] + got[0, place].astype(F32)
        for index in range(3):
            qkv[index, part, :] = value[:, index * dim : index * dim + dim]
        side_s[part, :] = value[:, 3 * dim : 4 * dim]
        value = other[0, place] + got[0, per + extra + place].astype(F32)
        fc1[part, pl.ds(pl.multiple_of(core * units, 128), units)] = value[:, :units]
        fc1[part, pl.ds(pl.multiple_of((1 - core) * units, 128), units)] = value[:, units:]
    for place in range(extra):
        raw[place * rows : place * rows + rows, :] = keep[0, per + place] + got[0, per + place].astype(F32)
    turned = side_s[...].T
    out_grad[pl.ds(pl.multiple_of(core * half, 8), half), :] = turned[:half]
    out_grad[pl.ds(pl.multiple_of((1 - core) * half, 8), half), :] = turned[half:]


def scatter_some(links, keep, got, flip, stop, extra, per, swap):
    while flip < stop:
        keep, send = halve(links, keep, got, flip, extra, per, swap and flip == 1)
        got = links.dp(send, flip)
        flip *= 2
    return keep, got


def scatter_all(links, own, got):
    per = own.shape[1] // links.parts
    keep, got = scatter_some(links, own, got, 1, links.parts, 0, per, True)
    done = keep + got.astype(F32)
    return done.reshape(done.shape[0], -1, done.shape[3])


def fetch(pairs, sems):
    copies = [pltpu.make_async_copy(source, target, sems.at[index]) for index, (source, target) in enumerate(pairs)]
    for copy in copies:
        copy.start()
    for copy in copies:
        copy.wait()


def pack_kernel(info, *refs):
    sources = refs[0:12]
    vec, column, params = refs[12:15]
    held = refs[15:27]
    fetch(list(zip(sources, held)), refs[27])
    wide = vec.shape[1]
    dim = held[9].shape[0]
    params[...] = jnp.zeros_like(params)
    for row in range(6):
        params[row : row + 1, :] = held[row][...].reshape(1, wide)
    vec[...] = jnp.zeros_like(vec)
    for row in range(3):
        vec[row : row + 1, :] = held[6 + row][...].astype(F32).reshape(1, wide)
    vec[3:4, 0:dim] = held[9][...].reshape(1, dim)
    vec[4:5, 0:dim] = held[10][...].reshape(1, dim)
    qv_bias = held[11]
    zero = jnp.zeros((6, dim), F32)
    turned = jnp.concatenate((qv_bias[...], zero), axis=0).T
    column[0:dim, :] = turned[:, 0:1]
    column[dim : 2 * dim, :] = jnp.zeros((dim, 1), F32)
    column[2 * dim : 3 * dim, :] = turned[:, 1:2]


def first_norm_kernel(info, rows_in, gain_in, bias_in, out, rows, gain, bias, sems):
    fetch([(rows_in, rows), (gain_in, gain), (bias_in, bias)], sems)
    model = rows.shape[1]
    wide_gain = gain[...].reshape(1, model)
    wide_bias = bias[...].reshape(1, model)

    def work(part, state):
        value = rows[part, :].astype(F32)
        centred = value - row_sum(value) / model
        scale = lax.rsqrt(row_sum(centred * centred) / model + EPS)
        out[part, :] = (centred * scale * wide_gain + wide_bias).astype(BF16)
        return state

    each(rows.shape[0], work, unroll=1)


def fetching(kernel, info, operands, outs):
    scratch = [pltpu.VMEM(value.shape, value.dtype) for value in operands]
    return pl.pallas_call(
        kernel,
        out_shape=outs,
        in_specs=[pl.BlockSpec(memory_space=pltpu.SMEM)] + [pl.BlockSpec(memory_space=pl.ANY)] * len(operands),
        out_specs=vmem_specs(len(outs)),
        scratch_shapes=scratch + [pltpu.SemaphoreType.DMA((len(operands),))],
        cost_estimate=pl.CostEstimate(flops=1 << 28, transcendentals=0, bytes_accessed=4 << 20),
        compiler_params=limit(operands),
    )(info, *operands)


def partial_kernel(info, part_a, part_b, low, high, out_a, out_b):
    half = low.shape[0]

    def work(part, state):
        upper = pl.ds(pl.multiple_of(part.start + half, ROWS), ROWS)
        out_a[part, :] = (part_a[part, :] + low[part, :].astype(F32)).astype(BF16)
        out_a[upper, :] = part_a[upper, :].astype(BF16)
        out_b[part, :] = part_b[part, :].astype(BF16)
        out_b[upper, :] = (part_b[upper, :] + high[part, :].astype(F32)).astype(BF16)
        return state

    each(half, work, unroll=1)


def final_kernel(info, rows, params, mid, mine, got_a, got_b, out):
    model = rows.shape[1]

    def work(part, state):
        value = rows[part, :].astype(F32)
        centred = value - row_sum(value) / model
        scale = lax.rsqrt(row_sum(centred * centred) / model + EPS)
        hat = centred * scale
        grad = mine[part, :] + got_a[part, :].astype(F32) + got_b[part, :].astype(F32)
        grad = grad * params[0:1, :]
        back = scale * (grad - row_sum(grad) / model - hat * (row_sum(grad * hat) / model))
        out[part, :] = (mid[part, :] + back).astype(BF16)
        return state

    each(rows.shape[0], work, unroll=1)


def layer(
    inputs,
    bucket,
    norm1_gain,
    norm1_bias,
    qkv_weight,
    qv_bias,
    inner_gain,
    inner_bias,
    out_weight,
    out_bias,
    norm2_gain,
    norm2_bias,
    fc1_weight,
    fc1_bias,
    ffn_gain,
    ffn_bias,
    fc2_weight,
    fc2_bias,
    cotangent,
):
    links = Links()
    core = links.core
    rows = inputs.shape[0]
    model = inputs.shape[2]
    dim = qkv_weight.shape[2]
    heads = dim // HEAD_DIM
    hidden_share = fc1_weight.shape[1]
    units = hidden_share // 2
    rank = lax.axis_index(HEAD)
    part = lax.axis_index(DP)
    bits = []
    while 2 ** len(bits) < links.parts:
        bits.append(lax.rem(part // 2 ** len(bits), 2))
    info = jnp.stack([rank, rank ^ (1 + core), rank ^ (2 - core), rank ^ 3, bucket[0], core, rank] + bits)
    info = info.astype(jnp.int32)
    links.info = info

    own_rows = inputs.reshape(rows, model)
    (first_own,) = fetching(first_norm_kernel, info, (own_rows, norm1_gain, norm1_bias), [struct((rows, model), BF16)])
    vec_own, bias_t, params = fetching(
        pack_kernel,
        info,
        (norm1_gain, norm1_bias, out_bias, norm2_gain, norm2_bias, fc2_bias)
        + (fc1_bias, ffn_gain, ffn_bias, inner_gain, inner_bias, qv_bias),
        [struct((8, hidden_share), F32), struct((3 * dim, 1), F32), struct((8, model), F32)],
    )
    first_a = links.a(first_own)
    first_b = links.b(first_own)
    half = rows // 2
    low_d = links.b(first_a[:half])
    high_d = links.a(first_b[half:])
    first_acts = (first_own, first_a, first_b, low_d, high_d)

    vecs = (vec_own, links.a(vec_own), links.b(vec_own), links.d(vec_own))

    w0 = gather_weight(links, out_weight, 1)
    w1 = gather_weight(links, fc1_weight, 1)
    w2 = gather_weight(links, fc2_weight, 0)

    qkv_t = jnp.swapaxes(qkv_weight, 1, 2).reshape(3 * dim, model)
    qkv = []
    for act in first_acts:
        qkv.append((dot(qkv_t, act, (1, 1)) + bias_t).astype(BF16))
    mixed, lse = attend(info, qkv, heads)

    mixes = (mixed[0], links.a(mixed[1]), links.b(mixed[2]), links.d(mixed[3]))
    resid_mid, second_act, second_t, hat_in, inv_in, act_in, wo, cols = mid_block(
        info, mixes, vecs, w0, own_rows, params
    )
    cot, cot_t = cot_block(info, cotangent.reshape(-1, model), rows)
    hidden0, slope0, vecs0, *sums = expand_block(info, False, vecs, w1, second_act, ())
    hidden1, slope1, vecs1, mean, inv = expand_block(info, True, vecs, w1, second_act, sums)
    ffn, grad0, fc2_own, fc2_near, sums_c0, *sums = contract_block(
        info, False, hidden0, vecs0, w2, cot, cot_t, mean, inv, ()
    )
    output, grad1, fc2_far, fc2_rest, sums_c1, hat_sum, hat_dot = contract_block(
        info, True, hidden1, vecs1, w2, cot, cot_t, mean, inv, (ffn, *sums, resid_mid, params)
    )
    columns = (mean, inv, hat_sum, hat_dot)
    total, fc1_far, fc1_rest, sums_b1 = back_block(
        info, True, hidden1, slope1, grad1, vecs1, w1, second_t, columns, ()
    )
    total, fc1_own, fc1_near, sums_b0 = back_block(
        info, False, hidden0, slope0, grad0, vecs0, w1, second_t, columns, (total,)
    )
    out_own, out_near, out_far, out_rest, grad_mid, ga_own, ga_a, ga_b, ga_d = tail_block(
        info, total, resid_mid, cot, params, hat_in, inv_in, act_in, wo, cols,
        (sums_c0, sums_c1, sums_b0, sums_b1), dim
    )

    fc2_grad = scatter_all(links, *over_head(links, fc2_own, fc2_near, fc2_far, fc2_rest, 0))
    group1 = over_head(links, fc1_own, fc1_near, fc1_far, fc1_rest, 0)
    group0 = over_head(links, out_own, out_near, out_far, out_rest, EXTRA)

    grads = (ga_own, links.a(ga_a), links.b(ga_b), links.d(ga_d))
    grad_qkv = attend_back(info, qkv, mixed, grads, lse, heads)

    low_d = links.b(dot(grad_qkv[3], qkv_t, (0, 0)).astype(BF16))
    high_d = links.a(dot(grad_qkv[4], qkv_t, (0, 0)).astype(BF16))
    part_a = dot(grad_qkv[1], qkv_t, (0, 0))
    part_b = dot(grad_qkv[2], qkv_t, (0, 0))
    mine = dot(grad_qkv[0], qkv_t, (0, 0))
    part_a, part_b = simple(partial_kernel, info, (part_a, part_b, low_d, high_d), [struct((rows, model), BF16)] * 2)
    got_a = links.a(part_a)
    got_b = links.b(part_b)
    (input_grad,) = simple(
        final_kernel, info, (own_rows, params, grad_mid, mine, got_a, got_b), [struct((rows, model), BF16)]
    )

    share = model // links.parts
    size = block_rows(share)
    per = share // size
    spare = -(-EXTRA // size)
    lanes = 4 * dim
    shape = (1, links.parts // 2 * per + spare, size, lanes)
    keep, send = run(
        functools.partial(weight_kernel, spare, per), info, (*first_acts, *grad_qkv, *group0, qkv_t),
        [struct(shape, F32), struct(shape, BF16)], [struct((links.parts * per, size, 3 * dim), F32)], 1 << 31
    )
    got = links.dp(send, 1)
    last = links.parts // 2
    value, got = scatter_some(links, keep, got, 2, last, spare, per, False)
    other, other_got = scatter_some(links, *group1, 1, last, 0, per, True)
    keep, other_keep, send = run(
        functools.partial(last_kernel, spare, per, last.bit_length() - 1),
        info,
        (value, got, other, other_got),
        [
            struct((1, per + spare, size, lanes), F32),
            struct((1, per, size, hidden_share), F32),
            struct((1, 2 * per + spare, size, lanes), BF16),
        ],
        [],
        1 << 28,
    )
    got = links.dp(send, last)
    norm1_sum = keep[0, per, 1:5, : model // 2]
    norm1_sum = norm1_sum + links.a(norm1_sum) + links.b(norm1_sum) + links.d(norm1_sum)
    norm1_sum = norm1_sum + links.dp(norm1_sum, last)
    norm1_sum = norm1_sum.reshape(2, model)
    qkv_grad, out_grad, fc1_grad, raw = simple(
        end_kernel,
        info,
        (keep, got, other_keep),
        [
            struct((3, share, dim), F32),
            struct((dim, share), F32),
            struct((share, hidden_share), F32),
            struct((spare * size, lanes), F32),
        ],
        [struct((share, dim), F32)],
    )
    vec_all = raw[:EXTRA, lanes - 256 :]
    vec_all = jnp.stack((vec_all[:, :128], vec_all[:, 128:]))
    side = 3 * dim // 2
    token_all = jnp.concatenate((raw[0, :side], raw[5, :side]))

    norm1_sum = lax.dynamic_slice_in_dim(norm1_sum, part * share, share, 1)
    my_gain = lax.dynamic_slice_in_dim(norm1_gain, part * share, share, 0)
    my_bias = lax.dynamic_slice_in_dim(norm1_bias, part * share, share, 0)
    grad_norm1_bias = norm1_sum[0]
    grad_norm1_gain = (norm1_sum[1] - my_bias * norm1_sum[0]) / my_gain

    def in_order(value):
        return jnp.where(core == 0, value, value[::-1])

    fc2_grad = jnp.swapaxes(in_order(fc2_grad), 1, 2).reshape(hidden_share, share)
    vec_all = in_order(vec_all)
    wide = vec_all[:, :21].reshape(2, 7, units)
    wide = jnp.swapaxes(wide, 0, 1).reshape(7, model)
    slim = jnp.swapaxes(vec_all[:, 21:23, : dim // 2], 0, 1).reshape(2, dim)
    mine = lax.dynamic_slice_in_dim(wide, part * share, share, 1)
    thin = lax.dynamic_slice_in_dim(slim, part * (dim // links.parts), dim // links.parts, 1)
    qv_all = token_all.reshape(3, dim)
    qv_grad = lax.dynamic_slice_in_dim(
        jnp.stack((qv_all[0], qv_all[2])), part * (dim // links.parts), dim // links.parts, 1
    )

    return (
        output.reshape(rows, 1, model),
        input_grad.reshape(rows, 1, model),
        qkv_grad,
        out_grad,
        fc1_grad,
        fc2_grad,
        qv_grad,
        thin[0],
        thin[1],
        mine[0],
        mine[1],
        mine[2],
        grad_norm1_gain,
        grad_norm1_bias,
        mine[3],
        mine[4],
        mine[5],
        mine[6],
    )


def solution(mesh):
    in_specs = (
        P(HEAD, DP, None),
        P(DP),
        P(),
        P(),
        P(None, None, HEAD),
        P(None, HEAD),
        P(HEAD),
        P(HEAD),
        P(HEAD, None),
        P(),
        P(),
        P(),
        P(None, HEAD),
        P(HEAD),
        P(HEAD),
        P(HEAD),
        P(HEAD, None),
        P(),
        P(None, DP, None),
    )
    out_specs = (
        P(HEAD, DP, None),
        P(HEAD, DP, None),
        P(None, DP, HEAD),
        P(HEAD, DP),
        P(DP, HEAD),
        P(HEAD, DP),
        P(None, (HEAD, DP)),
        P((HEAD, DP)),
        P((HEAD, DP)),
        P((HEAD, DP)),
        P((HEAD, DP)),
        P((HEAD, DP)),
        P(DP),
        P(DP),
        P(DP),
        P(DP),
        P(DP),
        P(DP),
    )

    return jax.shard_map(layer, mesh=mesh, in_specs=in_specs, out_specs=out_specs, check_vma=False)
```

```python
import functools

import jax
import jax.numpy as jnp
from jax import lax
from jax.experimental import pallas as pl
from jax.experimental.pallas import tpu as pltpu
from jax.sharding import PartitionSpec as P


HEAD = "head"
DP = "dp"
HEAD_DIM = 64
EPS = 1e-05
NEG = -1e30
F32 = jnp.float32
BF16 = jnp.bfloat16
SQRT_HALF = 0.7071067811865476
INV_SQRT_2PI = 0.3989422804014327


def dot(left, right, contract):
    return lax.dot_general(left, right, ((contract[0:1], contract[1:2]), ((), ())), preferred_element_type=F32)


def diag_mask(scores, start=0):
    key_pos = lax.broadcasted_iota(jnp.int32, scores.shape, 0)
    row_pos = lax.broadcasted_iota(jnp.int32, scores.shape, 1)
    return key_pos <= row_pos + start


def halves(rows):
    half = rows // 2
    return ((slice(0, half), slice(0, half)), (slice(0, rows), slice(half, rows)))


def spans(qkv):
    rows = qkv[0].shape[1]
    half = rows // 2
    result = [(slot, slice(0, rows), qkv[slot]) for slot in range(3)]
    return result + [(3, slice(0, half), qkv[3]), (3, slice(half, rows), qkv[4])]


def attend_kernel(heads, info, *refs):
    slots = 4
    qkv = refs[0:5]
    outs = refs[5:9]
    lse_ref = refs[9]
    q_s, k_s, v_s, o_s = refs[10:14]
    width = heads * HEAD_DIM
    scale = HEAD_DIM ** (-0.5)
    for slot, span, array in spans(qkv):
        block = info[slot]
        q_s[block, :, span] = array[0:width, :] * jnp.asarray(scale, BF16)
        v_s[block, :, span] = array[2 * width : 3 * width, :]
        for head in range(heads):
            low = width + head * HEAD_DIM
            k_s[block, head, span, :] = turn(array[low : low + HEAD_DIM, :])
    is_long = info[4]

    def step(row, key, carry, first):
        result = []
        for head in range(heads):
            part = pl.ds(head * HEAD_DIM, HEAD_DIM)
            scores = dot(k_s[key, head], q_s[row, part, :], (1, 0))
            if first:
                scores = jnp.where(diag_mask(scores), scores, NEG)
                peak = jnp.max(scores, axis=0, keepdims=True)
                weights = jnp.exp(scores - peak)
                total = jnp.sum(weights, axis=0, keepdims=True)
                mixed = dot(v_s[key, part, :], weights.astype(BF16), (1, 0))
            else:
                old_peak, old_total, old_mixed = carry[head]
                peak = jnp.maximum(old_peak, jnp.max(scores, axis=0, keepdims=True))
                fade = jnp.exp(old_peak - peak)
                weights = jnp.exp(scores - peak)
                total = old_total * fade + jnp.sum(weights, axis=0, keepdims=True)
                mixed = old_mixed * fade + dot(v_s[key, part, :], weights.astype(BF16), (1, 0))
            result.append((peak, total, mixed))
        return tuple(result)

    def row_block(row, unused):
        carry = step(row, row, None, True)
        low = jnp.where(is_long > 0, 0, row)
        carry = lax.fori_loop(low, row, lambda key, c: step(row, key, c, False), carry)
        for head in range(heads):
            peak, total, mixed = carry[head]
            o_s[row, pl.ds(head * HEAD_DIM, HEAD_DIM), :] = (mixed / total).astype(BF16)
            lse_ref[row, pl.ds(head, 1), :] = peak + jnp.log(total)
        return unused

    lax.fori_loop(0, slots, row_block, 0)
    for slot in range(slots):
        outs[slot][...] = o_s[info[slot]]


def back_step(heads, row, key, carry, first, arrays, grad_out):
    q_s, qr_s, k_s, kr_s, vr_s, g_s, gr_s, delta_s, lse_ref = arrays
    result = []
    for head in range(heads):
        part = pl.ds(head * HEAD_DIM, HEAD_DIM)
        if first:
            found = []
            for keys, rows in halves(kr_s.shape[2]):
                scores = dot(kr_s[key, head, keys, :], q_s[row, part, rows], (1, 0))
                weights = jnp.exp(scores - lse_ref[row, pl.ds(head, 1), rows])
                weights = jnp.where(diag_mask(scores, rows.start), weights, 0.0)
                grad_weights = dot(vr_s[key, head, keys, :], g_s[row, part, rows], (1, 0))
                grad_scores = (weights * (grad_weights - delta_s[row, pl.ds(head, 1), rows])).astype(BF16)
                grad_key = dot(grad_scores, qr_s[row, head, rows, :], (1, 0))
                grad_value = dot(weights.astype(BF16), gr_s[row, head, rows, :], (1, 0))
                found.append((grad_key, grad_value, dot(k_s[key, part, keys], grad_scores, (1, 0))))
            half = found[0][0].shape[0]
            sums = [
                jnp.concatenate((found[1][index][:half] + found[0][index], found[1][index][half:]), axis=0)
                for index in range(2)
            ]
            grad_out(key, head, *sums)
            result.append(jnp.concatenate((found[0][2], found[1][2]), axis=1))
            continue
        scores = dot(kr_s[key, head], q_s[row, part, :], (1, 0))
        weights = jnp.exp(scores - lse_ref[row, pl.ds(head, 1), :])
        grad_weights = dot(vr_s[key, head], g_s[row, part, :], (1, 0))
        grad_scores = (weights * (grad_weights - delta_s[row, pl.ds(head, 1), :])).astype(BF16)
        grad_out(key, head, dot(grad_scores, qr_s[row, head], (1, 0)), dot(weights.astype(BF16), gr_s[row, head], (1, 0)))
        grad_query = dot(k_s[key, part, :], grad_scores, (1, 0))
        result.append(carry[head] + grad_query)
    return tuple(result)


def early_kernel(heads, info, *refs):
    qkv = refs[0:5]
    mixed = refs[5:9]
    grads = refs[9:13]
    lse_ref = refs[13]
    q_s, qr_s, k_s, kr_s, vr_s, g_s, gr_s, delta_s, dq_s, dk_s, dv_s = refs[14:25]
    width = heads * HEAD_DIM
    scale = HEAD_DIM ** (-0.5)
    for slot, span, array in spans(qkv):
        block = info[slot]
        scaled = array[0:width, :] * jnp.asarray(scale, BF16)
        q_s[block, :, span] = scaled
        k_s[block, :, span] = array[width : 2 * width, :]
        for head in range(heads):
            low = head * HEAD_DIM
            high = low + HEAD_DIM
            qr_s[block, head, span, :] = turn(scaled[low:high, :])
            kr_s[block, head, span, :] = turn(array[width + low : width + high, :])
            vr_s[block, head, span, :] = turn(array[2 * width + low : 2 * width + high, :])
    for slot in range(4):
        block = info[slot]
        g_s[block] = grads[slot][...]
        for head in range(heads):
            low = head * HEAD_DIM
            high = low + HEAD_DIM
            gr_s[block, head] = turn(grads[slot][low:high, :])
            product = grads[slot][low:high, :].astype(F32) * mixed[slot][low:high, :].astype(F32)
            delta_s[block, pl.ds(head, 1), :] = jnp.sum(product, axis=0, keepdims=True)
    is_long = info[4]
    arrays = (q_s, qr_s, k_s, kr_s, vr_s, g_s, gr_s, delta_s, lse_ref)

    def write(key, head, grad_key, grad_value):
        dk_s[key, head] = grad_key
        dv_s[key, head] = grad_value

    def add(key, head, grad_key, grad_value):
        dk_s[key, head] += grad_key
        dv_s[key, head] += grad_value

    def row_block(row, unused):
        carry = back_step(heads, row, row, None, True, arrays, write)
        low = jnp.where(is_long > 0, 0, row)
        carry = lax.fori_loop(
            low, row, lambda key, c: back_step(heads, row, key, c, False, arrays, add), carry
        )
        for head in range(heads):
            dq_s[row, pl.ds(head * HEAD_DIM, HEAD_DIM), :] = (carry[head] * scale).astype(BF16)
        return unused

    lax.fori_loop(0, 3, row_block, 0)


def late_kernel(heads, info, *refs):
    arrays = refs[0:8] + (refs[11],)
    dq_in, dk_in, dv_in = refs[8:11]
    outs = refs[12:17]
    dq_s, dk_s, dv_s = refs[17:20]
    width = heads * HEAD_DIM
    scale = HEAD_DIM ** (-0.5)
    is_long = info[4]
    last = 3
    dq_s[0:last] = dq_in[0:last]

    def write(key, head, grad_key, grad_value):
        dk_s[key, head] = grad_key
        dv_s[key, head] = grad_value

    def add(key, head, grad_key, grad_value):
        dk_s[key, head] = dk_in[key, head] + grad_key
        dv_s[key, head] = dv_in[key, head] + grad_value

    carry = back_step(heads, last, last, None, True, arrays, write)
    low = jnp.where(is_long > 0, 0, last)
    carry = lax.fori_loop(low, last, lambda key, c: back_step(heads, last, key, c, False, arrays, add), carry)
    for head in range(heads):
        dq_s[last, pl.ds(head * HEAD_DIM, HEAD_DIM), :] = (carry[head] * scale).astype(BF16)

    @pl.when(is_long == 0)
    def _():
        dk_s[0:last] = dk_in[0:last]
        dv_s[0:last] = dv_in[0:last]

    for slot, span, array in spans(outs):
        block = info[slot]
        array[0:width, :] = dq_s[block, :, span]
        for head in range(heads):
            low = width + head * HEAD_DIM
            array[low : low + HEAD_DIM, :] = dk_s[block, head, span, :].T.astype(BF16)
            low = low + width
            array[low : low + HEAD_DIM, :] = dv_s[block, head, span, :].T.astype(BF16)


def turn(value):
    return value.astype(F32).T.astype(BF16)


def vmem_specs(count):
    return [pl.BlockSpec(memory_space=pltpu.VMEM)] * count


def footprint(array):
    shape = (1,) * (2 - len(array.shape)) + tuple(array.shape)
    size = jnp.dtype(array.dtype).itemsize
    rows = -(-shape[-2] // 8) * 8 if shape[-2] > 1 else 1
    lanes = -(-shape[-1] // 128) * 128
    total = rows * lanes * size
    for extent in shape[:-2]:
        total *= extent
    return total


def limit(arrays):
    total = sum(footprint(array) for array in arrays) + SPARE
    return pltpu.CompilerParams(vmem_limit_bytes=total)


SPARE = 6 * 1024 * 1024


def attend(info, qkv, heads):
    rows = qkv[0].shape[1]
    width = heads * HEAD_DIM
    flat = struct((4, width, rows), BF16)
    scratch = [flat, struct((4, heads, rows, HEAD_DIM), BF16), flat, flat]
    outs = [struct((width, rows), BF16)] * 4 + [struct((4, heads, rows), F32)]
    flops = 40 * heads * HEAD_DIM * rows * rows
    result = run(functools.partial(attend_kernel, heads), info, qkv, outs, scratch, flops)
    return result[:4], result[4]


def attend_back(info, qkv, mixed, grads, lse, heads):
    rows = qkv[0].shape[1]
    width = heads * HEAD_DIM
    flat = struct((4, width, rows), BF16)
    turned = struct((4, heads, rows, HEAD_DIM), BF16)
    total = struct((4, heads, rows, HEAD_DIM), F32)
    outs = [flat, turned, flat, turned, turned, flat, turned, struct((4, heads, rows), F32), flat, total, total]
    flops = 50 * heads * HEAD_DIM * rows * rows
    kernel = functools.partial(early_kernel, heads)
    kept = run(kernel, info, (*qkv, *mixed, *grads, lse), outs, [], flops)
    outs = [struct((3 * width, rows), BF16)] * 3 + [struct((3 * width, rows // 2), BF16)] * 2
    kernel = functools.partial(late_kernel, heads)
    return run(kernel, info, (*kept, lse), outs, [flat, total, total], flops)


ROWS = 128
UNROLL = 4


def fold(value):
    total = value[:, 0:128]
    for place in range(128, value.shape[1], 128):
        total = total + value[:, place : place + 128]
    return total


def row_sum(value):
    return jnp.sum(value, axis=1, keepdims=True)


def col_sum(value):
    return jnp.sum(value, axis=0, keepdims=True)


def each(rows, body, carry=0, unroll=UNROLL):
    def step(index, state):
        for place in range(unroll):
            state = body(pl.ds(pl.multiple_of((index * unroll + place) * ROWS, ROWS), ROWS), state)
        return state

    if rows == unroll * ROWS:
        for place in range(unroll):
            carry = body(pl.ds(place * ROWS, ROWS), carry)
        return carry
    return lax.fori_loop(0, rows // ROWS // unroll, step, carry)


def mid_kernel(
    info, mix_own, mix_a, mix_b, mix_d, vec_own, vec_a, vec_b, vec_d, w_own, w_near, w_far, w_b, w_other, rows_ref,
    params, resid_ref, second_ref, turned_ref, hat_ref, inv_ref, act_ref, wo_ref, cols_ref, side_s
):
    core = info[5]
    model = rows_ref.shape[1]
    mixes = (mix_own, mix_a, mix_b, mix_d)
    vecs = (vec_own, vec_a, vec_b, vec_d)
    dim = mix_own.shape[0]
    count = 4 * dim
    half = dim // 2
    split = model // 2
    total = 0.0
    for mix in mixes:
        total = total + col_sum(mix[...].astype(F32))
    mean = total / count
    square = 0.0
    for mix in mixes:
        centred = mix[...].astype(F32) - mean
        square = square + col_sum(centred * centred)
    inv = lax.rsqrt(square / count + EPS)
    inv_ref[...] = inv
    side_s[:, pl.ds(pl.multiple_of(core * split, 128), split)] = w_far[...]
    side_s[:, pl.ds(pl.multiple_of((1 - core) * split, 128), split)] = w_other[...]
    weights = (w_own, w_near, w_b, side_s)
    for slot in range(4):
        cols = vecs[slot][...].T
        for other in range(2):
            part = slice(other * half, other * half + half)
            low = (slot * 2 + other) * 128
            mine = slice(low, low + half)
            pad = slice(low + half, low + 128)
            wo_ref[mine, :] = weights[slot][part, :]
            wo_ref[pad, :] = jnp.zeros((128 - half, model), BF16)
            hat = (mixes[slot][part, :].astype(F32) - mean) * inv
            hat_ref[mine, :] = hat
            hat_ref[pad, :] = jnp.zeros((128 - half, hat.shape[1]), F32)
            cols_ref[mine, :] = cols[part, 3:5]
            cols_ref[pad, :] = jnp.zeros((128 - half, 2), F32)
            act = hat * cols[part, 3:4] + cols[part, 4:5]
            act_ref[:, mine] = turn(act)
            act_ref[:, pad] = jnp.zeros((act_ref.shape[0], 128 - half), BF16)

    def finish(part, state):
        branch = dot(act_ref[part, :], wo_ref[...], (1, 0))
        resid = rows_ref[part, :].astype(F32) + branch + params[2:3, :]
        resid_ref[part, :] = resid
        centred = resid - row_sum(resid) / model
        scale = lax.rsqrt(row_sum(centred * centred) / model + EPS)
        second = centred * scale * params[3:4, :] + params[4:5, :]
        second_ref[part, :] = second.astype(BF16)
        turned_ref[:, part] = turn(second)
        return state

    each(rows_ref.shape[0], finish)


def expand_kernel(last, info, *refs):
    if last:
        vec_b, vec_d, w_b, w_far, w_other, second, sum_in, square_in = refs[:8]
        hidden, slope, vecs, mean_ref, inv_ref, w_s = refs[8:]
    else:
        vec_own, vec_a, w_own, w_near, second = refs[:5]
        hidden, slope, vecs, sum_ref, square_ref = refs[5:]
    units = hidden.shape[2]
    split = units // 2
    core = info[5]
    if last:
        vecs[0] = vec_b[...]
        vecs[1, :, 0:split] = vec_d[:, pl.ds(pl.multiple_of(core * split, 128), split)]
        vecs[1, :, split:units] = vec_d[:, pl.ds(pl.multiple_of((1 - core) * split, 128), split)]
        w_s[:, 0:split] = w_far[...]
        w_s[:, split:units] = w_other[...]
        pairs = (w_b, w_s)
    else:
        vecs[0] = vec_own[...]
        vecs[1] = vec_a[...]
        pairs = (w_own, w_near)

    def work(part, state):
        sums = sum_in[part, :] if last else 0.0
        squares = square_in[part, :] if last else 0.0
        for pair in range(2):
            pre = dot(second[part, :], pairs[pair][...], (1, 0)) + vecs[pair, 0:1, :]
            phi = 0.5 + 0.5 * lax.erf(pre * SQRT_HALF)
            act = pre * phi
            hidden[pair, part, :] = act.astype(BF16)
            slope[pair, part, :] = (phi + pre * (INV_SQRT_2PI * jnp.exp(-0.5 * (pre * pre)))).astype(BF16)
            sums = sums + fold(act)
            squares = squares + fold(act * act)
        if last:
            mean = row_sum(sums) / (4 * units)
            mean_ref[part, :] = mean
            inv_ref[part, :] = lax.rsqrt(row_sum(squares) / (4 * units) - mean * mean + EPS)
        else:
            sum_ref[part, :] = sums
            square_ref[part, :] = squares
        return state

    each(second.shape[0], work)


def put_first(core, pair, value, own, near):
    target = own if pair == 0 else near
    split = value.shape[1] // 2
    target[core] = value[:, 0:split].astype(BF16)
    target[1 - core] = value[:, split:].astype(BF16)


def put_last(core, pair, value, far, rest):
    split = value.shape[1] // 2
    if pair == 0:
        rest[1 - core] = value[:, 0:split].astype(BF16)
        rest[core] = value[:, split:].astype(BF16)
    else:
        far[0] = value[:, 0:split].astype(BF16)
        rest[2] = value[:, split:].astype(BF16)


def contract_kernel(last, info, *refs):
    if last:
        hidden, vecs, w_b, w_far, w_other, cot, turned, mean, inv, total_in, sum_in, dot_in, resid, params = refs[:14]
        out, grad_hid, far, rest, sums, hat_sum, hat_dot, w_s, act_s = refs[14:]
    else:
        hidden, vecs, w_own, w_near, cot, turned, mean, inv = refs[:8]
        total, grad_hid, own, near, sums, sum_ref, dot_ref, act_s = refs[8:]
    units = hidden.shape[2]
    core = info[5]
    if last:
        w_s[0 : units // 2, :] = w_far[...]
        w_s[units // 2 : units, :] = w_other[...]
        pairs = (w_b, w_s)
    else:
        pairs = (w_own, w_near)

    def work(part, state):
        by_gain, by_bias = [list(value) for value in state]
        shift = mean[part, :]
        scale = inv[part, :]
        hat_sums = sum_in[part, :] if last else 0.0
        hat_dots = dot_in[part, :] if last else 0.0
        ffn = total_in[part, :] if last else 0.0
        for pair in range(2):
            gain = vecs[pair, 1:2, :]
            grad = dot(cot[part, :], pairs[pair][...], (1, 1))
            grad_hid[pair, part, :] = grad.astype(BF16)
            hat = (hidden[pair, part, :].astype(F32) - shift) * scale
            act = (hat * gain + vecs[pair, 2:3, :]).astype(BF16)
            act_s[pair, part, :] = act
            product = grad * hat
            hat_sums = hat_sums + fold(grad * gain)
            hat_dots = hat_dots + fold(product * gain)
            by_gain[pair] = by_gain[pair] + col_sum(product)
            by_bias[pair] = by_bias[pair] + col_sum(grad)
            ffn = ffn + dot(act, pairs[pair][...], (1, 0))
        if last:
            out[part, :] = (resid[part, :] + ffn + params[5:6, :]).astype(BF16)
            hat_sum[part, :] = row_sum(hat_sums) / (4 * units)
            hat_dot[part, :] = row_sum(hat_dots) / (4 * units)
        else:
            total[part, :] = ffn
            sum_ref[part, :] = hat_sums
            dot_ref[part, :] = hat_dots
        return tuple(by_gain), tuple(by_bias)

    zero = jnp.zeros((1, units), F32)
    by_gain, by_bias = each(cot.shape[0], work, ((zero, zero), (zero, zero)))
    for pair in range(2):
        sums[pair, 0:1, :] = by_gain[pair]
        sums[pair, 1:2, :] = by_bias[pair]
        value = dot(turned[...], act_s[pair], (1, 0))
        if last:
            put_last(core, pair, value, far, rest)
        else:
            put_first(core, pair, value, own, near)


def back_kernel(last, info, *refs):
    if last:
        hidden, slope, grad_hid, vecs, w_b, w_far, w_other, turned, mean, inv, hat_sum, hat_dot = refs[:12]
        total, far, rest, sums, w_s, pre_s = refs[12:]
    else:
        hidden, slope, grad_hid, vecs, w_own, w_near, turned, mean, inv, hat_sum, hat_dot, total_in = refs[:12]
        total, own, near, sums, pre_s = refs[12:]
    units = hidden.shape[2]
    core = info[5]
    if last:
        w_s[:, 0 : units // 2] = w_far[...]
        w_s[:, units // 2 : units] = w_other[...]
        pairs = (w_b, w_s)
    else:
        pairs = (w_own, w_near)

    def work(part, state):
        by_bias = list(state)
        shift = mean[part, :]
        scale = inv[part, :]
        second = 0.0 if last else total_in[part, :]
        for pair in range(2):
            hat = (hidden[pair, part, :].astype(F32) - shift) * scale
            grad = grad_hid[pair, part, :].astype(F32) * vecs[pair, 1:2, :] - hat_sum[part, :] - hat * hat_dot[part, :]
            pre = (scale * grad * slope[pair, part, :].astype(F32)).astype(BF16)
            pre_s[pair, part, :] = pre
            by_bias[pair] = by_bias[pair] + col_sum(pre.astype(F32))
            second = second + dot(pre, pairs[pair][...], (1, 1))
        total[part, :] = second
        return tuple(by_bias)

    zero = jnp.zeros((1, units), F32)
    by_bias = each(hidden.shape[1], work, (zero, zero))
    for pair in range(2):
        sums[pair, 0:1, :] = by_bias[pair]
        value = dot(turned[...], pre_s[pair], (1, 0))
        if last:
            put_last(core, pair, value, far, rest)
        else:
            put_first(core, pair, value, own, near)


def tail_kernel(
    info, total, resid, cot, params, hat_in, inv_in, act_in, wo, cols, sums_c0, sums_c1, sums_b0, sums_b1, own, near,
    far, rest, mid_ref, ga_own, ga_a, ga_b, ga_d, turned_s, gi_s, og_s, low_s, wide_s, slim_s
):
    rows, model = cot.shape
    core = info[5]

    def second_norm(part, state):
        to_gain, to_bias, to_out, to_last = state
        centred = resid[part, :]
        centred = centred - row_sum(centred) / model
        scale = lax.rsqrt(row_sum(centred * centred) / model + EPS)
        hat = centred * scale
        up = total[part, :]
        grad = up * params[3:4, :]
        back = scale * (grad - row_sum(grad) / model - hat * (row_sum(grad * hat) / model))
        wide = cot[part, :].astype(F32)
        mid = wide + back
        mid_ref[part, :] = mid
        low = mid.astype(BF16)
        low_s[part, :] = low
        turned_s[:, part] = turn(low)
        to_gain = to_gain + col_sum(up * hat)
        to_bias = to_bias + col_sum(up)
        to_out = to_out + col_sum(low.astype(F32))
        to_last = to_last + col_sum(wide)
        return to_gain, to_bias, to_out, to_last

    zero = jnp.zeros((1, model), F32)
    to_gain, to_bias, to_out, to_last = each(rows, second_norm, (zero, zero, zero, zero))
    gi_s[...] = dot(wo[...], turned_s[...], (1, 0))
    og_s[...] = dot(turned_s[...], act_in[...], (1, 0)).astype(BF16)
    features = 4 * ga_own.shape[0]
    half = ga_own.shape[0] // 2
    lane = lax.broadcasted_iota(jnp.int32, (128, 128), 1)

    def inner(part, state):
        index, first, second = state
        up = gi_s[part, :]
        hat = hat_in[part, :]
        side = jnp.where(lane == 0, row_sum(up * hat), jnp.where(lane == 1, row_sum(up), 0.0)).T
        slim_s[index] = side[0:8, :]
        grad = up * cols[part, 0:1]
        gi_s[part, :] = grad
        return index + 1, first + col_sum(grad), second + col_sum(grad * hat)

    zero = jnp.zeros((1, rows), F32)
    _, first, second = each(gi_s.shape[0], inner, (0, zero, zero))
    first = first / features
    second = second / features
    outs = (ga_own, ga_a, ga_b, ga_d)
    for tile in range(8):
        part = slice(tile * 128, tile * 128 + half)
        back = inv_in[...] * (gi_s[part, :] - first - hat_in[part, :] * second)
        low = (tile % 2) * half
        outs[tile // 2][low : low + half, :] = back.astype(BF16)
    split = sums_c0.shape[2] // 2
    whole_rows = (to_out, to_gain, to_bias, to_last)
    for pair in range(4):
        contract = (sums_c0, sums_c0, sums_c1, sums_c1)[pair]
        backward = (sums_b0, sums_b0, sums_b1, sums_b1)[pair]
        for other in range(2):
            base = other * split
            index = pair * 2 + other
            for place in range(split // 128):
                lanes = slice(base + place * 128, base + place * 128 + 128)
                wide_s[index, place : place + 1, :] = backward[pair % 2, 0:1, lanes]
                wide_s[index, 3 + place : 4 + place, :] = contract[pair % 2, 0:1, lanes]
                wide_s[index, 6 + place : 7 + place, :] = contract[pair % 2, 1:2, lanes]
                for row in range(4):
                    spot = 9 + 3 * row + place
                    if pair < 3:
                        wide_s[index, spot : spot + 1, :] = whole_rows[row][:, lanes]
                    else:
                        mine = slice(place * 128, place * 128 + 128)
                        yours = slice(split + place * 128, split + place * 128 + 128)
                        swap = core if other == 0 else 1 - core
                        value = jnp.where(swap == 0, whole_rows[row][:, mine], whole_rows[row][:, yours])
                        wide_s[index, spot : spot + 1, :] = value

    def write(target, place, tile, index, inner):
        target[place, 0:model, :] = og_s[:, tile]
        target[place, model : model + 21, :] = wide_s[index, 0:21, :].astype(BF16)
        target[place, model + 21 : model + 23, :] = inner[0:2, :].astype(BF16)
        target[place, model + 23 : model + 32, :] = jnp.zeros((9, 128), BF16)

    for other in range(2):
        swap = core if other == 0 else 1 - core
        write(own, swap, slice(other * 128, other * 128 + 128), other, slim_s[other])
        write(near, swap, slice((2 + other) * 128, (2 + other) * 128 + 128), 2 + other, slim_s[2 + other])
        write(rest, 1 - swap, slice((4 + other) * 128, (4 + other) * 128 + 128), 4 + other, slim_s[4 + other])
    write(far, 0, pl.ds(pl.multiple_of((6 + core) * 128, 128), 128), 6, slim_s[6 + core])
    write(rest, 2, pl.ds(pl.multiple_of((7 - core) * 128, 128), 128), 7, slim_s[7 - core])


def struct(shape, kind):
    return jax.ShapeDtypeStruct(shape, kind)


def run(kernel, info, operands, outs, scratch, flops):
    specs = vmem_specs(len(operands))
    return pl.pallas_call(
        kernel,
        out_shape=outs,
        in_specs=[pl.BlockSpec(memory_space=pltpu.SMEM)] + specs,
        out_specs=vmem_specs(len(outs)),
        scratch_shapes=[pltpu.VMEM(value.shape, value.dtype) for value in scratch],
        cost_estimate=pl.CostEstimate(flops=flops, transcendentals=0, bytes_accessed=8 << 20),
        compiler_params=limit(scratch),
    )(info, *operands)


def mid_block(info, mixes, vecs, pieces, rows, params):
    count, model = rows.shape
    dim = mixes[0].shape[0]
    operands = (*mixes, *vecs, *pieces, rows, params)
    wide = 8 * 128
    outs = [
        struct((count, model), F32),
        struct((count, model), BF16),
        struct((model, count), BF16),
        struct((wide, count), F32),
        struct((1, count), F32),
        struct((count, wide), BF16),
        struct((wide, model), BF16),
        struct((wide, 2), F32),
    ]
    scratch = [struct((dim, model), BF16)]
    return run(mid_kernel, info, operands, outs, scratch, 2 * count * model * wide)


def expand_block(info, last, vecs, pieces, second, sums):
    count, model = second.shape
    own, near, far, w_b, other = pieces
    units = near.shape[1]
    column = struct((count, 1), F32)
    partial = struct((count, 128), F32)
    outs = [struct((2, count, units), BF16)] * 2 + [struct((2, 8, units), F32)]
    flops = 8 * count * model * units
    kernel = functools.partial(expand_kernel, last)
    if last:
        operands = (*vecs[2:], w_b, far, other, second, *sums)
        scratch = [struct((model, units), BF16)]
        return run(kernel, info, operands, outs + [column] * 2, scratch, flops)
    operands = (*vecs[:2], own, near, second)
    return run(kernel, info, operands, outs + [partial] * 2, [], flops)


def grad_outs(last, model, split):
    if last:
        return [struct((1, model, split), BF16), struct((3, model, split), BF16)]
    return [struct((2, model, split), BF16)] * 2


def contract_block(info, last, hidden, vecs, pieces, cot, turned, mean, inv, more):
    count, model = cot.shape
    units = hidden.shape[2]
    own, near, far, w_b, other = pieces
    column = struct((count, 1), F32)
    partial = struct((count, 128), F32)
    act = struct((2, count, units), BF16)
    grads = grad_outs(last, model, units // 2)
    shared = [struct((2, count, units), BF16)] + grads + [struct((2, 8, units), F32)]
    flops = 12 * count * model * units
    kernel = functools.partial(contract_kernel, last)
    if last:
        operands = (hidden, vecs, w_b, far, other, cot, turned, mean, inv, *more)
        outs = [struct((count, model), BF16)] + shared + [column] * 2
        scratch = [struct((units, model), BF16), act]
        return run(kernel, info, operands, outs, scratch, flops)
    operands = (hidden, vecs, own, near, cot, turned, mean, inv)
    outs = [struct((count, model), F32)] + shared + [partial] * 2
    return run(kernel, info, operands, outs, [act], flops)


def back_block(info, last, hidden, slope, grad_hid, vecs, pieces, turned, columns, more):
    count, units = hidden.shape[1:]
    model = turned.shape[0]
    own, near, far, w_b, other = pieces
    pre = struct((2, count, units), BF16)
    outs = [struct((count, model), F32)] + grad_outs(last, model, units // 2) + [struct((2, 8, units), F32)]
    flops = 8 * count * model * units
    kernel = functools.partial(back_kernel, last)
    if last:
        operands = (hidden, slope, grad_hid, vecs, w_b, far, other, turned, *columns)
        scratch = [struct((model, units), BF16), pre]
        return run(kernel, info, operands, outs, scratch, flops)
    operands = (hidden, slope, grad_hid, vecs, own, near, turned, *columns, *more)
    return run(kernel, info, operands, outs, [pre], flops)


EXTRA = 32


def tail_block(info, total, resid, cot, params, hat_in, inv_in, act_in, wo, cols, sums, dim):
    count, model = cot.shape
    operands = (total, resid, cot, params, hat_in, inv_in, act_in, wo, cols, *sums)
    outs = [struct((places, model + EXTRA, 128), BF16) for places in (2, 2, 1, 3)]
    outs += [struct((count, model), F32)] + [struct((dim, count), BF16)] * 4
    scratch = [
        struct((model, count), BF16),
        struct((8 * 128, count), F32),
        struct((model, 8 * 128), BF16),
        struct((count, model), BF16),
        struct((8, 24, 128), F32),
        struct((8, 8, 128), F32),
    ]
    return run(tail_kernel, info, operands, outs, scratch, 4 * count * model * 1024)


class Links:
    def __init__(self):
        self.ranks = lax.axis_size(HEAD)
        self.parts = lax.axis_size(DP)
        self.core = lax.rem(lax.axis_index(DP), 2)

    def over(self, value, near, far):
        pairs = []
        for rank in range(self.ranks):
            for part in range(self.parts):
                flip = near if part % 2 == 0 else far
                pairs.append((rank * self.parts + part, (rank ^ flip) * self.parts + part))
        return lax.ppermute(value, (HEAD, DP), pairs)

    def a(self, value):
        return self.over(value, 1, 2)

    def b(self, value):
        return self.over(value, 2, 1)

    def d(self, value):
        return self.over(value, 3, 3)

    def dp(self, value, flip):
        return lax.ppermute(value, DP, [(part, part ^ flip) for part in range(self.parts)])


def gather_weight(links, own, axis):
    near = links.a(own)
    shape = list(own.shape)
    shape[axis] //= 2
    (half,) = simple(functools.partial(half_kernel, axis), links.info, (near,), [struct(tuple(shape), BF16)])
    far = links.b(half)
    return own, near, far, links.dp(near, 1), links.dp(far, 1)


def join_core_kernel(info, near, far, got, near_out, far_out):
    count = near.shape[0]

    def step(place, unused):
        for tile in range(count):
            total = near[tile, place].astype(F32) + got[tile, place].astype(F32)
            near_out[tile, place] = total.astype(BF16)
        total = far[0, place].astype(F32) + got[count, place].astype(F32)
        far_out[0, place] = total.astype(BF16)
        return unused

    lax.fori_loop(0, near.shape[1], step, 0)


def join_far_kernel(info, near, got, near_out):
    def step(place, unused):
        total = near[0, place].astype(F32) + got[0, place].astype(F32)
        near_out[0, place] = total.astype(BF16)
        near_out[1, place] = near[1, place]
        return unused

    lax.fori_loop(0, near.shape[1], step, 0)


def simple(kernel, info, operands, outs, scratch=()):
    return run(kernel, info, operands, outs, list(scratch), 1 << 28)


def halve_kernel(swap, extra, per, level, info, value, got, keep, send):
    tiles = value.shape[0]
    blocks = value.shape[1] - extra
    bit = info[7 + level]

    def step(place, unused):
        group = place // per
        for tile in range(tiles):
            other = tiles - 1 - tile if swap else tile
            mine = place + (group + bit) * per
            yours = place + (group + 1 - bit) * per
            keep[tile, place] = value[tile, mine].astype(F32) + got[tile, mine].astype(F32)
            total = value[tile, yours].astype(F32) + got[tile, yours].astype(F32)
            send[other, place] = total.astype(BF16)
        return unused

    lax.fori_loop(0, blocks // 2, step, 0)
    for place in range(extra):
        for tile in range(tiles):
            other = tiles - 1 - tile if swap else tile
            total = value[tile, blocks + place].astype(F32) + got[tile, blocks + place].astype(F32)
            keep[tile, blocks // 2 + place] = total
            send[other, blocks // 2 + place] = total.astype(BF16)


def weight_kernel(extra, per, info, *refs):
    acts, grads = refs[0:5], refs[5:10]
    own, got, weights, keep, send, total_s = refs[10:16]
    width = grads[0].shape[0]
    thin = (keep.shape[3] - width) // 2
    rows = keep.shape[2]
    blocks = own.shape[1] - extra
    bit = info[7]
    total = 0.0
    tokens = 0.0
    for act, grad in zip(acts, grads):
        total = total + dot(grad[...], act[...], (1, 0))
        tokens = tokens + fold(grad[...].astype(F32))
    tokens = row_sum(tokens)
    wide = weights[...].astype(F32)
    norm_rows = jnp.concatenate((col_sum(wide * tokens), col_sum(wide * total)), axis=0)
    total = total.T
    for place in range(blocks):
        total_s[place] = total[place * rows : place * rows + rows, :]
    tokens = jnp.broadcast_to(tokens, (width, 128)).T[0:1, :]
    base = keep.shape[3] - 256

    def step(place, unused):
        mine = place + (place // per + bit) * per
        yours = place + (place // per + 1 - bit) * per
        keep[0, place, :, 0:width] = total_s[mine]
        send[0, place, :, 0:width] = total_s[yours].astype(BF16)
        for tile in range(2):
            low = width + tile * thin
            swapped = width + (1 - tile) * thin
            value = own[tile, mine].astype(F32) + got[tile, mine].astype(F32)
            keep[0, place, :, low : low + thin] = value[:, 0:thin]
            value = own[tile, yours].astype(F32) + got[tile, yours].astype(F32)
            send[0, place, :, swapped : swapped + thin] = value[:, 0:thin].astype(BF16)
        return unused

    lax.fori_loop(0, blocks // 2, step, 0)
    for place in range(extra):
        spot = blocks // 2 + place
        keep[0, spot] = jnp.zeros(keep.shape[2:], F32)
        send[0, spot] = jnp.zeros(send.shape[2:], BF16)
        if place == 0:
            side = norm_rows.shape[1] // 2
            pieces = [tokens[:, : width // 2]]
            for row in range(4):
                pieces.append(norm_rows[row // 2 : row // 2 + 1, (row % 2) * side : (row % 2) * side + side])
            pieces.append(tokens[:, width // 2 :])
            for row, value in enumerate(pieces):
                keep[0, spot, row : row + 1, 0 : value.shape[1]] = value
                send[0, spot, row : row + 1, 0 : value.shape[1]] = value.astype(BF16)
        for tile in range(2):
            low = base + tile * 128
            swapped = base + (1 - tile) * 128
            value = own[tile, blocks + place].astype(F32) + got[tile, blocks + place].astype(F32)
            keep[0, spot, :, low : low + 128] = value
            send[0, spot, :, swapped : swapped + 128] = value.astype(BF16)


def cot_kernel(info, whole, rows_out, turned, sem):
    count = rows_out.shape[0]
    low = pl.multiple_of(info[6] * count, count)
    copy = pltpu.make_async_copy(whole.at[pl.ds(low, count), :], rows_out, sem)
    copy.start()
    copy.wait()

    def work(part, state):
        turned[:, part] = turn(rows_out[part, :])
        return state

    each(count, work, unroll=1)


def cot_block(info, whole, count):
    model = whole.shape[1]
    return pl.pallas_call(
        cot_kernel,
        out_shape=[struct((count, model), BF16), struct((model, count), BF16)],
        in_specs=[pl.BlockSpec(memory_space=pltpu.SMEM), pl.BlockSpec(memory_space=pl.ANY)],
        out_specs=vmem_specs(2),
        scratch_shapes=[pltpu.SemaphoreType.DMA(())],
        cost_estimate=pl.CostEstimate(flops=1 << 28, transcendentals=0, bytes_accessed=4 << 20),
        compiler_params=limit([]),
        name="ct",
    )(info, whole)


def half_kernel(axis, info, value, out):
    size = out.shape[axis]
    part = pl.ds(pl.multiple_of(info[5] * size, 128), size)
    out[...] = value[:, part] if axis else value[part, :]


def halve(links, value, got, flip, extra, per, swap):
    tiles, count, rows, units = value.shape
    shape = (tiles, (count - extra) // 2 + extra, rows, units)
    kernel = functools.partial(halve_kernel, swap, extra, per, flip.bit_length() - 1)
    return simple(kernel, links.info, (value, got), [struct(shape, F32), struct(shape, BF16)])


def block_rows(share):
    return EXTRA if share % EXTRA == 0 else share


def by_part(links, value, extra):
    tiles, rows, units = value.shape
    size = block_rows((rows - extra) // links.parts)
    spare = -rows % size
    if spare:
        value = jnp.concatenate((value, jnp.zeros((tiles, spare, units), value.dtype)), axis=1)
    return value.reshape(tiles, -1, size, units)


def over_head(links, own, near, far, rest, extra):
    own, near, far, rest = [by_part(links, value, extra) for value in (own, near, far, rest)]
    got = links.dp(rest, 1)
    near, far = simple(
        join_core_kernel, links.info, (near, far, got), [struct(near.shape, BF16), struct(far.shape, BF16)]
    )
    got = links.b(far)
    (near,) = simple(join_far_kernel, links.info, (near, got), [struct(near.shape, BF16)])
    return own, links.a(near)


def last_kernel(extra, per, level, info, value, got, other, other_got, keep, other_keep, send):
    bit = info[7 + level]
    mine = bit * per
    yours = (1 - bit) * per
    units = other.shape[3]
    base = per + extra
    for place in range(per):
        keep[0, place] = value[0, mine + place].astype(F32) + got[0, mine + place].astype(F32)
        total = value[0, yours + place].astype(F32) + got[0, yours + place].astype(F32)
        send[0, place] = total.astype(BF16)
        for tile in range(2):
            lanes = slice(tile * units, tile * units + units)
            total = other[tile, mine + place].astype(F32) + other_got[tile, mine + place].astype(F32)
            other_keep[0, place, :, lanes] = total
            total = other[tile, yours + place].astype(F32) + other_got[tile, yours + place].astype(F32)
            send[0, base + place, :, lanes] = total.astype(BF16)
    for place in range(extra):
        total = value[0, 2 * per + place].astype(F32) + got[0, 2 * per + place].astype(F32)
        keep[0, per + place] = total
        send[0, per + place] = total.astype(BF16)


def end_kernel(info, keep, got, other, qkv, out_grad, fc1, raw, side_s):
    per = other.shape[1]
    rows = other.shape[2]
    extra = keep.shape[1] - per
    dim = qkv.shape[2]
    half = dim // 2
    units = fc1.shape[1] // 2
    core = info[5]
    for place in range(per):
        part = slice(place * rows, place * rows + rows)
        value = keep[0, place] + got[0, place].astype(F32)
        for index in range(3):
            qkv[index, part, :] = value[:, index * dim : index * dim + dim]
        side_s[part, :] = value[:, 3 * dim : 4 * dim]
        value = other[0, place] + got[0, per + extra + place].astype(F32)
        fc1[part, pl.ds(pl.multiple_of(core * units, 128), units)] = value[:, :units]
        fc1[part, pl.ds(pl.multiple_of((1 - core) * units, 128), units)] = value[:, units:]
    for place in range(extra):
        raw[place * rows : place * rows + rows, :] = keep[0, per + place] + got[0, per + place].astype(F32)
    turned = side_s[...].T
    out_grad[pl.ds(pl.multiple_of(core * half, 8), half), :] = turned[:half]
    out_grad[pl.ds(pl.multiple_of((1 - core) * half, 8), half), :] = turned[half:]


def scatter_some(links, keep, got, flip, stop, extra, per, swap):
    while flip < stop:
        keep, send = halve(links, keep, got, flip, extra, per, swap and flip == 1)
        got = links.dp(send, flip)
        flip *= 2
    return keep, got


def scatter_all(links, own, got):
    per = own.shape[1] // links.parts
    keep, got = scatter_some(links, own, got, 1, links.parts, 0, per, True)
    done = keep + got.astype(F32)
    return done.reshape(done.shape[0], -1, done.shape[3])


def fetch(pairs, sems):
    copies = [pltpu.make_async_copy(source, target, sems.at[index]) for index, (source, target) in enumerate(pairs)]
    for copy in copies:
        copy.start()
    for copy in copies:
        copy.wait()


def pack_kernel(info, *refs):
    sources = refs[0:12]
    vec, column, params = refs[12:15]
    held = refs[15:27]
    fetch(list(zip(sources, held)), refs[27])
    wide = vec.shape[1]
    dim = held[9].shape[0]
    params[...] = jnp.zeros_like(params)
    for row in range(6):
        params[row : row + 1, :] = held[row][...].reshape(1, wide)
    vec[...] = jnp.zeros_like(vec)
    for row in range(3):
        vec[row : row + 1, :] = held[6 + row][...].astype(F32).reshape(1, wide)
    vec[3:4, 0:dim] = held[9][...].reshape(1, dim)
    vec[4:5, 0:dim] = held[10][...].reshape(1, dim)
    qv_bias = held[11]
    zero = jnp.zeros((6, dim), F32)
    turned = jnp.concatenate((qv_bias[...], zero), axis=0).T
    column[0:dim, :] = turned[:, 0:1]
    column[dim : 2 * dim, :] = jnp.zeros((dim, 1), F32)
    column[2 * dim : 3 * dim, :] = turned[:, 1:2]


def first_norm_kernel(info, rows_in, gain_in, bias_in, out, rows, gain, bias, sems):
    fetch([(rows_in, rows), (gain_in, gain), (bias_in, bias)], sems)
    model = rows.shape[1]
    wide_gain = gain[...].reshape(1, model)
    wide_bias = bias[...].reshape(1, model)

    def work(part, state):
        value = rows[part, :].astype(F32)
        centred = value - row_sum(value) / model
        scale = lax.rsqrt(row_sum(centred * centred) / model + EPS)
        out[part, :] = (centred * scale * wide_gain + wide_bias).astype(BF16)
        return state

    each(rows.shape[0], work, unroll=1)


def fetching(kernel, info, operands, outs):
    scratch = [pltpu.VMEM(value.shape, value.dtype) for value in operands]
    return pl.pallas_call(
        kernel,
        out_shape=outs,
        in_specs=[pl.BlockSpec(memory_space=pltpu.SMEM)] + [pl.BlockSpec(memory_space=pl.ANY)] * len(operands),
        out_specs=vmem_specs(len(outs)),
        scratch_shapes=scratch + [pltpu.SemaphoreType.DMA((len(operands),))],
        cost_estimate=pl.CostEstimate(flops=1 << 28, transcendentals=0, bytes_accessed=4 << 20),
        compiler_params=limit(operands),
    )(info, *operands)


def partial_kernel(info, part_a, part_b, low, high, out_a, out_b):
    half = low.shape[0]

    def work(part, state):
        upper = pl.ds(pl.multiple_of(part.start + half, ROWS), ROWS)
        out_a[part, :] = (part_a[part, :] + low[part, :].astype(F32)).astype(BF16)
        out_a[upper, :] = part_a[upper, :].astype(BF16)
        out_b[part, :] = part_b[part, :].astype(BF16)
        out_b[upper, :] = (part_b[upper, :] + high[part, :].astype(F32)).astype(BF16)
        return state

    each(half, work, unroll=1)


def final_kernel(info, rows, params, mid, mine, got_a, got_b, out):
    model = rows.shape[1]

    def work(part, state):
        value = rows[part, :].astype(F32)
        centred = value - row_sum(value) / model
        scale = lax.rsqrt(row_sum(centred * centred) / model + EPS)
        hat = centred * scale
        grad = mine[part, :] + got_a[part, :].astype(F32) + got_b[part, :].astype(F32)
        grad = grad * params[0:1, :]
        back = scale * (grad - row_sum(grad) / model - hat * (row_sum(grad * hat) / model))
        out[part, :] = (mid[part, :] + back).astype(BF16)
        return state

    each(rows.shape[0], work, unroll=1)


def layer(
    inputs,
    bucket,
    norm1_gain,
    norm1_bias,
    qkv_weight,
    qv_bias,
    inner_gain,
    inner_bias,
    out_weight,
    out_bias,
    norm2_gain,
    norm2_bias,
    fc1_weight,
    fc1_bias,
    ffn_gain,
    ffn_bias,
    fc2_weight,
    fc2_bias,
    cotangent,
):
    links = Links()
    core = links.core
    rows = inputs.shape[0]
    model = inputs.shape[2]
    dim = qkv_weight.shape[2]
    heads = dim // HEAD_DIM
    hidden_share = fc1_weight.shape[1]
    units = hidden_share // 2
    rank = lax.axis_index(HEAD)
    part = lax.axis_index(DP)
    bits = []
    while 2 ** len(bits) < links.parts:
        bits.append(lax.rem(part // 2 ** len(bits), 2))
    info = jnp.stack([rank, rank ^ (1 + core), rank ^ (2 - core), rank ^ 3, bucket[0], core, rank] + bits)
    info = info.astype(jnp.int32)
    links.info = info

    own_rows = inputs.reshape(rows, model)
    (first_own,) = fetching(first_norm_kernel, info, (own_rows, norm1_gain, norm1_bias), [struct((rows, model), BF16)])
    vec_own, bias_t, params = fetching(
        pack_kernel,
        info,
        (norm1_gain, norm1_bias, out_bias, norm2_gain, norm2_bias, fc2_bias)
        + (fc1_bias, ffn_gain, ffn_bias, inner_gain, inner_bias, qv_bias),
        [struct((8, hidden_share), F32), struct((3 * dim, 1), F32), struct((8, model), F32)],
    )
    first_a = links.a(first_own)
    first_b = links.b(first_own)
    half = rows // 2
    low_d = links.b(first_a[:half])
    high_d = links.a(first_b[half:])
    first_acts = (first_own, first_a, first_b, low_d, high_d)

    vecs = (vec_own, links.a(vec_own), links.b(vec_own), links.d(vec_own))

    w0 = gather_weight(links, out_weight, 1)
    w1 = gather_weight(links, fc1_weight, 1)
    w2 = gather_weight(links, fc2_weight, 0)

    qkv_t = jnp.swapaxes(qkv_weight, 1, 2).reshape(3 * dim, model)
    qkv = []
    for act in first_acts:
        qkv.append((dot(qkv_t, act, (1, 1)) + bias_t).astype(BF16))
    mixed, lse = attend(info, qkv, heads)

    mixes = (mixed[0], links.a(mixed[1]), links.b(mixed[2]), links.d(mixed[3]))
    resid_mid, second_act, second_t, hat_in, inv_in, act_in, wo, cols = mid_block(
        info, mixes, vecs, w0, own_rows, params
    )
    cot, cot_t = cot_block(info, cotangent.reshape(-1, model), rows)
    hidden0, slope0, vecs0, *sums = expand_block(info, False, vecs, w1, second_act, ())
    hidden1, slope1, vecs1, mean, inv = expand_block(info, True, vecs, w1, second_act, sums)
    ffn, grad0, fc2_own, fc2_near, sums_c0, *sums = contract_block(
        info, False, hidden0, vecs0, w2, cot, cot_t, mean, inv, ()
    )
    output, grad1, fc2_far, fc2_rest, sums_c1, hat_sum, hat_dot = contract_block(
        info, True, hidden1, vecs1, w2, cot, cot_t, mean, inv, (ffn, *sums, resid_mid, params)
    )
    columns = (mean, inv, hat_sum, hat_dot)
    total, fc1_far, fc1_rest, sums_b1 = back_block(
        info, True, hidden1, slope1, grad1, vecs1, w1, second_t, columns, ()
    )
    total, fc1_own, fc1_near, sums_b0 = back_block(
        info, False, hidden0, slope0, grad0, vecs0, w1, second_t, columns, (total,)
    )
    out_own, out_near, out_far, out_rest, grad_mid, ga_own, ga_a, ga_b, ga_d = tail_block(
        info, total, resid_mid, cot, params, hat_in, inv_in, act_in, wo, cols,
        (sums_c0, sums_c1, sums_b0, sums_b1), dim
    )

    fc2_grad = scatter_all(links, *over_head(links, fc2_own, fc2_near, fc2_far, fc2_rest, 0))
    group1 = over_head(links, fc1_own, fc1_near, fc1_far, fc1_rest, 0)
    group0 = over_head(links, out_own, out_near, out_far, out_rest, EXTRA)

    grads = (ga_own, links.a(ga_a), links.b(ga_b), links.d(ga_d))
    grad_qkv = attend_back(info, qkv, mixed, grads, lse, heads)

    low_d = links.b(dot(grad_qkv[3], qkv_t, (0, 0)).astype(BF16))
    high_d = links.a(dot(grad_qkv[4], qkv_t, (0, 0)).astype(BF16))
    part_a = dot(grad_qkv[1], qkv_t, (0, 0))
    part_b = dot(grad_qkv[2], qkv_t, (0, 0))
    mine = dot(grad_qkv[0], qkv_t, (0, 0))
    part_a, part_b = simple(partial_kernel, info, (part_a, part_b, low_d, high_d), [struct((rows, model), BF16)] * 2)
    got_a = links.a(part_a)
    got_b = links.b(part_b)
    (input_grad,) = simple(
        final_kernel, info, (own_rows, params, grad_mid, mine, got_a, got_b), [struct((rows, model), BF16)]
    )

    share = model // links.parts
    size = block_rows(share)
    per = share // size
    spare = -(-EXTRA // size)
    lanes = 4 * dim
    shape = (1, links.parts // 2 * per + spare, size, lanes)
    keep, send = run(
        functools.partial(weight_kernel, spare, per), info, (*first_acts, *grad_qkv, *group0, qkv_t),
        [struct(shape, F32), struct(shape, BF16)], [struct((links.parts * per, size, 3 * dim), F32)], 1 << 31
    )
    got = links.dp(send, 1)
    last = links.parts // 2
    value, got = scatter_some(links, keep, got, 2, last, spare, per, False)
    other, other_got = scatter_some(links, *group1, 1, last, 0, per, True)
    keep, other_keep, send = run(
        functools.partial(last_kernel, spare, per, last.bit_length() - 1),
        info,
        (value, got, other, other_got),
        [
            struct((1, per + spare, size, lanes), F32),
            struct((1, per, size, hidden_share), F32),
            struct((1, 2 * per + spare, size, lanes), BF16),
        ],
        [],
        1 << 28,
    )
    got = links.dp(send, last)
    norm1_sum = keep[0, per, 1:5, : model // 2]
    norm1_sum = norm1_sum + links.a(norm1_sum) + links.b(norm1_sum) + links.d(norm1_sum)
    norm1_sum = norm1_sum + links.dp(norm1_sum, last)
    norm1_sum = norm1_sum.reshape(2, model)
    qkv_grad, out_grad, fc1_grad, raw = simple(
        end_kernel,
        info,
        (keep, got, other_keep),
        [
            struct((3, share, dim), F32),
            struct((dim, share), F32),
            struct((share, hidden_share), F32),
            struct((spare * size, lanes), F32),
        ],
        [struct((share, dim), F32)],
    )
    vec_all = raw[:EXTRA, lanes - 256 :]
    vec_all = jnp.stack((vec_all[:, :128], vec_all[:, 128:]))
    side = 3 * dim // 2
    token_all = jnp.concatenate((raw[0, :side], raw[5, :side]))

    norm1_sum = lax.dynamic_slice_in_dim(norm1_sum, part * share, share, 1)
    my_gain = lax.dynamic_slice_in_dim(norm1_gain, part * share, share, 0)
    my_bias = lax.dynamic_slice_in_dim(norm1_bias, part * share, share, 0)
    grad_norm1_bias = norm1_sum[0]
    grad_norm1_gain = (norm1_sum[1] - my_bias * norm1_sum[0]) / my_gain

    def in_order(value):
        return jnp.where(core == 0, value, value[::-1])

    fc2_grad = jnp.swapaxes(in_order(fc2_grad), 1, 2).reshape(hidden_share, share)
    vec_all = in_order(vec_all)
    wide = vec_all[:, :21].reshape(2, 7, units)
    wide = jnp.swapaxes(wide, 0, 1).reshape(7, model)
    slim = jnp.swapaxes(vec_all[:, 21:23, : dim // 2], 0, 1).reshape(2, dim)
    mine = lax.dynamic_slice_in_dim(wide, part * share, share, 1)
    thin = lax.dynamic_slice_in_dim(slim, part * (dim // links.parts), dim // links.parts, 1)
    qv_all = token_all.reshape(3, dim)
    qv_grad = lax.dynamic_slice_in_dim(
        jnp.stack((qv_all[0], qv_all[2])), part * (dim // links.parts), dim // links.parts, 1
    )

    return (
        output.reshape(rows, 1, model),
        input_grad.reshape(rows, 1, model),
        qkv_grad,
        out_grad,
        fc1_grad,
        fc2_grad,
        qv_grad,
        thin[0],
        thin[1],
        mine[0],
        mine[1],
        mine[2],
        grad_norm1_gain,
        grad_norm1_bias,
        mine[3],
        mine[4],
        mine[5],
        mine[6],
    )


def solution(mesh):
    in_specs = (
        P(HEAD, DP, None),
        P(DP),
        P(),
        P(),
        P(None, None, HEAD),
        P(None, HEAD),
        P(HEAD),
        P(HEAD),
        P(HEAD, None),
        P(),
        P(),
        P(),
        P(None, HEAD),
        P(HEAD),
        P(HEAD),
        P(HEAD),
        P(HEAD, None),
        P(),
        P(None, DP, None),
    )
    out_specs = (
        P(HEAD, DP, None),
        P(HEAD, DP, None),
        P(None, DP, HEAD),
        P(HEAD, DP),
        P(DP, HEAD),
        P(HEAD, DP),
        P(None, (HEAD, DP)),
        P((HEAD, DP)),
        P((HEAD, DP)),
        P((HEAD, DP)),
        P((HEAD, DP)),
        P((HEAD, DP)),
        P(DP),
        P(DP),
        P(DP),
        P(DP),
        P(DP),
        P(DP),
    )

    return jax.shard_map(layer, mesh=mesh, in_specs=in_specs, out_specs=out_specs, check_vma=False)
```
